32 devices in a mesh: seq: 4 (over y, x), dp: 8 (over z, core).
Axes of the slice: x: 2, y: 2, z: 4, core: 2. Of those that a mesh axis runs over, the one named last changes fastest.
Arguments:
- frames: bfloat16 [8, 1024, 768], P('dp', 'seq'), may hold values from -6 to 6
- seg_ids: int32 [8, 1024], P('dp'), may hold values from 0 to 2, never falling along the last dimension, each value on 1 to 512 neighbouring positions
- padding: int32 [8, 1024], P('dp'), may hold values from 0 to 1, as said below
- step_ids: int32 [8, 3], P('dp'), may hold values from 0 to 999
- text_states: bfloat16 [8, 3, 256, 1024], P('dp', None, 'seq'), may hold values from -6 to 6
- text_len: int32 [8, 3], P('dp'), may hold values from 77 to 256
- w_ada: bfloat16 [768, 4608], replicated, may hold values from -0.21875 to 0.21875
- w_qkv: bfloat16 [768, 2304], replicated, may hold values from -0.21875 to 0.21875
- w_proj: bfloat16 [768, 768], replicated, may hold values from -1.25 to 1.25
- w_cq: bfloat16 [768, 768], replicated, may hold values from -0.21875 to 0.21875
- w_ckv: bfloat16 [1024, 1536], replicated, may hold values from -0.1875 to 0.1875
- w_cout: bfloat16 [768, 768], replicated, may hold values from -0.875 to 0.875
- w_fc1: bfloat16 [768, 3072], replicated, may hold values from -0.21875 to 0.21875
- w_fc2: bfloat16 [3072, 768], replicated, may hold values from -0.21875 to 0.21875
- cotangent: bfloat16 [8, 1024, 768], P('dp', 'seq'), may hold values from -6 to 6
Outputs:
- block_out: bfloat16 [8, 1024, 768], P('dp', 'seq')
- grad_frames: bfloat16 [8, 1024, 768], P('dp', 'seq')
- grad_text: bfloat16 [8, 3, 256, 1024], P('dp', None, 'seq')
- grad_ada: float32 [768, 4608], P('dp', 'seq')
- grad_qkv: float32 [768, 2304], P('dp', 'seq')
- grad_proj: float32 [768, 768], P('dp', 'seq')
- grad_cq: float32 [768, 768], P('dp', 'seq')
- grad_ckv: float32 [1024, 1536], P('dp', 'seq')
- grad_cout: float32 [768, 768], P('dp', 'seq')
- grad_fc1: float32 [768, 3072], P('dp', 'seq')
- grad_fc2: float32 [3072, 768], P('dp', 'seq')
The draws below stay inside these ranges and needn't reach their ends.
Inputs may be any that keep to these rules, and one draw needn't show every extreme that they name: `seg_ids`: in every row the clip numbers never fall; each of the 3 clips holds 1 to 512 frames, and one holds exactly 512. In every row the real frames come first, then at most 128 padding frames.
All inputs are finite; a program needn't handle non-finite values.
Results may differ from the reference program's by a relative error of at most 0.022.
Values may be sent and summed in bfloat16 or wider, within the bound.
A program may use at most 192 MiB of HBM per device.

```python
import math
import jax
import jax.numpy as jnp
import numpy as np
from jax import lax

D = 768
H = 12
HD = 64
FF = 3072
DC = 1024
SEQLEN = 1024
SEGS = 3
LTXT = 256
TXT_MIN = 77
ROWS = 8


def draw_padding(key, part):
    cut_len = jax.random.randint(key, (ROWS,), 0, SEQLEN // 8 + 1)
    cut_len = cut_len.at[0].set(SEQLEN // 8)
    positions = jnp.arange(SEQLEN)
    return (positions[None, :] < (SEQLEN - cut_len)[:, None]).astype(jnp.int32)


def draw_text_len(key, part):
    lengths = jax.random.randint(key, (ROWS, SEGS), TXT_MIN, LTXT + 1)
    return lengths.at[0, 0].set(LTXT).at[0, 1].set(TXT_MIN)


def set_ends(values, own_key, least, high):
    longest = values.shape.index(max(values.shape))
    spots = []
    for shift in (0, 1):
        where = [jax.random.randint(jax.random.fold_in(own_key, axis), (), 0, length) for axis, length in enumerate(values.shape)]
        where[longest] = (where[longest] + shift) % values.shape[longest]
        spots.append(tuple(where))
    return values.at[spots[0]].set(least).at[spots[1]].set(high)


def level_of(key, extent, shards, smallest, largest):
    factor_of = 1.0
    for dim, blocks in shards:
        heights = jax.random.uniform(jax.random.fold_in(jax.random.fold_in(key, 6), dim), (blocks,), jnp.float32, smallest / len(shards), largest / len(shards))
        factor_of = factor_of * jnp.repeat(jnp.exp(heights), extent[dim] // blocks).reshape((-1,) + (1,) * (len(extent) - 1 - dim))
    return factor_of


def profile(number_of, total, limit, slope):
    portions = [(1 << 20) // math.isqrt(grade ** slope) + 1 for grade in range(2, number_of + 1)]
    rest, given = total - limit - (number_of - 1), [1] * (number_of - 1)
    while rest > 0:
        free = [i for i in range(number_of - 1) if given[i] < limit]
        mass, left = sum([portions[i] for i in free]), rest
        for i in free:
            more = min(limit - given[i], max(1, left * portions[i] // mass), rest)
            given[i] = given[i] + more
            rest = rest - more
    return np.array([limit] + given)


def ragged(stream_key, count, total, bound, lean):
    if count == 2:
        one = jax.random.randint(stream_key, (), max(1, total - bound), min(bound, total - 1) + 1)
        return jnp.stack([one, total - one])
    sizes = jnp.asarray(profile(count, total, bound, lean), jnp.int32)
    twos = (count - 1) // 2
    source_of, taker = sizes[1:1 + 2 * twos:2], sizes[2:2 + 2 * twos:2]
    margin = jnp.minimum(source_of - 1, bound - taker)
    moved = jax.random.randint(jax.random.fold_in(stream_key, 1), (twos,), 0, 1 << 20) % (margin + 1)
    sizes = sizes.at[1:1 + 2 * twos:2].set(source_of - moved).at[2:2 + 2 * twos:2].set(taker + moved)
    return sizes[jax.random.permutation(jax.random.fold_in(stream_key, 2), count)]


def noise(rng, shape, width, bound, pieces=(), held_as=jnp.bfloat16):
    drawn = jax.random.normal(rng, shape, jnp.float32) * width
    if len(pieces) > 0:
        drawn = level_of(rng, shape, pieces, -0.22, 0.18) * drawn
    return jnp.clip(drawn, min=-bound, max=bound).astype(held_as)


def setup_inputs(seed: int = 0) -> dict:
    streams_of = jax.random.split(jax.random.key(seed), 16)
    return {
        "frames": noise(streams_of[0], (ROWS, SEQLEN, D), 1.0, 6.0, ((0, 8), (1, 4))),
        "seg_ids": jax.vmap(lambda own: jnp.searchsorted(jnp.cumsum(ragged(own, SEGS, SEQLEN, SEQLEN // 2, 1)), jnp.arange(SEQLEN), side="right"))(jax.random.split(streams_of[1], ROWS)).reshape((ROWS, SEQLEN)).astype(jnp.int32),
        "padding": draw_padding(jax.random.fold_in(streams_of[15], 71), 0),
        "step_ids": set_ends(jax.random.randint(streams_of[3], (ROWS, SEGS), 0, 1000), jax.random.fold_in(streams_of[3], 1), 0, 999).astype(jnp.int32),
        "text_states": noise(streams_of[4], (ROWS, SEGS, LTXT, DC), 1.0, 6.0, ((0, 8), (2, 4))),
        "text_len": draw_text_len(jax.random.fold_in(streams_of[15], 71), 0),
        "w_ada": noise(streams_of[6], (D, 6 * D), D ** -0.5, 0.21875),
        "w_qkv": noise(streams_of[7], (D, 3 * D), D ** -0.5, 0.21875),
        "w_proj": noise(streams_of[8], (D, D), (D // 32) ** -0.5, 1.25),
        "w_cq": noise(streams_of[9], (D, D), D ** -0.5, 0.21875),
        "w_ckv": noise(streams_of[10], (DC, 2 * D), DC ** -0.5, 0.1875),
        "w_cout": noise(streams_of[11], (D, D), (D // 16) ** -0.5, 0.875),
        "w_fc1": noise(streams_of[12], (D, FF), D ** -0.5, 0.21875),
        "w_fc2": noise(streams_of[13], (FF, D), (FF // 4) ** -0.5, 0.21875),
        "cotangent": noise(streams_of[14], (ROWS, SEQLEN, D), 1.0, 6.0, ((0, 8), (1, 4))),
    }


@jax.custom_vjp
def low(v):
    return lax.optimization_barrier(v.astype(jnp.bfloat16)).astype(jnp.float32)

@jax.custom_vjp
def low_back(v):
    return v

def low_keep(v):
    return (low(v), None)

def low_pass(kept, grad):
    return (grad,)

def back_keep(v):
    return (v, None)

def back_low(kept, grad):
    return (low(grad),)
low.defvjp(low_keep, low_pass)
low_back.defvjp(back_keep, back_low)
highest = lax.Precision.HIGHEST
masked_score = -1e+30
epsilon = 1e-06

def embed_steps(step_values, width_all):
    half_width = width_all // 2
    frequency = jnp.exp(-math.log(10000.0) * jnp.arange(half_width).astype(jnp.float32) / half_width)
    angles = step_values.astype(jnp.float32)[..., None] * frequency
    return jax.nn.silu(jnp.concatenate([jnp.cos(angles), jnp.sin(angles)], axis=-1))

def normalize(values):
    centered = values - lax.optimization_barrier(jnp.mean(values, axis=-1, keepdims=True))
    return centered * lax.rsqrt(lax.optimization_barrier(jnp.mean(centered * centered, axis=-1, keepdims=True)) + epsilon)

def project(left, right):
    return jnp.einsum('...d,de->...e', left, right, precision=highest)

def attention(query, key_in, value_in, allowed, score_scale):
    scores = low_back(jnp.einsum('gihe,gjhe->ghij', query, key_in, precision=highest) * score_scale)
    scores = jnp.where(allowed[:, None], scores, masked_score)
    peak = lax.optimization_barrier(jnp.max(scores, axis=-1, keepdims=True))
    expo = jnp.exp(scores - peak)
    attn_weights = expo / lax.optimization_barrier(jnp.sum(expo, axis=-1, keepdims=True))
    return jnp.einsum('ghij,gjhe->gihe', low(attn_weights), value_in, precision=highest)

def forward(x_in, text_in, matrices, clip_emb, seg_group, pad_group, len_group):
    w_ada, w_qkv, w_proj, w_cq, w_ckv, w_cout, w_fc1, w_fc2 = matrices
    group_rows, seq_len, width_all = x_in.shape
    score_scale = HD ** (-0.5)
    modulation = project(low(clip_emb), w_ada)
    selector = (seg_group[..., None] == jnp.arange(SEGS)).astype(jnp.float32)
    per_token = jnp.einsum('gls,gse->gle', selector, modulation, precision=highest)
    shift_a, scale_a, gate_a, shift_m, scale_m, gate_m = jnp.split(per_token, 6, axis=-1)
    normed_a = low(normalize(x_in) * (1.0 + scale_a) + shift_a)
    packed = project(normed_a, w_qkv).reshape(group_rows, seq_len, 3, H, HD)
    query = low(low_back(packed[:, :, 0]))
    keys = low(low_back(packed[:, :, 1]))
    values = low(low_back(packed[:, :, 2]))
    positions = jnp.arange(seq_len)
    same_clip = seg_group[:, :, None] == seg_group[:, None, :]
    open_key = (pad_group[:, None, :] == 1) | (positions[:, None] == positions[None, :])[None]
    attended = attention(query, keys, values, same_clip & open_key, score_scale)
    attended = low(low_back(attended.reshape(group_rows, seq_len, width_all)))
    branch_a = low_back(project(attended, w_proj))
    mid_one = x_in + gate_a * branch_a
    normed_c = low(normalize(mid_one))
    cross_q = low(low_back(project(normed_c, w_cq))).reshape(group_rows, seq_len, H, HD)
    kv_all = low(low_back(project(text_in, w_ckv))).reshape(group_rows, SEGS * LTXT, 2, H, HD)
    key_seg = jnp.repeat(jnp.arange(SEGS), LTXT)
    key_pos = jnp.tile(jnp.arange(LTXT), SEGS)
    key_len = len_group[:, key_seg]
    cross_ok = (seg_group[:, :, None] == key_seg[None, None, :]) & (key_pos[None, :] < key_len)[:, None, :]
    cross_out = attention(cross_q, kv_all[:, :, 0], kv_all[:, :, 1], cross_ok, score_scale)
    cross_out = low(low_back(cross_out.reshape(group_rows, seq_len, width_all)))
    branch_c = low_back(project(cross_out, w_cout))
    mid_two = mid_one + branch_c
    normed_m = low(normalize(mid_two) * (1.0 + scale_m) + shift_m)
    hidden = low(jax.nn.gelu(low_back(project(normed_m, w_fc1)), approximate=True))
    branch_m = low_back(project(hidden, w_fc2))
    return mid_two + gate_m * branch_m

def reference(frames, seg_ids, padding, step_ids, text_states, text_len, w_ada, w_qkv, w_proj, w_cq, w_ckv, w_cout, w_fc1, w_fc2, cotangent):
    group_rows = math.gcd(ROWS, max(1, 4096 // SEQLEN))
    group_count = ROWS // group_rows
    matrices = tuple((matrix.astype(jnp.float32) for matrix in (w_ada, w_qkv, w_proj, w_cq, w_ckv, w_cout, w_fc1, w_fc2)))
    clip_emb = embed_steps(step_ids, D)

    def regroup(array_in):
        return array_in.reshape((group_count, group_rows) + array_in.shape[1:])
    scanned = tuple((regroup(item) for item in (frames.astype(jnp.float32), text_states.astype(jnp.float32), cotangent.astype(jnp.float32), clip_emb, seg_ids, padding, text_len)))

    def scan_step(totals, items):
        x_group, text_group, cot_group, emb_group, seg_group, pad_group, len_group = items

        def local_forward(x_in, text_in, *mats):
            return forward(x_in, text_in, mats, emb_group, seg_group, pad_group, len_group)
        out_group, pullback = jax.vjp(local_forward, x_group, text_group, *matrices)
        grads = pullback(cot_group)
        totals = tuple((total + grad for total, grad in zip(totals, grads[2:])))
        return (totals, (out_group.astype(jnp.bfloat16), grads[0].astype(jnp.bfloat16), grads[1].astype(jnp.bfloat16)))
    starting = tuple((jnp.zeros_like(matrix) for matrix in matrices))
    totals, (outputs, grad_x, grad_t) = lax.scan(scan_step, starting, scanned)
    block_out = outputs.reshape(frames.shape)
    grad_frames = grad_x.reshape(frames.shape)
    grad_text = grad_t.reshape(text_states.shape)
    return (block_out, grad_frames, grad_text, totals[0], totals[1], totals[2], totals[3], totals[4], totals[5], totals[6], totals[7])
```

```python
import functools
import math

import jax
import jax.numpy as jnp
from jax import lax
from jax.experimental import pallas as pl
from jax.experimental.pallas import tpu as pltpu
from jax.sharding import PartitionSpec as P

H = 12
HD = 64
BLOCKS = 8
SEQ = "seq"
DP = "dp"
CUT, COLS, PACK = 3, 1, 2
BF = jnp.bfloat16
F32 = jnp.float32
MESH = pl.DeviceIdType.MESH
MASKED = -1e30
EPS = 1e-06
SCALE = HD ** (-0.5)
ANY = pl.BlockSpec(memory_space=pl.ANY)
INV = pl.BlockSpec(memory_space=pltpu.VMEM)


def nn(a, b):
    return lax.dot_general(a, b, (((1,), (0,)), ((), ())), preferred_element_type=F32)


def nt(a, b):
    return lax.dot_general(a, b, (((1,), (1,)), ((), ())), preferred_element_type=F32)


def tn(a, b):
    return lax.dot_general(a, b, (((0,), (0,)), ((), ())), preferred_element_type=F32)


def embed_steps(step_values, width_all):
    half_width = width_all // 2
    frequency = jnp.exp(
        -math.log(10000.0) * jnp.arange(half_width).astype(F32) / half_width
    )
    angles = step_values.astype(F32)[..., None] * frequency
    return jax.nn.silu(jnp.concatenate([jnp.cos(angles), jnp.sin(angles)], axis=-1))


def norm_parts(v):
    centered = v - jnp.mean(v, axis=-1, keepdims=True)
    rstd = lax.rsqrt(jnp.mean(centered * centered, axis=-1, keepdims=True) + EPS)
    return centered * rstd, rstd


def norm_back(g, n, rstd):
    return (g - jnp.mean(g, axis=-1, keepdims=True) - n * jnp.mean(g * n, axis=-1, keepdims=True)) * rstd


def pick(mods, seg, part, width):
    low = part * width
    a = mods[0:1, low : low + width]
    b = mods[1:2, low : low + width]
    c = mods[2:3, low : low + width]
    return jnp.where(seg == 0.0, a, jnp.where(seg == 1.0, b, c))


def column(row):
    return jnp.broadcast_to(row, (128, row.shape[1])).T


class Bag(dict):
    __getattr__ = dict.__getitem__


class Remote:
    def __init__(self, send, recv):
        self.send, self.recv, self.used, self.open = send, recv, 0, []

    def slots(self, count):
        first = self.used
        self.used += count
        return first

    def make(self, src, dst, slot, where):
        return pltpu.make_async_remote_copy(
            src_ref=src,
            dst_ref=dst,
            send_sem=self.send.at[slot],
            recv_sem=self.recv.at[slot],
            device_id=where,
            device_id_type=MESH,
        )

    def start(self, describe):
        slot = self.slots(1)

        def again():
            src, dst, where = describe()
            return self.make(src, dst, slot, where)

        again().start()
        self.open.append(again)
        return again


class Local:
    def __init__(self, sems):
        self.sems, self.used = sems, 0

    def start(self, src, dst):
        copy = pltpu.make_async_copy(src, dst, self.sems.at[self.used])
        self.used += 1
        copy.start()
        return copy


def greet(seq, at_seq, dp_peers):
    barrier = pltpu.get_barrier_semaphore()
    for k in range(1, seq):
        pl.semaphore_signal(
            barrier, inc=1, device_id={SEQ: lax.rem(at_seq + k, seq)}, device_id_type=MESH
        )
    for peer in dp_peers:
        pl.semaphore_signal(barrier, inc=1, device_id={DP: peer}, device_id_type=MESH)
    pl.semaphore_wait(barrier, seq - 1 + len(dp_peers))


K1_OUTS = tuple(dict(h1=0, qT=0, kT=0, kn=0, vn=0, lse=0, oT=0, aout=0, x1=0, h2T=0, cqT=0, kv=0, ckT=0, lsec=0, coT=0, x2=0, text=0))


def forward_kernel(dims, *refs):
    seq, tok, full, width, keys, group, dc = dims
    hl = H // seq
    ins, refs = refs[:9], refs[9:]
    x_hbm, text_hbm, codes, mods, wg_hbm, wckv_hbm, wp_hbm, wcq_hbm, wco_hbm = ins
    outs, refs = Bag(zip(K1_OUTS, refs[: len(K1_OUTS)])), refs[len(K1_OUTS) :]
    (
        x_all, text_all, wg, wckv, wp, wcq, wco, qT, kT, vT, kn, vn, lse, osend, orecv, aout, x1, h2T, cqT, kv, kvT,
        lsec, coT, x2, bias, biasc, kcol, tcol, xin, lsem, ssem, rsem,
    ) = refs
    local, remote = Local(lsem), Remote(ssem, rsem)
    s = lax.axis_index(SEQ)
    load_x = local.start(x_hbm, xin)
    load_own = local.start(x_hbm, x_all.at[s])
    load_wg = local.start(wg_hbm, wg)
    load_text = local.start(text_hbm, text_all.at[s])
    load_w = [local.start(a, b) for a, b in ((wckv_hbm, wckv), (wp_hbm, wp), (wcq_hbm, wcq), (wco_hbm, wco))]
    greet(seq, s, ())

    base_x = remote.slots(seq)
    base_t = remote.slots(seq)
    base_o = remote.slots(seq)

    def send_x(k):
        return remote.make(x_hbm, x_all.at[s], base_x + k, {SEQ: lax.rem(s + k, seq)})

    def send_t(k):
        return remote.make(text_hbm, text_all.at[s], base_t + k, {SEQ: lax.rem(s + k, seq)})

    for k in range(1, seq):
        send_x(k).start()
    for k in range(1, seq):
        send_t(k).start()

    kcol[...] = column(codes[1:2, :full])
    tcol[...] = column(codes[2:3, :keys])
    load_x.wait()
    load_own.wait()
    load_wg.wait()

    def project(k, carry):
        @pl.when(k > 0)
        def _():
            send_x(k).wait_recv()

        at = lax.rem(s - k + seq, seq)
        rows = pl.ds(pl.multiple_of(at * tok, tok), tok)
        seg = column(codes[0:1, rows])[:, :1]
        seg = jnp.broadcast_to(seg, (tok, width))
        n, _ = norm_parts(x_all[at].astype(F32))
        h1 = (n * (1.0 + pick(mods, seg, 1, width)) + pick(mods, seg, 0, width)).astype(BF)
        x_all[at] = h1
        out = nn(h1, wg[...])
        for h in range(hl):
            kn[h, rows, :] = out[:, group + h * HD : group + (h + 1) * HD].astype(BF)
            vn[h, rows, :] = out[:, 2 * group + h * HD : 2 * group + (h + 1) * HD].astype(BF)
        low = out.astype(BF).astype(F32)
        outT = low.T
        qT[:, rows] = (outT[:group] * SCALE).astype(BF)
        kT[:, rows] = outT[group : 2 * group].astype(BF)
        vT[:, rows] = outT[2 * group :].astype(BF)
        return carry

    lax.fori_loop(0, seq, project, 0)
    saves = [
        local.start(a, b)
        for a, b in ((x_all, outs.h1), (qT, outs.qT), (kT, outs.kT), (kn, outs.kn), (vn, outs.vn))
    ]

    def send_o(k):
        at = lax.rem(s + k, seq)
        return remote.make(osend.at[at], orecv.at[s], base_o + k, {SEQ: at})

    def attend(k, carry):
        at = lax.rem(s + 1 + k, seq)
        rows = pl.ds(pl.multiple_of(at * tok, tok), tok)
        seg = codes[0:1, rows]
        row_id = lax.broadcasted_iota(jnp.int32, (full, tok), 0)
        col_id = lax.broadcasted_iota(jnp.int32, (full, tok), 1) + at * tok
        key = jnp.broadcast_to(kcol[:, :1], (full, tok))
        bias[...] = jnp.where((key == seg) | (row_id == col_id), 0.0, MASKED)

        def head(h, c2):
            hrows = pl.ds(pl.multiple_of(h * HD, HD), HD)
            st = nn(kn[h], qT[hrows, rows]) + bias[...]
            peak = jnp.max(st, axis=0, keepdims=True)
            ex = jnp.exp(st - peak)
            total = jnp.sum(ex, axis=0, keepdims=True)
            ov = nn(vT[hrows, :], ex.astype(BF)) * (1.0 / total)
            osend[at, hrows, :] = ov.astype(BF)
            lse[pl.ds(h, 1), rows] = peak + jnp.log(total)
            return c2

        lax.fori_loop(0, hl, head, 0)

        @pl.when(k < seq - 1)
        def _():
            send_o(k + 1).start()

        return carry

    lax.fori_loop(0, seq, attend, 0)
    orecv[s] = osend[s]

    load_text.wait()
    for k in range(1, seq):
        send_t(k).wait_recv()
    saves.append(local.start(text_all, outs.text))
    saves.append(local.start(lse, outs.lse))
    for c in load_w:
        c.wait()
    tl = keys // seq

    def project_text(b, carry):
        trows = pl.ds(pl.multiple_of(b * tl, tl), tl)
        kv[trows, :] = nn(text_all[b], wckv[...]).astype(BF)
        return carry

    lax.fori_loop(0, seq, project_text, 0)

    def turn_text(c, carry):
        cols = pl.ds(pl.multiple_of(c * 256, 256), 256)
        kvT[cols, :] = kv[:, cols].astype(F32).T.astype(BF)
        return carry

    lax.fori_loop(0, 2 * width // 256, turn_text, 0)
    rows = pl.ds(pl.multiple_of(s * tok, tok), tok)
    seg_row = codes[0:1, rows]
    biasc[...] = jnp.where(jnp.broadcast_to(tcol[:, :1], (keys, tok)) == seg_row, 0.0, MASKED)
    saves.append(local.start(kv, outs.kv))
    saves.append(local.start(kvT.at[pl.ds(0, width)], outs.ckT))

    for k in range(1, seq):
        send_o(k).wait_recv()
    saves.append(local.start(orecv, outs.oT))
    seg = jnp.broadcast_to(column(seg_row)[:, :1], (tok, width))
    branch = tn(orecv[...].reshape(width, tok), wp[...])
    aout[...] = branch
    mid = xin[...].astype(F32) + pick(mods, seg, 2, width) * branch
    x1[...] = mid
    n, _ = norm_parts(mid)
    h2 = n.astype(BF)
    h2T[...] = n.astype(BF).astype(F32).T.astype(BF)
    cq = nn(h2, wcq[...]).astype(BF).astype(F32)
    cqT[...] = (cq.T * SCALE).astype(BF)
    saves += [local.start(a, b) for a, b in ((aout, outs.aout), (x1, outs.x1), (h2T, outs.h2T), (cqT, outs.cqT))]

    def cross(p, carry):
        cols = pl.ds(pl.multiple_of(p * 128, 128), 128)
        pair = kv[:, cols]
        for a in range(2):
            hrows = pl.ds(pl.multiple_of(p * 128 + a * HD, HD), HD)
            vrows = pl.ds(pl.multiple_of(width + p * 128 + a * HD, HD), HD)
            st = nn(pair[:, a * HD : (a + 1) * HD], cqT[hrows, :]) + biasc[...]
            peak = jnp.max(st, axis=0, keepdims=True)
            ex = jnp.exp(st - peak)
            total = jnp.sum(ex, axis=0, keepdims=True)
            ov = nn(kvT[vrows, :], ex.astype(BF)) * (1.0 / total)
            coT[hrows, :] = ov.astype(BF)
            lsec[pl.ds(2 * p + a, 1), :] = peak + jnp.log(total)
        return carry

    lax.fori_loop(0, H // 2, cross, 0)
    x2[...] = x1[...] + tn(coT[...], wco[...])
    saves += [local.start(a, b) for a, b in ((lsec, outs.lsec), (coT, outs.coT), (x2, outs.x2))]
    for k in range(1, seq):
        send_x(k).wait_send()
        send_t(k).wait_send()
        send_o(k).wait_send()
    for c in saves:
        c.wait()


def run_forward(dims, args):
    seq, tok, full, width, keys, group, dc = dims
    hl = H // seq
    shapes = dict(
        h1=((seq, tok, width), BF),
        qT=((group, full), BF),
        kT=((group, full), BF),
        kn=((hl, full, HD), BF),
        vn=((hl, full, HD), BF),
        lse=((8, full), F32),
        oT=((seq, group, tok), BF),
        aout=((tok, width), F32),
        x1=((tok, width), F32),
        h2T=((width, tok), BF),
        cqT=((width, tok), BF),
        kv=((keys, 2 * width), BF),
        ckT=((width, keys), BF),
        lsec=((16, tok), F32),
        coT=((width, tok), BF),
        x2=((tok, width), F32),
        text=((seq, keys // seq, dc), BF),
    )
    v = pltpu.VMEM
    scratch = [
        v((seq, tok, width), BF), v((seq, keys // seq, dc), BF), v((width, 3 * group), BF), v((dc, 2 * width), BF),
        v((width, width), BF), v((width, width), BF), v((width, width), BF),
        v((group, full), BF), v((group, full), BF), v((group, full), BF), v((hl, full, HD), BF), v((hl, full, HD), BF),
        v((8, full), F32), v((seq, group, tok), BF), v((seq, group, tok), BF),
        v((tok, width), F32), v((tok, width), F32), v((width, tok), BF), v((width, tok), BF),
        v((keys, 2 * width), BF), v((2 * width, keys), BF), v((16, tok), F32), v((width, tok), BF), v((tok, width), F32),
        v((full, tok), F32), v((keys, tok), F32), v((full, 128), F32), v((keys, 128), F32), v((tok, width), BF),
        pltpu.SemaphoreType.DMA((32,)), pltpu.SemaphoreType.DMA((3 * seq,)), pltpu.SemaphoreType.DMA((3 * seq,)),
    ]
    outs = pl.pallas_call(
        functools.partial(forward_kernel, dims),
        out_shape=[jax.ShapeDtypeStruct(*shapes[n]) for n in K1_OUTS],
        in_specs=[ANY, ANY, INV, INV, ANY, ANY, ANY, ANY, ANY],
        out_specs=[ANY] * len(K1_OUTS),
        scratch_shapes=scratch,
        compiler_params=pltpu.CompilerParams(
            collective_id=0, has_side_effects=True, vmem_limit_bytes=60 * 1024 * 1024
        ),
        name="forward_part",
    )(*args)
    return Bag(zip(K1_OUTS, outs))


class Grad:
    def __init__(self, ref, kind, order, bufs, where, remote, finish):
        self.ref, self.kind, self.order, self.bufs = ref, kind, order, bufs
        self.s, self.seq, self.d, self.stride, self.bits = where
        self.remote, self.finish = remote, finish
        self.fixed, self.cut, self.stage, self.copies = {}, False, 0, []

    def view(self, fixed, quarter, lead=None):
        index, lead = [], list(lead or [])
        for bit in (2, 1, 0):
            if bit in fixed:
                index.append(fixed[bit])
            elif lead:
                index.append(lead.pop(0))
            else:
                index.append(slice(None))
        if quarter is not None:
            size = self.ref.shape[-1] // (self.seq if self.kind == COLS else 2)
            if self.kind == COLS:
                lanes = pl.ds(pl.multiple_of(quarter * size, 128), size)
                index += [slice(None), lanes]
            else:
                lanes = pl.ds(pl.multiple_of(lax.rem(quarter, 2) * size, 128), size)
                index += [lax.div(quarter, 2), slice(None), lanes]
        return self.ref.at[tuple(index)]

    def begin(self):
        what, buf = self.order[self.stage], self.bufs[self.stage]
        self.copies = []
        if what == CUT:
            for k in range(1, self.seq):

                def describe(k=k, fixed=dict(self.fixed)):
                    to = lax.rem(self.s + k, self.seq)
                    return self.view(fixed, to), buf.at[k - 1], {SEQ: to}

                self.copies.append(self.remote.start(describe))
        else:

            def describe(fixed=dict(self.fixed), quarter=self.s if self.cut else None):
                mine = self.bits[what]
                peer = self.d + (1 - 2 * mine) * (self.stride << what)
                return self.view({**fixed, what: 1 - mine}, quarter), buf, {DP: peer}

            self.copies.append(self.remote.start(describe))

    def end(self):
        what, buf = self.order[self.stage], self.bufs[self.stage]
        for c in self.copies:
            c().wait_recv()
        if what == CUT:
            self.cut = True
        else:
            self.fixed[what] = self.bits[what]
        free = 3 - len(self.fixed)
        quarter = self.s if self.cut else None
        last = self.stage == len(self.order) - 1
        self.stage += 1

        def add(i, carry):
            lead = [lax.rem(lax.div(i, 2 ** (free - 1 - j)), 2) for j in range(free)]
            own = self.view(self.fixed, quarter, lead)
            total = own[...].astype(F32)
            if what == CUT:
                for k in range(self.seq - 1):
                    total = total + buf[tuple([k] + lead)].astype(F32)
            elif lead:
                total = total + buf[tuple(lead)].astype(F32)
            else:
                total = total + buf[...].astype(F32)
            if last:
                self.finish(total)
            else:
                own[...] = total.astype(BF)
            return carry

        if free == 0:
            add(0, 0)
        else:
            lax.fori_loop(0, 2**free, add, 0)

    def step(self):
        self.end()
        if self.stage < len(self.order):
            self.begin()


def grad_buffers(shape, kind, order, seq):
    lead, payload, out, cut, free = 3, list(shape), [], False, 3
    for what in order:
        if what == CUT:
            cut = True
        else:
            free -= 1
        p = list(payload)
        if cut:
            if kind == COLS:
                p[-1] //= seq
            else:
                p = [p[1], p[2] // 2]
        head = [seq - 1] if what == CUT else []
        out.append(pltpu.VMEM(tuple(head + [2] * free + p), BF))
    return out


GRADS = dict(
    fc2=(PACK, (0, CUT, 1, 2)),
    fc1=(COLS, (0, 1, 2, CUT)),
    cout=(PACK, (0, CUT, 1, 2)),
    cq=(PACK, (0, CUT, 1, 2)),
    proj=(PACK, (0, CUT, 1, 2)),
    ckv=(None, (0, 1, 2)),
    qkv=(None, (0, 1, 2)),
)
K2_OUTS = tuple(dict(block_out=0, grad_frames=0, grad_text=0, ada=0, qkv=0, proj=0, cq=0, ckv=0, cout=0, fc1=0, fc2=0))
K2_LOADS = tuple(dict(x2=0, x1=0, aout=0, oT=0, h2T=0, cqT=0, coT=0, lsec=0, lse=0, kv=0))
K2_HELD = tuple(dict(ckT=0, qT=0, kT=0, kn=0, vn=0))
K2_WEIGHTS = tuple(dict(fc1=0, fc2=0, cout=0, cq=0, proj=0))


def backward_kernel(dims, names, dp, *refs):
    seq, tok, full, width, keys, group, dc_all = dims
    hl, chunk, tl, stride = H // seq, width, keys // seq, dp // BLOCKS
    r = Bag(zip(names, refs))
    local, remote = Local(r.lsem), Remote(r.ssem, r.rsem)
    s, d = lax.axis_index(SEQ), lax.axis_index(DP)
    bits = [lax.rem(lax.div(d, stride << b), 2) for b in range(3)]
    where = (s, seq, d, stride, bits)
    codes, mods = r.codes, r.mods

    loads = Bag()
    loads["x2"] = local.start(r.in_x2, r.x2)
    loads["cot"] = local.start(r.in_cot, r.cot)
    for n in K2_WEIGHTS:
        loads["w_" + n] = local.start(r["w_" + n], r["g_" + n])
    for n in K2_LOADS[1:]:
        loads[n] = local.start(r["in_" + n], r[n])
    loads.x = local.start(r.in_x, r.x)

    barrier = pltpu.get_barrier_semaphore()
    for k in range(1, seq):
        pl.semaphore_signal(barrier, inc=1, device_id={SEQ: lax.rem(s + k, seq)}, device_id_type=MESH)

    def greet_dp(j, carry):
        pl.semaphore_signal(barrier, inc=1, device_id={DP: lax.rem(d + j, dp)}, device_id_type=MESH)
        return carry

    lax.fori_loop(1, dp, greet_dp, 0)
    pl.semaphore_wait(barrier, seq - 1 + dp - 1)

    emb_base = remote.slots(dp)
    dm_base = remote.slots(dp)

    def send_emb(j):
        to = lax.rem(d + j, dp)
        return remote.make(r.in_emb.at[to], r.emball.at[d], emb_base + j, {DP: to})

    def start_emb(j, carry):
        send_emb(j).start()
        return carry

    lax.fori_loop(1, dp, start_emb, 0)
    own_emb = local.start(r.in_emb.at[d], r.emball.at[d])

    def into_cols(n):
        def finish(total):
            r["out_" + n][...] = total

        return finish

    def into_pack(n):
        def finish(total):
            rows, lanes = total.shape
            r["out_" + n][0:rows, :] = total[:, : lanes // 2]
            r["out_" + n][rows : 2 * rows, :] = total[:, lanes // 2 :]

        return finish

    def into_blocks(total):
        for t in range(3):
            r.fq[t] = total[:, t * group : (t + 1) * group]

    grads = Bag()
    for n, (kind, order) in GRADS.items():
        finish = into_blocks if n == "qkv" else (into_pack(n) if kind == PACK else into_cols(n))
        bufs = [r["r_%s%d" % (n, i)] for i in range(len(order))]
        grads[n] = Grad(r["g_" + n], kind, order, bufs, where, remote, finish)

    rows_own = pl.ds(pl.multiple_of(s * tok, tok), tok)
    seg_row = codes[0:1, rows_own]
    seg = jnp.broadcast_to(column(seg_row)[:, :1], (tok, width))
    clip_id = lax.broadcasted_iota(jnp.int32, (16, tok), 0).astype(F32)
    onehot = jnp.where(clip_id == seg_row, 1.0, 0.0).astype(BF)

    def clip_sum(part, value):
        high = value.astype(BF)
        rest = (value - high.astype(F32)).astype(BF)
        r.dmod[:, part * width : (part + 1) * width] = (nn(onehot, high) + nn(onehot, rest))[:8]

    def square(n, lhs, rhs):
        g = r["g_" + n]

        def four(i, carry):
            val = nn(lhs(i), rhs).astype(BF)
            for g0 in range(2):
                for q in range(seq):
                    half = val.shape[0] // 4
                    low = g0 * 2 * half
                    lane = (q % 2) * 2 * group
                    at = (lax.div(i, 2), lax.rem(i, 2), g0, q // 2)
                    g[at + (slice(None), slice(lane, lane + group))] = val[low : low + half, q * group : (q + 1) * group]
                    g[at + (slice(None), slice(lane + group, lane + 2 * group))] = val[
                        low + half : low + 2 * half, q * group : (q + 1) * group
                    ]
            return carry

        lax.fori_loop(0, 4, four, 0)

    def weight(n):
        return r["g_" + n][...].reshape(width, width)

    v = pltpu.VMEM
    dkv_copies = []
    quarter = 2 * width // seq
    do_base = remote.slots(seq)

    def send_do(k):
        to = lax.rem(s + k, seq)
        return remote.make(r.dosend.at[to], r.dorecv.at[s], do_base + k, {SEQ: to})

    def middle(*held):
        for n, ref in zip(K2_HELD, held):
            r[n] = ref
            loads[n] = local.start(r["in_" + n], ref)

        loads.x2.wait()
        loads.cot.wait()
        x2v = r.x2[...]
        n3, _ = norm_parts(x2v)
        h3 = (n3 * (1.0 + pick(mods, seg, 4, width)) + pick(mods, seg, 3, width)).astype(BF)

        def feed(h3_ref, h3T_ref, dm_ref, m_ref, dh_ref):
            h3_ref[...] = h3
            h3T_ref[...] = h3.astype(F32).T.astype(BF)
            dm_ref[...] = (pick(mods, seg, 5, width) * r.cot[...].astype(F32)).astype(BF)
            m_ref[...] = jnp.zeros_like(m_ref)
            dh_ref[...] = jnp.zeros_like(dh_ref)
            loads.w_fc1.wait()
            loads.w_fc2.wait()
            g1, g2 = r.g_fc1, r.g_fc2
            k0, k1 = math.sqrt(2.0 / math.pi), 0.044715

            def one(c, carry):
                cols = pl.ds(pl.multiple_of(c * chunk, chunk), chunk)
                ca, cb = lax.div(c, 2), lax.rem(c, 2)
                w1 = g1[:, :, :, :, cols].reshape(width, chunk)
                w2 = g2[ca, cb].reshape(chunk, width)
                z = nn(h3_ref[...], w1)
                zz = z * z
                t = jnp.tanh(k0 * (z + k1 * z * zz))
                u = (0.5 * z * (1.0 + t)).astype(BF)
                slope = 0.5 * (1.0 + t) + 0.5 * z * (1.0 - t * t) * (k0 * (1.0 + 3.0 * k1 * zz))
                m_ref[...] += nn(u, w2)
                dz = (nt(dm_ref[...], w2) * slope).astype(BF)
                dh_ref[...] += nt(dz, w1)
                g1[:, :, :, :, cols] = nn(h3T_ref[...], dz).astype(BF).reshape(2, 2, 2, width // BLOCKS, chunk)
                for g0 in range(2):
                    half = chunk // 4
                    val = tn(u[:, g0 * 2 * half : (g0 + 1) * 2 * half], dm_ref[...]).astype(BF)
                    for q in range(seq):
                        lane = (q % 2) * 2 * group
                        g2[ca, cb, g0, q // 2, :, lane : lane + group] = val[:half, q * group : (q + 1) * group]
                        g2[ca, cb, g0, q // 2, :, lane + group : lane + 2 * group] = val[half:, q * group : (q + 1) * group]
                return carry

            lax.fori_loop(0, seq, one, 0)
            grads.fc2.begin()
            grads.fc1.begin()
            dy = r.cot[...].astype(F32)
            m = m_ref[...]
            x2w = r.x2[...]
            r.out_block_out[...] = (x2w + pick(mods, seg, 5, width) * m).astype(BF)
            clip_sum(5, dy * m)
            dh = dh_ref[...]
            nw, rstd = norm_parts(x2w)
            clip_sum(3, dh)
            clip_sum(4, dh * nw)
            r.dx[...] = dy + norm_back(dh * (1.0 + pick(mods, seg, 4, width)), nw, rstd)

        pl.run_scoped(feed, v((tok, width), BF), v((width, tok), BF), v((tok, width), BF), v((tok, width), F32), v((tok, width), F32))

        for c in (loads.w_cout, loads.coT, loads.cqT, loads.lsec, loads.kv, loads.ckT):
            c.wait()

        def cross_back(dcoT, dcqT, biasc):
            dc = r.dx[...].astype(BF)
            dcoT[...] = nt(weight("cout"), dc).astype(BF)
            square("cout", lambda i: r.coT[pl.ds(pl.multiple_of(i * group, group), group), :], dc)
            grads.cout.begin()
            tcol = column(codes[2:3, :keys])
            biasc[...] = jnp.where(jnp.broadcast_to(tcol[:, :1], (keys, tok)) == seg_row, 0.0, MASKED)
            grads.fc2.step()
            grads.fc1.step()
            kv = r.kv

            def pair(p, carry):
                cols = pl.ds(pl.multiple_of(p * 128, 128), 128)
                vcols = pl.ds(pl.multiple_of(width + p * 128, 128), 128)
                ck, cv = kv[:, cols], kv[:, vcols]
                parts_k, parts_v = [], []
                for a in range(2):
                    hrows = pl.ds(pl.multiple_of(p * 128 + a * HD, HD), HD)
                    q_h, do_h = r.cqT[hrows, :], dcoT[hrows, :]
                    lse_h = r.lsec[pl.ds(2 * p + a, 1), :]
                    pr = jnp.exp(nn(ck[:, a * HD : (a + 1) * HD], q_h) + biasc[...] - lse_h)
                    dpr = nn(cv[:, a * HD : (a + 1) * HD], do_h)
                    delta = jnp.sum(pr * dpr, axis=0, keepdims=True)
                    ds = (pr * (dpr - delta)).astype(BF)
                    parts_k.append(nt(ds, q_h))
                    parts_v.append(nt(pr.astype(BF), do_h))
                    dcqT[hrows, :] = nn(r.ckT[hrows, :], ds) * SCALE
                kv[:, cols] = jnp.concatenate(parts_k, axis=1).astype(BF)
                kv[:, vcols] = jnp.concatenate(parts_v, axis=1).astype(BF)
                return carry

            lax.fori_loop(0, H // 2, pair, 0)
            dcq = dcqT[...].T.astype(BF)
            loads.w_cq.wait()
            loads.h2T.wait()
            loads.x1.wait()
            dh2 = nt(dcq, weight("cq"))
            square("cq", lambda i: r.h2T[pl.ds(pl.multiple_of(i * group, group), group), :], dcq)
            nw, rstd = norm_parts(r.x1[...])
            r.dx[...] += norm_back(dh2, nw, rstd)

        pl.run_scoped(cross_back, v((width, tok), BF), v((width, tok), F32), v((keys, tok), F32))

        for c in (loads.w_proj, loads.aout, loads.oT):
            c.wait()
        dx1 = r.dx[...]
        da = (pick(mods, seg, 2, width) * dx1).astype(BF)
        doT = nt(weight("proj"), da).astype(BF)
        for q in range(seq):
            r.dosend[q] = doT[q * group : (q + 1) * group, :]
        for k in range(1, seq):
            send_do(k).start()
        r.dorecv[s] = r.dosend[s]
        grads.cq.begin()
        clip_sum(2, dx1 * r.aout[...])
        square("proj", lambda i: r.oT[i], da)
        grads.proj.begin()
        grads.cout.step()
        grads.fc1.step()
        for k in range(1, seq):

            def describe_kv(k=k):
                to = lax.rem(s + k, seq)
                lanes = pl.ds(pl.multiple_of(to * quarter, quarter), quarter)
                return r.kv.at[:, lanes], r.dkvr.at[k - 1], {SEQ: to}

            dkv_copies.append(remote.start(describe_kv))
        grads.fc2.step()
        for c in (loads.qT, loads.kT, loads.kn, loads.vn, loads.lse):
            c.wait()

        def self_back(kcol, bias, dk, dv):
            kcol[...] = column(codes[1:2, :full])
            dk[...] = jnp.zeros_like(dk)
            dv[...] = jnp.zeros_like(dv)

            def block(k, carry):
                @pl.when(k > 0)
                def _():
                    send_do(k).wait_recv()

                at = lax.rem(s - k + seq, seq)
                rows = pl.ds(pl.multiple_of(at * tok, tok), tok)
                row_id = lax.broadcasted_iota(jnp.int32, (full, tok), 0)
                col_id = lax.broadcasted_iota(jnp.int32, (full, tok), 1) + at * tok
                key = jnp.broadcast_to(kcol[:, :1], (full, tok))
                bias[...] = jnp.where((key == codes[0:1, rows]) | (row_id == col_id), 0.0, MASKED)
                for h in range(hl):
                    hs = slice(h * HD, (h + 1) * HD)
                    q_h, do_h = r.qT[hs, rows], r.dorecv[at, hs, :]
                    pr = jnp.exp(nn(r.kn[h], q_h) + bias[...] - r.lse[h : h + 1, rows])
                    dpr = nn(r.vn[h], do_h)
                    delta = jnp.sum(pr * dpr, axis=0, keepdims=True)
                    ds = (pr * (dpr - delta)).astype(BF)
                    dk[h] += nt(ds, q_h)
                    dv[h] += nt(pr.astype(BF), do_h)
                    dq = nn(r.kT[hs, :], ds) * SCALE
                    r.dqs[at, :, hs] = dq.T.astype(BF)
                return carry

            lax.fori_loop(0, seq, block, 0)
            for h in range(hl):
                for b in range(seq):
                    br = slice(b * tok, (b + 1) * tok)
                    r.dqs[b, :, group + h * HD : group + (h + 1) * HD] = dk[h, br, :].astype(BF)
                    r.dqs[b, :, 2 * group + h * HD : 2 * group + (h + 1) * HD] = dv[h, br, :].astype(BF)

        pl.run_scoped(self_back, v((full, 128), F32), v((full, tok), F32), v((hl, full, HD), F32), v((hl, full, HD), F32))

    pl.run_scoped(
        middle,
        v((width, keys), BF),
        v((group, full), BF),
        v((group, full), BF),
        v((hl, full, HD), BF),
        v((hl, full, HD), BF),
    )

    dq_base = remote.slots(seq)

    def send_dq(k):
        to = lax.rem(s + k, seq)
        return remote.make(r.dqs.at[to], r.dqr.at[s], dq_base + k, {SEQ: to})

    for k in range(1, seq):
        send_dq(k).start()
    r.dqr[s] = r.dqs[s]

    def tail(h1, text, wqkv, wckv, dqf):
        tail_loads = [
            local.start(a, b)
            for a, b in ((r.in_h1, h1), (r.w_qkv, wqkv), (r.in_text, text), (r.w_ckv, wckv))
        ]
        loads.x.wait()
        tail_loads[0].wait()
        gq = tn(h1[...].reshape(full, width), r.dqs[...].reshape(full, 3 * group))
        r.g_qkv[...] = gq.astype(BF).reshape(2, 2, 2, width // BLOCKS, 3 * group)
        grads.qkv.begin()
        grads.cq.step()
        grads.proj.step()
        grads.fc2.step()
        grads.cout.step()
        grads.fc1.step()
        for c in dkv_copies:
            c().wait_recv()
        own = r.kv[:, pl.ds(pl.multiple_of(s * quarter, quarter), quarter)].astype(F32)
        for k in range(seq - 1):
            own = own + r.dkvr[k].astype(F32)
        r.dkvq[...] = own.astype(BF).reshape(seq, tl, quarter)
        kv_base = remote.slots(seq)

        def send_kv(k):
            to = lax.rem(s + k, seq)
            return remote.make(r.dkvq.at[to], r.dkvl.at[s], kv_base + k, {SEQ: to})

        for k in range(1, seq):
            send_kv(k).start()
        r.dkvl[s] = r.dkvq[s]
        tail_loads[2].wait()
        gc = tn(text[...].reshape(keys, dc_all), r.dkvq[...].reshape(keys, quarter))
        r.g_ckv[...] = gc.astype(BF).reshape(2, 2, 2, dc_all // BLOCKS, quarter)
        grads.ckv.begin()
        grads.qkv.step()
        for k in range(1, seq):
            send_dq(k).wait_recv()
        for b in range(seq):
            got = r.dqr[b]
            for t in range(3):
                dqf[:, t * width + b * group : t * width + (b + 1) * group] = got[:, t * group : (t + 1) * group]
        tail_loads[1].wait()
        dh1 = nt(dqf[...], wqkv[...])
        nx, rstd = norm_parts(r.x[...].astype(F32))
        clip_sum(0, dh1)
        clip_sum(1, dh1 * nx)
        dm_copies = []
        part = 6 * width // seq
        for k in range(1, seq):

            def describe_dm(k=k):
                to = lax.rem(s + k, seq)
                lanes = pl.ds(pl.multiple_of(to * part, part), part)
                return r.dmod.at[:, lanes], r.dmr.at[k - 1], {SEQ: to}

            dm_copies.append(remote.start(describe_dm))
        back = norm_back(dh1 * (1.0 + pick(mods, seg, 1, width)), nx, rstd)
        r.out_grad_frames[...] = (r.dx[...] + back).astype(BF)
        grads.ckv.step()
        grads.qkv.step()
        grads.cq.step()
        grads.proj.step()
        for c in dm_copies:
            c().wait_recv()
        total = r.dmod[:, pl.ds(pl.multiple_of(s * part, part), part)]
        for k in range(seq - 1):
            total = total + r.dmr[k]
        r.dmall[d] = total

        def send_dm(j):
            to = lax.rem(d + j, dp)
            return remote.make(r.dmall.at[d], r.dmall.at[d], dm_base + j, {DP: to})

        def start_dm(j, carry):
            send_dm(j).start()
            return carry

        lax.fori_loop(1, dp, start_dm, 0)
        for k in range(1, seq):
            send_kv(k).wait_recv()
        tail_loads[3].wait()
        gt = nt(r.dkvl[0], wckv[:, 0:quarter])
        for b in range(1, seq):
            gt = gt + nt(r.dkvl[b], wckv[:, b * quarter : (b + 1) * quarter])
        r.out_grad_text[...] = gt.astype(BF)
        grads.fc2.step()
        grads.cout.step()
        grads.qkv.step()
        q_base = remote.slots(3)

        def send_q(t):
            b = 4 * t + s
            to = lax.div(b, 3)
            slot = b - 3 * to
            return to, slot, pltpu.make_async_remote_copy(
                src_ref=r.fq.at[t],
                dst_ref=r.rq.at[slot],
                send_sem=r.ssem.at[q_base + t],
                recv_sem=r.rsem.at[q_base + slot],
                device_id={SEQ: to},
                device_id_type=MESH,
            )

        for t in range(3):
            to, slot, copy = send_q(t)

            @pl.when(to != s)
            def _():
                copy.start()

            @pl.when(to == s)
            def _():
                r.rq[slot] = r.fq[t]

        grads.ckv.step()
        grads.cq.step()
        grads.proj.step()
        grads.fc1.step()
        grads.cout.step()
        grads.ckv.step()
        grads.cq.step()
        grads.proj.step()

        def wait_dm(j, carry):
            send_dm(j).wait_recv()
            send_emb(j).wait_recv()
            return carry

        own_emb.wait()
        lax.fori_loop(1, dp, wait_dm, 0)
        emb = r.emball[...].reshape(dp * 8, 128)
        allm = r.dmall[...].reshape(dp * 8, part)
        high = allm.astype(BF)
        rest = (allm - high.astype(F32)).astype(BF)
        ga = tn(emb, high) + tn(emb, rest)
        r.out_ada[...] = ga[: width // dp]
        for j in range(3):
            src = lax.rem(3 * s + j, seq)

            @pl.when(src != s)
            def _():
                remote.make(r.fq.at[j], r.rq.at[j], q_base + j, {SEQ: src}).wait_recv()

            r.out_qkv[:, j * group : (j + 1) * group] = r.rq[j]

        for t in range(3):
            to, slot, copy = send_q(t)

            @pl.when(to != s)
            def _():
                copy.wait_send()

        for k in range(1, seq):
            send_do(k).wait_send()
            send_dq(k).wait_send()
            send_kv(k).wait_send()

        def wait_sent(j, carry):
            send_dm(j).wait_send()
            send_emb(j).wait_send()
            return carry

        lax.fori_loop(1, dp, wait_sent, 0)
        for c in remote.open:
            c().wait_send()

    pl.run_scoped(
        tail,
        v((seq, tok, width), BF),
        v((seq, tl, dc_all), BF),
        v((width, 3 * width), BF),
        v((dc_all, 2 * width), BF),
        v((tok, 3 * width), BF),
    )


def run_backward(dims, dp, fwd, args):
    seq, tok, full, width, keys, group, dc = dims
    hl, tl, block = H // seq, keys // seq, width // BLOCKS
    ff = 4 * width
    v = pltpu.VMEM
    lead = (2, 2, 2)
    gshape = dict(
        fc1=(block, ff),
        fc2=(2, ff // BLOCKS // 2, width),
        cout=(2, block // 2, width),
        cq=(2, block // 2, width),
        proj=(2, block // 2, width),
        ckv=(dc // BLOCKS, 2 * width // seq),
        qkv=(block, 3 * group),
    )
    names, ins, specs = [], [], []

    def add_in(spec=ANY, **kw):
        for name, value in kw.items():
            names.append(name)
            ins.append(value)
            specs.append(spec)

    add_in(codes=args.codes, spec=INV)
    add_in(mods=args.mods, spec=INV)
    add_in(in_x=args.x)
    add_in(in_cot=args.cot)
    add_in(in_emb=args.emb)
    for n in K2_LOADS + K2_HELD + ("h1", "text"):
        add_in(**{"in_" + n: fwd[n]})
    for n in K2_WEIGHTS:
        add_in(**{"w_" + n: args[n].reshape(lead + gshape[n])})
    add_in(w_ckv=args.ckv)
    add_in(w_qkv=args.qkv)

    outs = dict(
        block_out=((tok, width), BF),
        grad_frames=((tok, width), BF),
        grad_text=((tl, dc), BF),
        ada=((width // dp, 6 * width // seq), F32),
        qkv=((block, 3 * group), F32),
        proj=((block, group), F32),
        cq=((block, group), F32),
        ckv=((dc // BLOCKS, 2 * width // seq), F32),
        cout=((block, group), F32),
        fc1=((block, ff // seq), F32),
        fc2=((ff // BLOCKS, group), F32),
    )
    for n in K2_OUTS:
        names.append("out_" + n)
    scratch = []

    def add(**kw):
        for name, (shape, dtype) in kw.items():
            names.append(name)
            scratch.append(v(shape, dtype))

    add(cot=((tok, width), BF))
    add(x=((tok, width), BF))
    for n in K2_LOADS:
        add(**{n: (fwd[n].shape, fwd[n].dtype)})
    for n, (kind, order) in GRADS.items():
        add(**{"g_" + n: (lead + gshape[n], BF)})
        for i, b in enumerate(grad_buffers(gshape[n], kind, order, seq)):
            names.append("r_%s%d" % (n, i))
            scratch.append(b)
    quarter = 2 * width // seq
    add(dx=((tok, width), F32))
    add(dkvr=((seq - 1, keys, quarter), BF))
    add(dkvq=((seq, tl, quarter), BF))
    add(dkvl=((seq, tl, quarter), BF))
    add(dosend=((seq, group, tok), BF))
    add(dorecv=((seq, group, tok), BF))
    add(dqs=((seq, tok, 3 * group), BF))
    add(dqr=((seq, tok, 3 * group), BF))
    add(dmod=((8, 6 * width), F32))
    add(dmr=((seq - 1, 8, 6 * width // seq), F32))
    add(dmall=((dp, 8, 6 * width // seq), F32))
    add(emball=((dp, 8, 128), BF))
    add(fq=((3, block, group), F32))
    add(rq=((3, block, group), F32))
    count = 2 * dp + 64
    for n, k in dict(lsem=40, ssem=count, rsem=count).items():
        names.append(n)
        scratch.append(pltpu.SemaphoreType.DMA((k,)))
    got = pl.pallas_call(
        functools.partial(backward_kernel, dims, tuple(names), dp),
        out_shape=[jax.ShapeDtypeStruct(*outs[n]) for n in K2_OUTS],
        in_specs=specs,
        out_specs=[INV] * len(K2_OUTS),
        scratch_shapes=scratch,
        compiler_params=pltpu.CompilerParams(
            collective_id=1, has_side_effects=True, vmem_limit_bytes=67043328
        ),
        name="backward_part",
    )(*ins)
    return Bag(zip(K2_OUTS, got))


def per_device(
    frames, seg_ids, padding, step_ids, text_states, text_len, w_ada, w_qkv, w_proj, w_cq, w_ckv, w_cout, w_fc1, w_fc2,
    cotangent,
):
    rows, tok, width = frames.shape
    seq, dp = lax.axis_size(SEQ), lax.axis_size(DP)
    segs = step_ids.shape[1]
    full = seg_ids.shape[1]
    tl, dc = text_states.shape[2], text_states.shape[3]
    keys = segs * tl * seq
    group = (H // seq) * HD
    dims = (seq, tok, full, width, keys, group, dc)
    s = lax.axis_index(SEQ)

    emb = embed_steps(step_ids[0], width).astype(BF)
    mods = jnp.dot(emb, w_ada, preferred_element_type=F32)
    mods = jnp.pad(mods, ((0, 8 - segs), (0, 0)))
    span = width // dp
    emb_parts = jnp.pad(
        jnp.swapaxes(emb.reshape(segs, dp, span), 0, 1), ((0, 0), (0, 8 - segs), (0, 128 - span))
    )
    place = jnp.arange(keys)
    clip = (place // tl) % segs
    position = (place // (tl * segs)) * tl + place % tl
    length = jnp.sum(jnp.where(clip[None, :] == jnp.arange(segs)[:, None], text_len[0][:, None], 0), axis=0)
    text_code = jnp.where(position < length, clip, -1)
    codes = jnp.stack(
        [seg_ids[0], jnp.where(padding[0] == 1, seg_ids[0], -1), jnp.pad(text_code, (0, full - keys))]
    ).astype(F32)
    codes = jnp.pad(codes, ((0, 5), (0, 0)))
    x = frames[0]
    text = text_states.reshape(segs * tl, dc)
    w_group = lax.dynamic_index_in_dim(
        w_qkv.reshape(width, 3, seq, group), s, 2, keepdims=False
    ).reshape(width, 3 * group)
    fwd = run_forward(dims, (x, text, codes, mods, w_group, w_ckv, w_proj, w_cq, w_cout))
    args = Bag(
        codes=codes, mods=mods, x=x, cot=cotangent[0], emb=emb_parts, ckv=w_ckv, qkv=w_qkv,
        fc1=w_fc1, fc2=w_fc2, cout=w_cout, cq=w_cq, proj=w_proj,
    )
    g = run_backward(dims, dp, fwd, args)
    stride = dp // BLOCKS
    if stride > 1:
        groups = [[b * stride + j for j in range(stride)] for b in range(BLOCKS)]
        for n in GRADS:
            g[n] = lax.psum_scatter(g[n], DP, scatter_dimension=0, axis_index_groups=groups, tiled=True)
    return (
        g.block_out.reshape(frames.shape),
        g.grad_frames.reshape(frames.shape),
        g.grad_text.reshape(text_states.shape),
        g.ada, g.qkv, g.proj, g.cq, g.ckv, g.cout, g.fc1, g.fc2,
    )


def solution(mesh):
    own, row, rep = P(DP, SEQ, None), P(DP, None), P()
    text, grad = P(DP, None, SEQ, None), P(DP, SEQ)
    return jax.shard_map(
        per_device,
        mesh=mesh,
        in_specs=(own, row, row, row, text, row) + (rep,) * 8 + (own,),
        out_specs=(own, own, text) + (grad,) * 8,
        check_vma=False,
    )
```

```python
import functools
import math

import jax
import jax.numpy as jnp
from jax import lax
from jax.experimental import pallas as pl
from jax.experimental.pallas import tpu as pltpu
from jax.sharding import PartitionSpec as P

H = 12
HD = 64
BLOCKS = 8
SEQ = "seq"
DP = "dp"
CUT, COLS, PACK = 3, 1, 2
BF = jnp.bfloat16
F32 = jnp.float32
MESH = pl.DeviceIdType.MESH
MASKED = -1e30
EPS = 1e-06
SCALE = HD ** (-0.5)
ANY = pl.BlockSpec(memory_space=pl.ANY)
INV = pl.BlockSpec(memory_space=pltpu.VMEM)


def nn(a, b):
    return lax.dot_general(a, b, (((1,), (0,)), ((), ())), preferred_element_type=F32)


def nt(a, b):
    return lax.dot_general(a, b, (((1,), (1,)), ((), ())), preferred_element_type=F32)


def tn(a, b):
    return lax.dot_general(a, b, (((0,), (0,)), ((), ())), preferred_element_type=F32)


def embed_steps(step_values, width_all):
    half_width = width_all // 2
    frequency = jnp.exp(
        -math.log(10000.0) * jnp.arange(half_width).astype(F32) / half_width
    )
    angles = step_values.astype(F32)[..., None] * frequency
    return jax.nn.silu(jnp.concatenate([jnp.cos(angles), jnp.sin(angles)], axis=-1))


def norm_parts(v):
    centered = v - jnp.mean(v, axis=-1, keepdims=True)
    rstd = lax.rsqrt(jnp.mean(centered * centered, axis=-1, keepdims=True) + EPS)
    return centered * rstd, rstd


def norm_back(g, n, rstd):
    return (g - jnp.mean(g, axis=-1, keepdims=True) - n * jnp.mean(g * n, axis=-1, keepdims=True)) * rstd


def pick(mods, seg, part, width):
    low = part * width
    a = mods[0:1, low : low + width]
    b = mods[1:2, low : low + width]
    c = mods[2:3, low : low + width]
    return jnp.where(seg == 0.0, a, jnp.where(seg == 1.0, b, c))


def column(row):
    return jnp.broadcast_to(row, (128, row.shape[1])).T


class Bag(dict):
    __getattr__ = dict.__getitem__


class Remote:
    def __init__(self, send, recv):
        self.send, self.recv, self.used, self.open = send, recv, 0, []

    def slots(self, count):
        first = self.used
        self.used += count
        return first

    def make(self, src, dst, slot, where):
        return pltpu.make_async_remote_copy(
            src_ref=src,
            dst_ref=dst,
            send_sem=self.send.at[slot],
            recv_sem=self.recv.at[slot],
            device_id=where,
            device_id_type=MESH,
        )

    def start(self, describe):
        slot = self.slots(1)

        def again():
            src, dst, where = describe()
            return self.make(src, dst, slot, where)

        again().start()
        self.open.append(again)
        return again


class Local:
    def __init__(self, sems):
        self.sems, self.used = sems, 0

    def start(self, src, dst):
        copy = pltpu.make_async_copy(src, dst, self.sems.at[self.used])
        self.used += 1
        copy.start()
        return copy


def greet(seq, at_seq, dp_peers):
    barrier = pltpu.get_barrier_semaphore()
    for k in range(1, seq):
        pl.semaphore_signal(
            barrier, inc=1, device_id={SEQ: lax.rem(at_seq + k, seq)}, device_id_type=MESH
        )
    for peer in dp_peers:
        pl.semaphore_signal(barrier, inc=1, device_id={DP: peer}, device_id_type=MESH)
    pl.semaphore_wait(barrier, seq - 1 + len(dp_peers))


K1_OUTS = tuple(dict(h1=0, qT=0, kT=0, kn=0, vn=0, lse=0, oT=0, aout=0, x1=0, h2T=0, cqT=0, kv=0, ckT=0, lsec=0, coT=0, x2=0, text=0, mods=0, codes=0))


def forward_kernel(dims, segs, *refs):
    seq, tok, full, width, keys, group, dc = dims
    hl = H // seq
    ins, refs = refs[:12], refs[12:]
    x_hbm, text_hbm, seg_in, pad_in, len_in, emb, wada_hbm, wqkv_hbm, wckv_hbm, wp_hbm, wcq_hbm, wco_hbm = ins
    outs, refs = Bag(zip(K1_OUTS, refs[: len(K1_OUTS)])), refs[len(K1_OUTS) :]
    (
        x_all, text_all, wg, wckv, wp, wcq, wco, qT, kT, vT, kn, vn, lse, osend, orecv, aout, x1, h2T, cqT, kv, kvT,
        lsec, coT, x2, bias, biasc, kcol, tcol, xin, wada, mods, codes, lsem, ssem, rsem,
    ) = refs
    local, remote = Local(lsem), Remote(ssem, rsem)
    s = lax.axis_index(SEQ)
    load_x = local.start(x_hbm, xin)
    load_own = local.start(x_hbm, x_all.at[s])
    load_ada = local.start(wada_hbm, wada)
    first = lax.div(s * group, 128) * 128
    odd = lax.rem(s * group, 128) > 0
    load_wg = [
        local.start(
            wqkv_hbm.at[:, pl.ds(pl.multiple_of(t * width + first, 128), 256)], wg.at[:, pl.ds(t * 256, 256)]
        )
        for t in range(3)
    ]
    load_text = local.start(text_hbm, text_all.at[s])
    load_w = [local.start(a, b) for a, b in ((wckv_hbm, wckv), (wp_hbm, wp), (wcq_hbm, wcq), (wco_hbm, wco))]
    greet(seq, s, ())

    base_x = remote.slots(seq)
    base_t = remote.slots(seq)
    base_o = remote.slots(seq)

    def send_x(k):
        return remote.make(x_hbm, x_all.at[s], base_x + k, {SEQ: lax.rem(s + k, seq)})

    def send_t(k):
        return remote.make(text_hbm, text_all.at[s], base_t + k, {SEQ: lax.rem(s + k, seq)})

    for k in range(1, seq):
        send_x(k).start()
    for k in range(1, seq):
        send_t(k).start()

    tl = keys // seq // segs
    place = lax.broadcasted_iota(jnp.int32, (1, full), 1).astype(F32)
    block = jnp.floor((place + 0.5) / tl)
    owner = jnp.floor((block + 0.5) / segs)
    clip = block - owner * segs
    length = jnp.zeros((1, full), F32)
    for c in range(segs):
        length = jnp.where(clip == c, jnp.broadcast_to(len_in[0:1, c : c + 1].astype(F32), (1, full)), length)
    codes[...] = jnp.zeros_like(codes)
    codes[0:1, :] = seg_in[...].astype(F32)
    codes[1:2, :] = jnp.where(pad_in[...] == 1, seg_in[...].astype(F32), -1.0)
    codes[2:3, :] = jnp.where(owner * tl + place - block * tl < length, clip, -1.0)
    save_codes = local.start(codes, outs.codes)
    kcol[...] = column(codes[1:2, :full])
    tcol[...] = column(codes[2:3, :keys])
    load_x.wait()
    load_own.wait()
    load_ada.wait()
    mods[...] = nn(emb[...], wada[...])
    save_mods = local.start(mods, outs.mods)
    for c in load_wg:
        c.wait()

    def project(k, carry):
        @pl.when(k > 0)
        def _():
            send_x(k).wait_recv()

        at = lax.rem(s - k + seq, seq)
        rows = pl.ds(pl.multiple_of(at * tok, tok), tok)
        seg = column(codes[0:1, rows])[:, :1]
        seg = jnp.broadcast_to(seg, (tok, width))
        n, _ = norm_parts(x_all[at].astype(F32))
        h1 = (n * (1.0 + pick(mods, seg, 1, width)) + pick(mods, seg, 0, width)).astype(BF)
        x_all[at] = h1
        wide = nn(h1, wg[...])
        out = jnp.concatenate(
            [
                jnp.where(odd, wide[:, t * 256 + 64 : t * 256 + 64 + group], wide[:, t * 256 : t * 256 + group])
                for t in range(3)
            ],
            axis=1,
        )
        for h in range(hl):
            kn[h, rows, :] = out[:, group + h * HD : group + (h + 1) * HD].astype(BF)
            vn[h, rows, :] = out[:, 2 * group + h * HD : 2 * group + (h + 1) * HD].astype(BF)
        low = out.astype(BF).astype(F32)
        outT = low.T
        qT[:, rows] = (outT[:group] * SCALE).astype(BF)
        kT[:, rows] = outT[group : 2 * group].astype(BF)
        vT[:, rows] = outT[2 * group :].astype(BF)
        return carry

    lax.fori_loop(0, seq, project, 0)
    saves = [save_mods, save_codes] + [
        local.start(a, b)
        for a, b in ((x_all, outs.h1), (qT, outs.qT), (kT, outs.kT), (kn, outs.kn), (vn, outs.vn))
    ]

    def send_o(k):
        at = lax.rem(s + k, seq)
        return remote.make(osend.at[at], orecv.at[s], base_o + k, {SEQ: at})

    def attend(k, carry):
        at = lax.rem(s + 1 + k, seq)
        rows = pl.ds(pl.multiple_of(at * tok, tok), tok)
        seg = codes[0:1, rows]
        row_id = lax.broadcasted_iota(jnp.int32, (full, tok), 0)
        col_id = lax.broadcasted_iota(jnp.int32, (full, tok), 1) + at * tok
        key = jnp.broadcast_to(kcol[:, :1], (full, tok))
        bias[...] = jnp.where((key == seg) | (row_id == col_id), 0.0, MASKED)

        def head(h, c2):
            hrows = pl.ds(pl.multiple_of(h * HD, HD), HD)
            st = nn(kn[h], qT[hrows, rows]) + bias[...]
            peak = jnp.max(st, axis=0, keepdims=True)
            ex = jnp.exp(st - peak)
            total = jnp.sum(ex, axis=0, keepdims=True)
            ov = nn(vT[hrows, :], ex.astype(BF)) * (1.0 / total)
            osend[at, hrows, :] = ov.astype(BF)
            lse[pl.ds(h, 1), rows] = peak + jnp.log(total)
            return c2

        lax.fori_loop(0, hl, head, 0)

        @pl.when(k < seq - 1)
        def _():
            send_o(k + 1).start()

        return carry

    lax.fori_loop(0, seq, attend, 0)
    orecv[s] = osend[s]

    load_text.wait()
    for k in range(1, seq):
        send_t(k).wait_recv()
    saves.append(local.start(text_all, outs.text))
    saves.append(local.start(lse, outs.lse))
    for c in load_w:
        c.wait()
    tl = keys // seq

    def project_text(b, carry):
        trows = pl.ds(pl.multiple_of(b * tl, tl), tl)
        kv[trows, :] = nn(text_all[b], wckv[...]).astype(BF)
        return carry

    lax.fori_loop(0, seq, project_text, 0)

    def turn_text(c, carry):
        cols = pl.ds(pl.multiple_of(c * 256, 256), 256)
        kvT[cols, :] = kv[:, cols].astype(F32).T.astype(BF)
        return carry

    lax.fori_loop(0, 2 * width // 256, turn_text, 0)
    rows = pl.ds(pl.multiple_of(s * tok, tok), tok)
    seg_row = codes[0:1, rows]
    biasc[...] = jnp.where(jnp.broadcast_to(tcol[:, :1], (keys, tok)) == seg_row, 0.0, MASKED)
    saves.append(local.start(kv, outs.kv))
    saves.append(local.start(kvT.at[pl.ds(0, width)], outs.ckT))

    for k in range(1, seq):
        send_o(k).wait_recv()
    saves.append(local.start(orecv, outs.oT))
    seg = jnp.broadcast_to(column(seg_row)[:, :1], (tok, width))
    branch = tn(orecv[...].reshape(width, tok), wp[...])
    aout[...] = branch
    mid = xin[...].astype(F32) + pick(mods, seg, 2, width) * branch
    x1[...] = mid
    n, _ = norm_parts(mid)
    h2 = n.astype(BF)
    h2T[...] = n.astype(BF).astype(F32).T.astype(BF)
    cq = nn(h2, wcq[...]).astype(BF).astype(F32)
    cqT[...] = (cq.T * SCALE).astype(BF)
    saves += [local.start(a, b) for a, b in ((aout, outs.aout), (x1, outs.x1), (h2T, outs.h2T), (cqT, outs.cqT))]

    def cross(p, carry):
        cols = pl.ds(pl.multiple_of(p * 128, 128), 128)
        pair = kv[:, cols]
        for a in range(2):
            hrows = pl.ds(pl.multiple_of(p * 128 + a * HD, HD), HD)
            vrows = pl.ds(pl.multiple_of(width + p * 128 + a * HD, HD), HD)
            st = nn(pair[:, a * HD : (a + 1) * HD], cqT[hrows, :]) + biasc[...]
            peak = jnp.max(st, axis=0, keepdims=True)
            ex = jnp.exp(st - peak)
            total = jnp.sum(ex, axis=0, keepdims=True)
            ov = nn(kvT[vrows, :], ex.astype(BF)) * (1.0 / total)
            coT[hrows, :] = ov.astype(BF)
            lsec[pl.ds(2 * p + a, 1), :] = peak + jnp.log(total)
        return carry

    lax.fori_loop(0, H // 2, cross, 0)
    x2[...] = x1[...] + tn(coT[...], wco[...])
    saves += [local.start(a, b) for a, b in ((lsec, outs.lsec), (coT, outs.coT), (x2, outs.x2))]
    for k in range(1, seq):
        send_x(k).wait_send()
        send_t(k).wait_send()
        send_o(k).wait_send()
    for c in saves:
        c.wait()


def run_forward(dims, args):
    seq, tok, full, width, keys, group, dc = dims
    hl = H // seq
    shapes = dict(
        h1=((seq, tok, width), BF),
        qT=((group, full), BF),
        kT=((group, full), BF),
        kn=((hl, full, HD), BF),
        vn=((hl, full, HD), BF),
        lse=((8, full), F32),
        oT=((seq, group, tok), BF),
        aout=((tok, width), F32),
        x1=((tok, width), F32),
        h2T=((width, tok), BF),
        cqT=((width, tok), BF),
        kv=((keys, 2 * width), BF),
        ckT=((width, keys), BF),
        lsec=((16, tok), F32),
        coT=((width, tok), BF),
        x2=((tok, width), F32),
        text=((seq, keys // seq, dc), BF),
        mods=((8, 6 * width), F32),
        codes=((8, full), F32),
    )
    v = pltpu.VMEM
    scratch = [
        v((seq, tok, width), BF), v((seq, keys // seq, dc), BF), v((width, 3 * 256), BF), v((dc, 2 * width), BF),
        v((width, width), BF), v((width, width), BF), v((width, width), BF),
        v((group, full), BF), v((group, full), BF), v((group, full), BF), v((hl, full, HD), BF), v((hl, full, HD), BF),
        v((8, full), F32), v((seq, group, tok), BF), v((seq, group, tok), BF),
        v((tok, width), F32), v((tok, width), F32), v((width, tok), BF), v((width, tok), BF),
        v((keys, 2 * width), BF), v((2 * width, keys), BF), v((16, tok), F32), v((width, tok), BF), v((tok, width), F32),
        v((full, tok), F32), v((keys, tok), F32), v((full, 128), F32), v((keys, 128), F32), v((tok, width), BF),
        v((width, 6 * width), BF), v((8, 6 * width), F32), v((8, full), F32),
        pltpu.SemaphoreType.DMA((32,)), pltpu.SemaphoreType.DMA((3 * seq,)), pltpu.SemaphoreType.DMA((3 * seq,)),
    ]
    outs = pl.pallas_call(
        functools.partial(forward_kernel, dims, args[4].shape[1]),
        out_shape=[jax.ShapeDtypeStruct(*shapes[n]) for n in K1_OUTS],
        in_specs=[ANY, ANY, INV, INV, INV, INV, ANY, ANY, ANY, ANY, ANY, ANY],
        out_specs=[ANY] * len(K1_OUTS),
        scratch_shapes=scratch,
        compiler_params=pltpu.CompilerParams(
            collective_id=0, has_side_effects=True, vmem_limit_bytes=60 * 1024 * 1024
        ),
        name="forward_part",
    )(*args)
    return Bag(zip(K1_OUTS, outs))


class Grad:
    def __init__(self, ref, kind, order, bufs, where, remote, finish):
        self.ref, self.kind, self.order, self.bufs = ref, kind, order, bufs
        self.s, self.seq, self.d, self.stride, self.bits = where
        self.remote, self.finish = remote, finish
        self.fixed, self.cut, self.stage, self.copies = {}, False, 0, []

    def view(self, fixed, quarter, lead=None):
        index, lead = [], list(lead or [])
        for bit in (2, 1, 0):
            if bit in fixed:
                index.append(fixed[bit])
            elif lead:
                index.append(lead.pop(0))
            else:
                index.append(slice(None))
        if quarter is not None:
            size = self.ref.shape[-1] // (self.seq if self.kind == COLS else 2)
            if self.kind == COLS:
                lanes = pl.ds(pl.multiple_of(quarter * size, 128), size)
                index += [slice(None), lanes]
            else:
                lanes = pl.ds(pl.multiple_of(lax.rem(quarter, 2) * size, 128), size)
                index += [lax.div(quarter, 2), slice(None), lanes]
        return self.ref.at[tuple(index)]

    def begin(self):
        what, buf = self.order[self.stage], self.bufs[self.stage]
        self.copies = []
        if what == CUT:
            for k in range(1, self.seq):

                def describe(k=k, fixed=dict(self.fixed)):
                    to = lax.rem(self.s + k, self.seq)
                    return self.view(fixed, to), buf.at[k - 1], {SEQ: to}

                self.copies.append(self.remote.start(describe))
        else:

            def describe(fixed=dict(self.fixed), quarter=self.s if self.cut else None):
                mine = self.bits[what]
                peer = self.d + (1 - 2 * mine) * (self.stride << what)
                return self.view({**fixed, what: 1 - mine}, quarter), buf, {DP: peer}

            self.copies.append(self.remote.start(describe))

    def end(self):
        what, buf = self.order[self.stage], self.bufs[self.stage]
        for c in self.copies:
            c().wait_recv()
        if what == CUT:
            self.cut = True
        else:
            self.fixed[what] = self.bits[what]
        free = 3 - len(self.fixed)
        quarter = self.s if self.cut else None
        last = self.stage == len(self.order) - 1
        self.stage += 1

        def add(i, carry):
            lead = [lax.rem(lax.div(i, 2 ** (free - 1 - j)), 2) for j in range(free)]
            own = self.view(self.fixed, quarter, lead)
            total = own[...].astype(F32)
            if what == CUT:
                for k in range(self.seq - 1):
                    total = total + buf[tuple([k] + lead)].astype(F32)
            elif lead:
                total = total + buf[tuple(lead)].astype(F32)
            else:
                total = total + buf[...].astype(F32)
            if last:
                self.finish(total)
            else:
                own[...] = total.astype(BF)
            return carry

        if free == 0:
            add(0, 0)
        else:
            lax.fori_loop(0, 2**free, add, 0)

    def step(self):
        self.end()
        if self.stage < len(self.order):
            self.begin()


def grad_buffers(shape, kind, order, seq):
    lead, payload, out, cut, free = 3, list(shape), [], False, 3
    for what in order:
        if what == CUT:
            cut = True
        else:
            free -= 1
        p = list(payload)
        if cut:
            if kind == COLS:
                p[-1] //= seq
            else:
                p = [p[1], p[2] // 2]
        head = [seq - 1] if what == CUT else []
        out.append(pltpu.VMEM(tuple(head + [2] * free + p), BF))
    return out


GRADS = dict(
    fc2=(PACK, (0, CUT, 1, 2)),
    fc1=(COLS, (0, 1, 2, CUT)),
    cout=(PACK, (0, CUT, 1, 2)),
    cq=(PACK, (0, CUT, 1, 2)),
    proj=(PACK, (0, CUT, 1, 2)),
    ckv=(None, (0, 1, 2)),
    qkv=(None, (0, 1, 2)),
)
K2_OUTS = tuple(dict(block_out=0, grad_frames=0, grad_text=0, ada=0, qkv=0, proj=0, cq=0, ckv=0, cout=0, fc1=0, fc2=0))
K2_LOADS = tuple(dict(x2=0, x1=0, aout=0, oT=0, h2T=0, cqT=0, coT=0, lsec=0, lse=0, kv=0))
K2_HELD = tuple(dict(ckT=0, qT=0, kT=0, kn=0, vn=0))
K2_WEIGHTS = tuple(dict(fc1=0, fc2=0, cout=0, cq=0, proj=0))


def backward_kernel(dims, names, dp, *refs):
    seq, tok, full, width, keys, group, dc_all = dims
    hl, chunk, tl, stride = H // seq, width, keys // seq, dp // BLOCKS
    r = Bag(zip(names, refs))
    local, remote = Local(r.lsem), Remote(r.ssem, r.rsem)
    s, d = lax.axis_index(SEQ), lax.axis_index(DP)
    bits = [lax.rem(lax.div(d, stride << b), 2) for b in range(3)]
    where = (s, seq, d, stride, bits)
    codes, mods = r.codes, r.mods

    loads = Bag()
    loads["x2"] = local.start(r.in_x2, r.x2)
    loads["cot"] = local.start(r.in_cot, r.cot)
    for n in K2_WEIGHTS:
        loads["w_" + n] = local.start(r["w_" + n], r["g_" + n])
    for n in K2_LOADS[1:]:
        loads[n] = local.start(r["in_" + n], r[n])
    loads.x = local.start(r.in_x, r.x)

    stores = []

    def stored(n, slot):
        return pltpu.make_async_copy(r["out_" + n], r["hbm_" + n], r.lsem.at[slot])

    def store(n):
        stores.append((n, local.used))
        stored(n, local.used).start()
        local.used += 1

    barrier = pltpu.get_barrier_semaphore()
    for k in range(1, seq):
        pl.semaphore_signal(barrier, inc=1, device_id={SEQ: lax.rem(s + k, seq)}, device_id_type=MESH)

    def greet_dp(j, carry):
        pl.semaphore_signal(barrier, inc=1, device_id={DP: lax.rem(d + j, dp)}, device_id_type=MESH)
        return carry

    lax.fori_loop(1, dp, greet_dp, 0)
    pl.semaphore_wait(barrier, seq - 1 + dp - 1)

    emb_base = remote.slots(dp)
    dm_base = remote.slots(dp)

    def send_emb(j):
        to = lax.rem(d + j, dp)
        return remote.make(r.in_emb.at[to], r.emball.at[d], emb_base + j, {DP: to})

    def start_emb(j, carry):
        send_emb(j).start()
        return carry

    lax.fori_loop(1, dp, start_emb, 0)
    own_emb = local.start(r.in_emb.at[d], r.emball.at[d])

    def into_cols(n):
        def finish(total):
            r["out_" + n][...] = total
            store(n)

        return finish

    def into_pack(n):
        def finish(total):
            rows, lanes = total.shape
            if n == "fc2":
                turned = total.T
                r.out_fc2[:, 0:rows] = turned[: lanes // 2]
                r.out_fc2[:, rows : 2 * rows] = turned[lanes // 2 :]
            else:
                r["out_" + n][0:rows, :] = total[:, : lanes // 2]
                r["out_" + n][rows : 2 * rows, :] = total[:, lanes // 2 :]
            store(n)

        return finish

    def into_blocks(total):
        for t in range(3):
            r.fq[t] = total[:, t * group : (t + 1) * group]

    grads = Bag()
    for n, (kind, order) in GRADS.items():
        finish = into_blocks if n == "qkv" else (into_pack(n) if kind == PACK else into_cols(n))
        bufs = [r["r_%s%d" % (n, i)] for i in range(len(order))]
        grads[n] = Grad(r["g_" + n], kind, order, bufs, where, remote, finish)

    rows_own = pl.ds(pl.multiple_of(s * tok, tok), tok)
    seg_row = codes[0:1, rows_own]
    seg = jnp.broadcast_to(column(seg_row)[:, :1], (tok, width))
    clip_id = lax.broadcasted_iota(jnp.int32, (16, tok), 0).astype(F32)
    onehot = jnp.where(clip_id == seg_row, 1.0, 0.0).astype(BF)

    def clip_sum(part, value):
        high = value.astype(BF)
        rest = (value - high.astype(F32)).astype(BF)
        r.dmod[:, part * width : (part + 1) * width] = (nn(onehot, high) + nn(onehot, rest))[:8]

    def square(n, lhs, rhs):
        g = r["g_" + n]

        def four(i, carry):
            val = nn(lhs(i), rhs).astype(BF)
            for g0 in range(2):
                for q in range(seq):
                    half = val.shape[0] // 4
                    low = g0 * 2 * half
                    lane = (q % 2) * 2 * group
                    at = (lax.div(i, 2), lax.rem(i, 2), g0, q // 2)
                    g[at + (slice(None), slice(lane, lane + group))] = val[low : low + half, q * group : (q + 1) * group]
                    g[at + (slice(None), slice(lane + group, lane + 2 * group))] = val[
                        low + half : low + 2 * half, q * group : (q + 1) * group
                    ]
            return carry

        lax.fori_loop(0, 4, four, 0)

    def weight(n):
        return r["g_" + n][...].reshape(width, width)

    v = pltpu.VMEM
    dkv_copies = []
    quarter = 2 * width // seq
    do_base = remote.slots(seq)

    def send_do(k):
        to = lax.rem(s + k, seq)
        return remote.make(r.dosend.at[to], r.dorecv.at[s], do_base + k, {SEQ: to})

    def middle(*held):
        for n, ref in zip(K2_HELD, held):
            r[n] = ref
            loads[n] = local.start(r["in_" + n], ref)

        loads.x2.wait()
        loads.cot.wait()
        x2v = r.x2[...]
        n3, _ = norm_parts(x2v)
        h3 = (n3 * (1.0 + pick(mods, seg, 4, width)) + pick(mods, seg, 3, width)).astype(BF)

        def feed(h3_ref, h3T_ref, dm_ref, m_ref, dh_ref):
            h3_ref[...] = h3
            h3T_ref[...] = h3.astype(F32).T.astype(BF)
            dm_ref[...] = (pick(mods, seg, 5, width) * r.cot[...].astype(F32)).astype(BF)
            m_ref[...] = jnp.zeros_like(m_ref)
            dh_ref[...] = jnp.zeros_like(dh_ref)
            loads.w_fc1.wait()
            loads.w_fc2.wait()
            g1, g2 = r.g_fc1, r.g_fc2
            k0, k1 = math.sqrt(2.0 / math.pi), 0.044715

            def one(c, carry):
                cols = pl.ds(pl.multiple_of(c * chunk, chunk), chunk)
                ca, cb = lax.div(c, 2), lax.rem(c, 2)
                w1 = g1[:, :, :, :, cols].reshape(width, chunk)
                w2 = g2[ca, cb].reshape(chunk, width)
                z = nn(h3_ref[...], w1)
                zz = z * z
                t = jnp.tanh(k0 * (z + k1 * z * zz))
                u = (0.5 * z * (1.0 + t)).astype(BF)
                slope = 0.5 * (1.0 + t) + 0.5 * z * (1.0 - t * t) * (k0 * (1.0 + 3.0 * k1 * zz))
                m_ref[...] += nn(u, w2)
                dz = (nt(dm_ref[...], w2) * slope).astype(BF)
                dh_ref[...] += nt(dz, w1)
                g1[:, :, :, :, cols] = nn(h3T_ref[...], dz).astype(BF).reshape(2, 2, 2, width // BLOCKS, chunk)
                for g0 in range(2):
                    half = chunk // 4
                    val = tn(u[:, g0 * 2 * half : (g0 + 1) * 2 * half], dm_ref[...]).astype(BF)
                    for q in range(seq):
                        lane = (q % 2) * 2 * group
                        g2[ca, cb, g0, q // 2, :, lane : lane + group] = val[:half, q * group : (q + 1) * group]
                        g2[ca, cb, g0, q // 2, :, lane + group : lane + 2 * group] = val[half:, q * group : (q + 1) * group]
                return carry

            lax.fori_loop(0, seq, one, 0)
            grads.fc2.begin()
            grads.fc1.begin()
            dy = r.cot[...].astype(F32)
            m = m_ref[...]
            x2w = r.x2[...]
            r.out_block_out[...] = (x2w + pick(mods, seg, 5, width) * m).astype(BF)
            store("block_out")
            clip_sum(5, dy * m)
            dh = dh_ref[...]
            nw, rstd = norm_parts(x2w)
            clip_sum(3, dh)
            clip_sum(4, dh * nw)
            r.dx[...] = dy + norm_back(dh * (1.0 + pick(mods, seg, 4, width)), nw, rstd)

        pl.run_scoped(feed, v((tok, width), BF), v((width, tok), BF), v((tok, width), BF), v((tok, width), F32), v((tok, width), F32))

        for c in (loads.w_cout, loads.coT, loads.cqT, loads.lsec, loads.kv, loads.ckT):
            c.wait()

        def cross_back(dcoT, dcqT, biasc):
            dc = r.dx[...].astype(BF)
            dcoT[...] = nt(weight("cout"), dc).astype(BF)
            square("cout", lambda i: r.coT[pl.ds(pl.multiple_of(i * group, group), group), :], dc)
            grads.cout.begin()
            tcol = column(codes[2:3, :keys])
            biasc[...] = jnp.where(jnp.broadcast_to(tcol[:, :1], (keys, tok)) == seg_row, 0.0, MASKED)
            grads.fc2.step()
            grads.fc1.step()
            kv = r.kv

            def pair(p, carry):
                cols = pl.ds(pl.multiple_of(p * 128, 128), 128)
                vcols = pl.ds(pl.multiple_of(width + p * 128, 128), 128)
                ck, cv = kv[:, cols], kv[:, vcols]
                parts_k, parts_v = [], []
                for a in range(2):
                    hrows = pl.ds(pl.multiple_of(p * 128 + a * HD, HD), HD)
                    q_h, do_h = r.cqT[hrows, :], dcoT[hrows, :]
                    lse_h = r.lsec[pl.ds(2 * p + a, 1), :]
                    pr = jnp.exp(nn(ck[:, a * HD : (a + 1) * HD], q_h) + biasc[...] - lse_h)
                    dpr = nn(cv[:, a * HD : (a + 1) * HD], do_h)
                    delta = jnp.sum(pr * dpr, axis=0, keepdims=True)
                    ds = (pr * (dpr - delta)).astype(BF)
                    parts_k.append(nt(ds, q_h))
                    parts_v.append(nt(pr.astype(BF), do_h))
                    dcqT[hrows, :] = nn(r.ckT[hrows, :], ds) * SCALE
                kv[:, cols] = jnp.concatenate(parts_k, axis=1).astype(BF)
                kv[:, vcols] = jnp.concatenate(parts_v, axis=1).astype(BF)
                return carry

            lax.fori_loop(0, H // 2, pair, 0)
            dcq = dcqT[...].T.astype(BF)
            loads.w_cq.wait()
            loads.h2T.wait()
            loads.x1.wait()
            dh2 = nt(dcq, weight("cq"))
            square("cq", lambda i: r.h2T[pl.ds(pl.multiple_of(i * group, group), group), :], dcq)
            nw, rstd = norm_parts(r.x1[...])
            r.dx[...] += norm_back(dh2, nw, rstd)

        pl.run_scoped(cross_back, v((width, tok), BF), v((width, tok), F32), v((keys, tok), F32))

        for c in (loads.w_proj, loads.aout, loads.oT):
            c.wait()
        dx1 = r.dx[...]
        da = (pick(mods, seg, 2, width) * dx1).astype(BF)
        doT = nt(weight("proj"), da).astype(BF)
        for q in range(seq):
            r.dosend[q] = doT[q * group : (q + 1) * group, :]
        for k in range(1, seq):
            send_do(k).start()
        r.dorecv[s] = r.dosend[s]
        grads.cq.begin()
        clip_sum(2, dx1 * r.aout[...])
        square("proj", lambda i: r.oT[i], da)
        grads.proj.begin()
        grads.cout.step()
        grads.fc1.step()
        for k in range(1, seq):

            def describe_kv(k=k):
                to = lax.rem(s + k, seq)
                lanes = pl.ds(pl.multiple_of(to * quarter, quarter), quarter)
                return r.kv.at[:, lanes], r.dkvr.at[k - 1], {SEQ: to}

            dkv_copies.append(remote.start(describe_kv))
        grads.fc2.step()
        for c in (loads.qT, loads.kT, loads.kn, loads.vn, loads.lse):
            c.wait()

        def self_back(kcol, bias, dk, dv):
            kcol[...] = column(codes[1:2, :full])
            dk[...] = jnp.zeros_like(dk)
            dv[...] = jnp.zeros_like(dv)

            def block(k, carry):
                @pl.when(k > 0)
                def _():
                    send_do(k).wait_recv()

                at = lax.rem(s - k + seq, seq)
                rows = pl.ds(pl.multiple_of(at * tok, tok), tok)
                row_id = lax.broadcasted_iota(jnp.int32, (full, tok), 0)
                col_id = lax.broadcasted_iota(jnp.int32, (full, tok), 1) + at * tok
                key = jnp.broadcast_to(kcol[:, :1], (full, tok))
                bias[...] = jnp.where((key == codes[0:1, rows]) | (row_id == col_id), 0.0, MASKED)
                for h in range(hl):
                    hs = slice(h * HD, (h + 1) * HD)
                    q_h, do_h = r.qT[hs, rows], r.dorecv[at, hs, :]
                    pr = jnp.exp(nn(r.kn[h], q_h) + bias[...] - r.lse[h : h + 1, rows])
                    dpr = nn(r.vn[h], do_h)
                    delta = jnp.sum(pr * dpr, axis=0, keepdims=True)
                    ds = (pr * (dpr - delta)).astype(BF)
                    dk[h] += nt(ds, q_h)
                    dv[h] += nt(pr.astype(BF), do_h)
                    dq = nn(r.kT[hs, :], ds) * SCALE
                    r.dqs[at, :, hs] = dq.T.astype(BF)
                return carry

            lax.fori_loop(0, seq, block, 0)
            for h in range(hl):
                for b in range(seq):
                    br = slice(b * tok, (b + 1) * tok)
                    r.dqs[b, :, group + h * HD : group + (h + 1) * HD] = dk[h, br, :].astype(BF)
                    r.dqs[b, :, 2 * group + h * HD : 2 * group + (h + 1) * HD] = dv[h, br, :].astype(BF)

        pl.run_scoped(self_back, v((full, 128), F32), v((full, tok), F32), v((hl, full, HD), F32), v((hl, full, HD), F32))

    pl.run_scoped(
        middle,
        v((width, keys), BF),
        v((group, full), BF),
        v((group, full), BF),
        v((hl, full, HD), BF),
        v((hl, full, HD), BF),
    )

    dq_base = remote.slots(seq)

    def send_dq(k):
        to = lax.rem(s + k, seq)
        return remote.make(r.dqs.at[to], r.dqr.at[s], dq_base + k, {SEQ: to})

    for k in range(1, seq):
        send_dq(k).start()
    r.dqr[s] = r.dqs[s]

    def tail(h1, text, wqkv, wckv, dqf):
        tail_loads = [
            local.start(a, b)
            for a, b in ((r.in_h1, h1), (r.w_qkv, wqkv), (r.in_text, text), (r.w_ckv, wckv))
        ]
        loads.x.wait()
        tail_loads[0].wait()
        gq = tn(h1[...].reshape(full, width), r.dqs[...].reshape(full, 3 * group))
        r.g_qkv[...] = gq.astype(BF).reshape(2, 2, 2, width // BLOCKS, 3 * group)
        grads.qkv.begin()
        grads.cq.step()
        grads.proj.step()
        grads.fc2.step()
        grads.cout.step()
        grads.fc1.step()
        for c in dkv_copies:
            c().wait_recv()
        own = r.kv[:, pl.ds(pl.multiple_of(s * quarter, quarter), quarter)].astype(F32)
        for k in range(seq - 1):
            own = own + r.dkvr[k].astype(F32)
        r.dkvq[...] = own.astype(BF).reshape(seq, tl, quarter)
        kv_base = remote.slots(seq)

        def send_kv(k):
            to = lax.rem(s + k, seq)
            return remote.make(r.dkvq.at[to], r.dkvl.at[s], kv_base + k, {SEQ: to})

        for k in range(1, seq):
            send_kv(k).start()
        r.dkvl[s] = r.dkvq[s]
        tail_loads[2].wait()
        gc = tn(text[...].reshape(keys, dc_all), r.dkvq[...].reshape(keys, quarter))
        r.g_ckv[...] = gc.astype(BF).reshape(2, 2, 2, dc_all // BLOCKS, quarter)
        grads.ckv.begin()
        grads.qkv.step()
        for k in range(1, seq):
            send_dq(k).wait_recv()
        for b in range(seq):
            got = r.dqr[b]
            for t in range(3):
                dqf[:, t * width + b * group : t * width + (b + 1) * group] = got[:, t * group : (t + 1) * group]
        tail_loads[1].wait()
        dh1 = nt(dqf[...], wqkv[...])
        nx, rstd = norm_parts(r.x[...].astype(F32))
        clip_sum(0, dh1)
        clip_sum(1, dh1 * nx)
        dm_copies = []
        part = 6 * width // seq
        for k in range(1, seq):

            def describe_dm(k=k):
                to = lax.rem(s + k, seq)
                lanes = pl.ds(pl.multiple_of(to * part, part), part)
                return r.dmod.at[:, lanes], r.dmr.at[k - 1], {SEQ: to}

            dm_copies.append(remote.start(describe_dm))
        back = norm_back(dh1 * (1.0 + pick(mods, seg, 1, width)), nx, rstd)
        r.out_grad_frames[...] = (r.dx[...] + back).astype(BF)
        store("grad_frames")
        grads.ckv.step()
        grads.qkv.step()
        grads.cq.step()
        grads.proj.step()
        for c in dm_copies:
            c().wait_recv()
        total = r.dmod[:, pl.ds(pl.multiple_of(s * part, part), part)]
        for k in range(seq - 1):
            total = total + r.dmr[k]
        r.dmall[d] = total

        def send_dm(j):
            to = lax.rem(d + j, dp)
            return remote.make(r.dmall.at[d], r.dmall.at[d], dm_base + j, {DP: to})

        def start_dm(j, carry):
            send_dm(j).start()
            return carry

        lax.fori_loop(1, dp, start_dm, 0)
        for k in range(1, seq):
            send_kv(k).wait_recv()
        tail_loads[3].wait()
        gt = nt(r.dkvl[0], wckv[:, 0:quarter])
        for b in range(1, seq):
            gt = gt + nt(r.dkvl[b], wckv[:, b * quarter : (b + 1) * quarter])
        r.out_grad_text[...] = gt.astype(BF)
        store("grad_text")
        grads.fc2.step()
        grads.cout.step()
        grads.qkv.step()
        q_base = remote.slots(3)

        def send_q(t):
            b = 4 * t + s
            to = lax.div(b, 3)
            slot = b - 3 * to
            return to, slot, pltpu.make_async_remote_copy(
                src_ref=r.fq.at[t],
                dst_ref=r.rq.at[slot],
                send_sem=r.ssem.at[q_base + t],
                recv_sem=r.rsem.at[q_base + slot],
                device_id={SEQ: to},
                device_id_type=MESH,
            )

        for t in range(3):
            to, slot, copy = send_q(t)

            @pl.when(to != s)
            def _():
                copy.start()

            @pl.when(to == s)
            def _():
                r.rq[slot] = r.fq[t]

        grads.ckv.step()
        grads.cq.step()
        grads.proj.step()
        grads.fc1.step()
        grads.cout.step()
        grads.ckv.step()
        grads.cq.step()
        grads.proj.step()

        def wait_dm(j, carry):
            send_dm(j).wait_recv()
            send_emb(j).wait_recv()
            return carry

        own_emb.wait()
        lax.fori_loop(1, dp, wait_dm, 0)
        emb = r.emball[...].reshape(dp * 8, 128)
        allm = r.dmall[...].reshape(dp * 8, part)
        high = allm.astype(BF)
        rest = (allm - high.astype(F32)).astype(BF)
        ga = tn(emb, high) + tn(emb, rest)
        r.out_ada[...] = ga[: width // dp]
        store("ada")
        for j in range(3):
            src = lax.rem(3 * s + j, seq)

            @pl.when(src != s)
            def _():
                remote.make(r.fq.at[j], r.rq.at[j], q_base + j, {SEQ: src}).wait_recv()

            r.out_qkv[:, j * group : (j + 1) * group] = r.rq[j]
        store("qkv")

        for t in range(3):
            to, slot, copy = send_q(t)

            @pl.when(to != s)
            def _():
                copy.wait_send()

        for k in range(1, seq):
            send_do(k).wait_send()
            send_dq(k).wait_send()
            send_kv(k).wait_send()

        def wait_sent(j, carry):
            send_dm(j).wait_send()
            send_emb(j).wait_send()
            return carry

        lax.fori_loop(1, dp, wait_sent, 0)
        for c in remote.open:
            c().wait_send()
        for n, slot in stores:
            stored(n, slot).wait()

    pl.run_scoped(
        tail,
        v((seq, tok, width), BF),
        v((seq, tl, dc_all), BF),
        v((width, 3 * width), BF),
        v((dc_all, 2 * width), BF),
        v((tok, 3 * width), BF),
    )


def run_backward(dims, dp, fwd, args):
    seq, tok, full, width, keys, group, dc = dims
    hl, tl, block = H // seq, keys // seq, width // BLOCKS
    ff = 4 * width
    v = pltpu.VMEM
    lead = (2, 2, 2)
    gshape = dict(
        fc1=(block, ff),
        fc2=(2, ff // BLOCKS // 2, width),
        cout=(2, block // 2, width),
        cq=(2, block // 2, width),
        proj=(2, block // 2, width),
        ckv=(dc // BLOCKS, 2 * width // seq),
        qkv=(block, 3 * group),
    )
    names, ins, specs = [], [], []

    def add_in(spec=ANY, **kw):
        for name, value in kw.items():
            names.append(name)
            ins.append(value)
            specs.append(spec)

    add_in(codes=fwd.codes, spec=INV)
    add_in(mods=fwd.mods, spec=INV)
    add_in(in_x=args.x)
    add_in(in_cot=args.cot)
    add_in(in_emb=args.emb)
    for n in K2_LOADS + K2_HELD + ("h1", "text"):
        add_in(**{"in_" + n: fwd[n]})
    for n in K2_WEIGHTS:
        add_in(**{"w_" + n: args[n].reshape(lead + gshape[n])})
    add_in(w_ckv=args.ckv)
    add_in(w_qkv=args.qkv)

    outs = dict(
        block_out=((tok, width), BF),
        grad_frames=((tok, width), BF),
        grad_text=((tl, dc), BF),
        ada=((width // dp, 6 * width // seq), F32),
        qkv=((block, 3 * group), F32),
        proj=((block, group), F32),
        cq=((block, group), F32),
        ckv=((dc // BLOCKS, 2 * width // seq), F32),
        cout=((block, group), F32),
        fc1=((block, ff // seq), F32),
        fc2=((group, ff // BLOCKS), F32),
    )
    for n in K2_OUTS:
        names.append("hbm_" + n)
    scratch = []

    def add(**kw):
        for name, (shape, dtype) in kw.items():
            names.append(name)
            scratch.append(v(shape, dtype))

    for n in K2_OUTS:
        add(**{"out_" + n: outs[n]})
    add(cot=((tok, width), BF))
    add(x=((tok, width), BF))
    for n in K2_LOADS:
        add(**{n: (fwd[n].shape, fwd[n].dtype)})
    for n, (kind, order) in GRADS.items():
        add(**{"g_" + n: (lead + gshape[n], BF)})
        for i, b in enumerate(grad_buffers(gshape[n], kind, order, seq)):
            names.append("r_%s%d" % (n, i))
            scratch.append(b)
    quarter = 2 * width // seq
    add(dx=((tok, width), F32))
    add(dkvr=((seq - 1, keys, quarter), BF))
    add(dkvq=((seq, tl, quarter), BF))
    add(dkvl=((seq, tl, quarter), BF))
    add(dosend=((seq, group, tok), BF))
    add(dorecv=((seq, group, tok), BF))
    add(dqs=((seq, tok, 3 * group), BF))
    add(dqr=((seq, tok, 3 * group), BF))
    add(dmod=((8, 6 * width), F32))
    add(dmr=((seq - 1, 8, 6 * width // seq), F32))
    add(dmall=((dp, 8, 6 * width // seq), F32))
    add(emball=((dp, 8, 128), BF))
    add(fq=((3, block, group), F32))
    add(rq=((3, block, group), F32))
    count = 2 * dp + 64
    for n, k in dict(lsem=64, ssem=count, rsem=count).items():
        names.append(n)
        scratch.append(pltpu.SemaphoreType.DMA((k,)))
    got = pl.pallas_call(
        functools.partial(backward_kernel, dims, tuple(names), dp),
        out_shape=[jax.ShapeDtypeStruct(*outs[n]) for n in K2_OUTS],
        in_specs=specs,
        out_specs=[ANY] * len(K2_OUTS),
        scratch_shapes=scratch,
        compiler_params=pltpu.CompilerParams(
            collective_id=1, has_side_effects=True, vmem_limit_bytes=67043328
        ),
        name="backward_part",
    )(*ins)
    return Bag(zip(K2_OUTS, got))


def hand_over(*refs):
    count = len(K2_OUTS)
    ins, outs, held, sems = refs[:count], refs[count : 2 * count], refs[2 * count : -1], refs[-1]
    first = [pltpu.make_async_copy(a, b, sems.at[0, i]) for i, (a, b) in enumerate(zip(ins, held))]
    second = [pltpu.make_async_copy(a, b, sems.at[1, i]) for i, (a, b) in enumerate(zip(held, outs))]
    for c in first:
        c.start()
    for c, n in zip(first, second):
        c.wait()
        n.start()
    for c in second:
        c.wait()


def run_hand_over(g):
    values = [g[n] for n in K2_OUTS]
    got = pl.pallas_call(
        hand_over,
        out_shape=[jax.ShapeDtypeStruct(a.shape, a.dtype) for a in values],
        in_specs=[ANY] * len(values),
        out_specs=[ANY] * len(values),
        scratch_shapes=[pltpu.VMEM(a.shape, a.dtype) for a in values] + [pltpu.SemaphoreType.DMA((2, len(values)))],
        name="hand_over",
    )(*values)
    return Bag(zip(K2_OUTS, got))


def per_device(
    frames, seg_ids, padding, step_ids, text_states, text_len, w_ada, w_qkv, w_proj, w_cq, w_ckv, w_cout, w_fc1, w_fc2,
    cotangent,
):
    rows, tok, width = frames.shape
    seq, dp = lax.axis_size(SEQ), lax.axis_size(DP)
    segs = step_ids.shape[1]
    full = seg_ids.shape[1]
    tl, dc = text_states.shape[2], text_states.shape[3]
    keys = segs * tl * seq
    group = (H // seq) * HD
    dims = (seq, tok, full, width, keys, group, dc)
    emb = embed_steps(jnp.pad(step_ids[0], (0, 8 - segs)), width).astype(BF)
    span = width // dp
    emb_parts = jnp.pad(jnp.swapaxes(emb.reshape(8, dp, span), 0, 1), ((0, 0), (0, 0), (0, 128 - span)))
    x = frames[0]
    text = text_states.reshape(segs * tl, dc)
    fwd = run_forward(dims, (x, text, seg_ids, padding, text_len, emb, w_ada, w_qkv, w_ckv, w_proj, w_cq, w_cout))
    args = Bag(
        x=x, cot=cotangent[0], emb=emb_parts, ckv=w_ckv, qkv=w_qkv,
        fc1=w_fc1, fc2=w_fc2, cout=w_cout, cq=w_cq, proj=w_proj,
    )
    g = run_hand_over(run_backward(dims, dp, fwd, args))
    stride = dp // BLOCKS
    if stride > 1:
        groups = [[b * stride + j for j in range(stride)] for b in range(BLOCKS)]
        for n in GRADS:
            g[n] = lax.psum_scatter(g[n], DP, scatter_dimension=1 if n == "fc2" else 0, axis_index_groups=groups, tiled=True)
    return (
        g.block_out.reshape(frames.shape),
        g.grad_frames.reshape(frames.shape),
        g.grad_text.reshape(text_states.shape),
        g.ada, g.qkv, g.proj, g.cq, g.ckv, g.cout, g.fc1, g.fc2.T,
    )


def solution(mesh):
    own, row, rep = P(DP, SEQ, None), P(DP, None), P()
    text, grad = P(DP, None, SEQ, None), P(DP, SEQ)
    return jax.shard_map(
        per_device,
        mesh=mesh,
        in_specs=(own, row, row, row, text, row) + (rep,) * 8 + (own,),
        out_specs=(own, own, text) + (grad,) * 8,
        check_vma=False,
    )
```

```python
import functools
import math

import jax
import jax.numpy as jnp
from jax import lax
from jax.experimental import pallas as pl
from jax.experimental.pallas import tpu as pltpu
from jax.sharding import PartitionSpec as P

H = 12
HD = 64
BLOCKS = 8
SEQ = "seq"
DP = "dp"
COLS, PACK = 1, 2
CUT, XY1, XY2, L0, L1, L2 = 3, 4, 5, 6, 7, 8
BF = jnp.bfloat16
F32 = jnp.float32
MESH = pl.DeviceIdType.MESH
MASKED = -1e30
EPS = 1e-06
SCALE = HD ** (-0.5)
ANY = pl.BlockSpec(memory_space=pl.ANY)
INV = pl.BlockSpec(memory_space=pltpu.VMEM)


def nn(a, b):
    return lax.dot_general(a, b, (((1,), (0,)), ((), ())), preferred_element_type=F32)


def nt(a, b):
    return lax.dot_general(a, b, (((1,), (1,)), ((), ())), preferred_element_type=F32)


def tn(a, b):
    return lax.dot_general(a, b, (((0,), (0,)), ((), ())), preferred_element_type=F32)


def embed_steps(step_values, width_all):
    half_width = width_all // 2
    frequency = jnp.exp(
        -math.log(10000.0) * jnp.arange(half_width).astype(F32) / half_width
    )
    angles = step_values.astype(F32)[..., None] * frequency
    return jax.nn.silu(jnp.concatenate([jnp.cos(angles), jnp.sin(angles)], axis=-1))


def norm_parts(v):
    centered = v - jnp.mean(v, axis=-1, keepdims=True)
    rstd = lax.rsqrt(jnp.mean(centered * centered, axis=-1, keepdims=True) + EPS)
    return centered * rstd, rstd


def norm_back(g, n, rstd):
    return (g - jnp.mean(g, axis=-1, keepdims=True) - n * jnp.mean(g * n, axis=-1, keepdims=True)) * rstd


def pick(mods, seg, part, width):
    low = part * width
    a = mods[0:1, low : low + width]
    b = mods[1:2, low : low + width]
    c = mods[2:3, low : low + width]
    return jnp.where(seg == 0.0, a, jnp.where(seg == 1.0, b, c))


def column(row):
    return jnp.broadcast_to(row, (128, row.shape[1])).T


class Bag(dict):
    __getattr__ = dict.__getitem__


class Remote:
    def __init__(self, send, recv):
        self.send, self.recv, self.used, self.open = send, recv, 0, []

    def slots(self, count):
        first = self.used
        self.used += count
        return first

    def make(self, src, dst, slot, where):
        return pltpu.make_async_remote_copy(
            src_ref=src,
            dst_ref=dst,
            send_sem=self.send.at[slot],
            recv_sem=self.recv.at[slot],
            device_id=where,
            device_id_type=MESH,
        )

    def start(self, describe, when=None):
        slot = self.slots(1)

        def again():
            src, dst, where = describe()
            return self.make(src, dst, slot, where)

        def launch():
            again().start()

        def sent():
            again().wait_send()

        if when is None:
            launch()
            self.open.append(sent)
        else:
            pl.when(when())(launch)
            self.open.append(lambda: pl.when(when())(sent))
        return again


class Local:
    def __init__(self, sems):
        self.sems, self.used = sems, 0

    def start(self, src, dst):
        copy = pltpu.make_async_copy(src, dst, self.sems.at[self.used])
        self.used += 1
        copy.start()
        return copy


def greet(seq, at_seq, dp_peers):
    barrier = pltpu.get_barrier_semaphore()
    for k in range(1, seq):
        pl.semaphore_signal(
            barrier, inc=1, device_id={SEQ: lax.rem(at_seq + k, seq)}, device_id_type=MESH
        )
    for peer in dp_peers:
        pl.semaphore_signal(barrier, inc=1, device_id={DP: peer}, device_id_type=MESH)
    pl.semaphore_wait(barrier, seq - 1 + len(dp_peers))


K1_OUTS = tuple(dict(h1=0, qT=0, kT=0, kn=0, vn=0, lse=0, oT=0, aout=0, x1=0, h2T=0, cqT=0, kv=0, ckT=0, lsec=0, coT=0, x2=0, text=0, mods=0, codes=0))


def forward_kernel(dims, segs, *refs):
    seq, tok, full, width, keys, group, dc = dims
    hl = H // seq
    ins, refs = refs[:12], refs[12:]
    x_hbm, text_hbm, seg_in, pad_in, len_in, emb, wada_hbm, wqkv_hbm, wckv_hbm, wp_hbm, wcq_hbm, wco_hbm = ins
    outs, refs = Bag(zip(K1_OUTS, refs[: len(K1_OUTS)])), refs[len(K1_OUTS) :]
    (
        x_all, text_all, wg, wckv, wp, wcq, wco, qT, kT, vT, kn, vn, lse, osend, orecv, aout, x1, h2T, cqT, kv, kvT,
        lsec, coT, x2, bias, biasc, kcol, tcol, xin, wada, mods, codes, lsem, ssem, rsem,
    ) = refs
    local, remote = Local(lsem), Remote(ssem, rsem)
    s = lax.axis_index(SEQ)
    load_x = local.start(x_hbm, xin)
    load_own = local.start(x_hbm, x_all.at[s])
    load_ada = local.start(wada_hbm, wada)
    first = lax.div(s * group, 128) * 128
    odd = lax.rem(s * group, 128) > 0
    load_wg = [
        local.start(
            wqkv_hbm.at[:, pl.ds(pl.multiple_of(t * width + first, 128), 256)], wg.at[:, pl.ds(t * 256, 256)]
        )
        for t in range(3)
    ]
    load_text = local.start(text_hbm, text_all.at[s])
    load_w = [local.start(a, b) for a, b in ((wckv_hbm, wckv), (wp_hbm, wp), (wcq_hbm, wcq), (wco_hbm, wco))]
    greet(seq, s, ())

    base_x = remote.slots(seq)
    base_t = remote.slots(seq)
    base_o = remote.slots(seq)

    def send_x(k):
        return remote.make(x_hbm, x_all.at[s], base_x + k, {SEQ: lax.rem(s + k, seq)})

    def send_t(k):
        return remote.make(text_hbm, text_all.at[s], base_t + k, {SEQ: lax.rem(s + k, seq)})

    for k in range(1, seq):
        send_x(k).start()
    for k in range(1, seq):
        send_t(k).start()

    tl = keys // seq // segs
    place = lax.broadcasted_iota(jnp.int32, (1, full), 1).astype(F32)
    block = jnp.floor((place + 0.5) / tl)
    owner = jnp.floor((block + 0.5) / segs)
    clip = block - owner * segs
    length = jnp.zeros((1, full), F32)
    for c in range(segs):
        length = jnp.where(clip == c, jnp.broadcast_to(len_in[0:1, c : c + 1].astype(F32), (1, full)), length)
    codes[...] = jnp.zeros_like(codes)
    codes[0:1, :] = seg_in[...].astype(F32)
    codes[1:2, :] = jnp.where(pad_in[...] == 1, seg_in[...].astype(F32), -1.0)
    codes[2:3, :] = jnp.where(owner * tl + place - block * tl < length, clip, -1.0)
    save_codes = local.start(codes, outs.codes)
    kcol[...] = column(codes[1:2, :full])
    tcol[...] = column(codes[2:3, :keys])
    load_x.wait()
    load_own.wait()
    load_ada.wait()
    mods[...] = nn(emb[...], wada[...])
    save_mods = local.start(mods, outs.mods)
    for c in load_wg:
        c.wait()

    def project(k, carry):
        @pl.when(k > 0)
        def _():
            send_x(k).wait_recv()

        at = lax.rem(s - k + seq, seq)
        rows = pl.ds(pl.multiple_of(at * tok, tok), tok)
        seg = column(codes[0:1, rows])[:, :1]
        seg = jnp.broadcast_to(seg, (tok, width))
        n, _ = norm_parts(x_all[at].astype(F32))
        h1 = (n * (1.0 + pick(mods, seg, 1, width)) + pick(mods, seg, 0, width)).astype(BF)
        x_all[at] = h1
        wide = nn(h1, wg[...])
        out = jnp.concatenate(
            [
                jnp.where(odd, wide[:, t * 256 + 64 : t * 256 + 64 + group], wide[:, t * 256 : t * 256 + group])
                for t in range(3)
            ],
            axis=1,
        )
        for h in range(hl):
            kn[h, rows, :] = out[:, group + h * HD : group + (h + 1) * HD].astype(BF)
            vn[h, rows, :] = out[:, 2 * group + h * HD : 2 * group + (h + 1) * HD].astype(BF)
        low = out.astype(BF).astype(F32)
        outT = low.T
        qT[:, rows] = (outT[:group] * SCALE).astype(BF)
        kT[:, rows] = outT[group : 2 * group].astype(BF)
        vT[:, rows] = outT[2 * group :].astype(BF)
        return carry

    lax.fori_loop(0, seq, project, 0)
    saves = [save_mods, save_codes] + [
        local.start(a, b)
        for a, b in ((x_all, outs.h1), (qT, outs.qT), (kT, outs.kT), (kn, outs.kn), (vn, outs.vn))
    ]

    def send_o(k):
        at = lax.rem(s + k, seq)
        return remote.make(osend.at[at], orecv.at[s], base_o + k, {SEQ: at})

    def attend(k, carry):
        at = lax.rem(s + 1 + k, seq)
        rows = pl.ds(pl.multiple_of(at * tok, tok), tok)
        seg = codes[0:1, rows]
        row_id = lax.broadcasted_iota(jnp.int32, (full, tok), 0)
        col_id = lax.broadcasted_iota(jnp.int32, (full, tok), 1) + at * tok
        key = jnp.broadcast_to(kcol[:, :1], (full, tok))
        bias[...] = jnp.where((key == seg) | (row_id == col_id), 0.0, MASKED)

        def head(h, c2):
            hrows = pl.ds(pl.multiple_of(h * HD, HD), HD)
            st = nn(kn[h], qT[hrows, rows]) + bias[...]
            peak = jnp.max(st, axis=0, keepdims=True)
            ex = jnp.exp(st - peak)
            total = jnp.sum(ex, axis=0, keepdims=True)
            ov = nn(vT[hrows, :], ex.astype(BF)) * (1.0 / total)
            osend[at, hrows, :] = ov.astype(BF)
            lse[pl.ds(h, 1), rows] = peak + jnp.log(total)
            return c2

        lax.fori_loop(0, hl, head, 0)

        @pl.when(k < seq - 1)
        def _():
            send_o(k + 1).start()

        return carry

    lax.fori_loop(0, seq, attend, 0)
    orecv[s] = osend[s]

    load_text.wait()
    for k in range(1, seq):
        send_t(k).wait_recv()
    saves.append(local.start(text_all, outs.text))
    saves.append(local.start(lse, outs.lse))
    for c in load_w:
        c.wait()
    tl = keys // seq

    def project_text(b, carry):
        trows = pl.ds(pl.multiple_of(b * tl, tl), tl)
        kv[trows, :] = nn(text_all[b], wckv[...]).astype(BF)
        return carry

    lax.fori_loop(0, seq, project_text, 0)

    def turn_text(c, carry):
        cols = pl.ds(pl.multiple_of(c * 256, 256), 256)
        kvT[cols, :] = kv[:, cols].astype(F32).T.astype(BF)
        return carry

    lax.fori_loop(0, 2 * width // 256, turn_text, 0)
    rows = pl.ds(pl.multiple_of(s * tok, tok), tok)
    seg_row = codes[0:1, rows]
    biasc[...] = jnp.where(jnp.broadcast_to(tcol[:, :1], (keys, tok)) == seg_row, 0.0, MASKED)
    saves.append(local.start(kv, outs.kv))
    saves.append(local.start(kvT.at[pl.ds(0, width)], outs.ckT))

    for k in range(1, seq):
        send_o(k).wait_recv()
    saves.append(local.start(orecv, outs.oT))
    seg = jnp.broadcast_to(column(seg_row)[:, :1], (tok, width))
    branch = tn(orecv[...].reshape(width, tok), wp[...])
    aout[...] = branch
    mid = xin[...].astype(F32) + pick(mods, seg, 2, width) * branch
    x1[...] = mid
    n, _ = norm_parts(mid)
    h2 = n.astype(BF)
    h2T[...] = n.astype(BF).astype(F32).T.astype(BF)
    cq = nn(h2, wcq[...]).astype(BF).astype(F32)
    cqT[...] = (cq.T * SCALE).astype(BF)
    saves += [local.start(a, b) for a, b in ((aout, outs.aout), (x1, outs.x1), (h2T, outs.h2T), (cqT, outs.cqT))]

    def cross(p, carry):
        cols = pl.ds(pl.multiple_of(p * 128, 128), 128)
        pair = kv[:, cols]
        for a in range(2):
            hrows = pl.ds(pl.multiple_of(p * 128 + a * HD, HD), HD)
            vrows = pl.ds(pl.multiple_of(width + p * 128 + a * HD, HD), HD)
            st = nn(pair[:, a * HD : (a + 1) * HD], cqT[hrows, :]) + biasc[...]
            peak = jnp.max(st, axis=0, keepdims=True)
            ex = jnp.exp(st - peak)
            total = jnp.sum(ex, axis=0, keepdims=True)
            ov = nn(kvT[vrows, :], ex.astype(BF)) * (1.0 / total)
            coT[hrows, :] = ov.astype(BF)
            lsec[pl.ds(2 * p + a, 1), :] = peak + jnp.log(total)
        return carry

    lax.fori_loop(0, H // 2, cross, 0)
    x2[...] = x1[...] + tn(coT[...], wco[...])
    saves += [local.start(a, b) for a, b in ((lsec, outs.lsec), (coT, outs.coT), (x2, outs.x2))]
    for k in range(1, seq):
        send_x(k).wait_send()
        send_t(k).wait_send()
        send_o(k).wait_send()
    for c in saves:
        c.wait()


def run_forward(dims, args):
    seq, tok, full, width, keys, group, dc = dims
    hl = H // seq
    shapes = dict(
        h1=((seq, tok, width), BF),
        qT=((group, full), BF),
        kT=((group, full), BF),
        kn=((hl, full, HD), BF),
        vn=((hl, full, HD), BF),
        lse=((8, full), F32),
        oT=((seq, group, tok), BF),
        aout=((tok, width), F32),
        x1=((tok, width), F32),
        h2T=((width, tok), BF),
        cqT=((width, tok), BF),
        kv=((keys, 2 * width), BF),
        ckT=((width, keys), BF),
        lsec=((16, tok), F32),
        coT=((width, tok), BF),
        x2=((tok, width), F32),
        text=((seq, keys // seq, dc), BF),
        mods=((8, 6 * width), F32),
        codes=((8, full), F32),
    )
    v = pltpu.VMEM
    scratch = [
        v((seq, tok, width), BF), v((seq, keys // seq, dc), BF), v((width, 3 * 256), BF), v((dc, 2 * width), BF),
        v((width, width), BF), v((width, width), BF), v((width, width), BF),
        v((group, full), BF), v((group, full), BF), v((group, full), BF), v((hl, full, HD), BF), v((hl, full, HD), BF),
        v((8, full), F32), v((seq, group, tok), BF), v((seq, group, tok), BF),
        v((tok, width), F32), v((tok, width), F32), v((width, tok), BF), v((width, tok), BF),
        v((keys, 2 * width), BF), v((2 * width, keys), BF), v((16, tok), F32), v((width, tok), BF), v((tok, width), F32),
        v((full, tok), F32), v((keys, tok), F32), v((full, 128), F32), v((keys, 128), F32), v((tok, width), BF),
        v((width, 6 * width), BF), v((8, 6 * width), F32), v((8, full), F32),
        pltpu.SemaphoreType.DMA((32,)), pltpu.SemaphoreType.DMA((3 * seq,)), pltpu.SemaphoreType.DMA((3 * seq,)),
    ]
    outs = pl.pallas_call(
        functools.partial(forward_kernel, dims, args[4].shape[1]),
        out_shape=[jax.ShapeDtypeStruct(*shapes[n]) for n in K1_OUTS],
        in_specs=[ANY, ANY, INV, INV, INV, INV, ANY, ANY, ANY, ANY, ANY, ANY],
        out_specs=[ANY] * len(K1_OUTS),
        scratch_shapes=scratch,
        compiler_params=pltpu.CompilerParams(
            collective_id=0, has_side_effects=True, vmem_limit_bytes=60 * 1024 * 1024
        ),
        name="forward_part",
    )(*args)
    return Bag(zip(K1_OUTS, outs))


class Grad:
    def __init__(self, ref, kind, order, bufs, where, remote, finish):
        self.ref, self.kind, self.order, self.bufs = ref, kind, order, bufs
        self.s, self.seq, self.d, self.stride, self.bits, self.flip, self.dp = where
        self.remote, self.finish = remote, finish
        self.fixed, self.cut, self.stage, self.copies = {}, False, 0, []

    def view(self, fixed, quarter, lead=None):
        index, lead = [], list(lead or [])
        for bit in (2, 1, 0):
            if bit in fixed:
                index.append(fixed[bit])
            elif lead:
                index.append(lead.pop(0))
            else:
                index.append(slice(None))
        if quarter is not None:
            size = self.ref.shape[-1] // (self.seq if self.kind == COLS else 2)
            if self.kind == COLS:
                lanes = pl.ds(pl.multiple_of(quarter * size, 128), size)
                index += [slice(None), lanes]
            else:
                lanes = pl.ds(pl.multiple_of(lax.rem(quarter, 2) * size, 128), size)
                index += [lax.div(quarter, 2), slice(None), lanes]
        return self.ref.at[tuple(index)]

    def line(self):
        return 2 * self.bits[2] + self.bits[1]

    def chunk(self, fixed, quarter, number):
        number = lax.rem(number, 4)
        return self.view({**fixed, 2: lax.div(number, 2), 1: lax.rem(number, 2)}, quarter)

    def end_halving(self, what, buf):
        for a in range(2):
            for w in range(2 if what == XY1 else 1):
                owner = self.flip[2 - a] if w else self.s

                def add(b, carry):
                    own = self.view({**self.fixed, 2: a}, owner, [b])
                    more = buf[a, w, b] if what == XY1 else buf[a, b]
                    own[...] = (own[...].astype(F32) + more.astype(F32)).astype(BF)
                    return carry

                lax.fori_loop(0, 2, add, 0)

    def end_line(self, t, buf):
        quarter, line = self.s if self.cut else None, self.line()
        above, below = self.copies

        def take(copy, side, number):
            copy().wait_recv()
            own = self.chunk(self.fixed, quarter, number)
            own[...] = (own[...].astype(F32) + buf[side].astype(F32)).astype(BF)

        @pl.when((line >= 1) & (line <= t + 1))
        def _():
            take(above, 0, line + 2 - t)

        @pl.when((line <= 2) & (line >= 2 - t))
        def _():
            take(below, 1, line + 2 + t)

    def begin(self):
        what, buf = self.order[self.stage], self.bufs[self.stage]
        self.copies = []
        if what == XY1:
            for a in range(2):
                to = self.flip[1 + a]
                for w, owner in enumerate((to, self.flip[3])):

                    def describe(a=a, w=w, owner=owner, to=to, fixed=dict(self.fixed)):
                        return self.view({**fixed, 2: a}, owner), buf.at[a, w], {SEQ: to}

                    self.copies.append(self.remote.start(describe))
        elif what == XY2:
            for a in range(2):

                def describe(a=a, to=self.flip[2 - a], fixed=dict(self.fixed)):
                    return self.view({**fixed, 2: a}, to), buf.at[a], {SEQ: to}

                self.copies.append(self.remote.start(describe))
        elif what >= L0:
            t = what - L0

            def upward(fixed=dict(self.fixed), quarter=self.s if self.cut else None):
                peer = lax.rem(self.d + 2 * self.stride, self.dp)
                return self.chunk(fixed, quarter, self.line() + 3 - t), buf.at[0], {DP: peer}

            def downward(fixed=dict(self.fixed), quarter=self.s if self.cut else None):
                peer = lax.rem(self.d - 2 * self.stride + self.dp, self.dp)
                return self.chunk(fixed, quarter, self.line() + 1 + t), buf.at[1], {DP: peer}

            self.copies.append(self.remote.start(upward, lambda: self.line() <= t))
            self.copies.append(self.remote.start(downward, lambda: self.line() >= 3 - t))
        elif what == CUT:
            for k in range(1, self.seq):

                def describe(k=k, fixed=dict(self.fixed)):
                    to = lax.rem(self.s + k, self.seq)
                    return self.view(fixed, to), buf.at[k - 1], {SEQ: to}

                self.copies.append(self.remote.start(describe))
        else:

            def describe(fixed=dict(self.fixed), quarter=self.s if self.cut else None):
                mine = self.bits[what]
                peer = self.d + (1 - 2 * mine) * (self.stride << what)
                return self.view({**fixed, what: 1 - mine}, quarter), buf, {DP: peer}

            self.copies.append(self.remote.start(describe))

    def end(self):
        what, buf = self.order[self.stage], self.bufs[self.stage]
        if what >= L0:
            self.end_line(what - L0, buf)
            self.stage += 1
            if what == L2:
                self.fixed[1], self.fixed[2] = self.bits[1], self.bits[2]
            return
        for c in self.copies:
            c().wait_recv()
        if what in (XY1, XY2):
            self.end_halving(what, buf)
            self.stage += 1
            self.cut = what == XY2
            return
        if what == CUT:
            self.cut = True
        else:
            self.fixed[what] = self.bits[what]
        free = 3 - len(self.fixed)
        quarter = self.s if self.cut else None
        last = self.stage == len(self.order) - 1
        self.stage += 1

        def add(i, carry):
            lead = [lax.rem(lax.div(i, 2 ** (free - 1 - j)), 2) for j in range(free)]
            own = self.view(self.fixed, quarter, lead)
            total = own[...].astype(F32)
            if what == CUT:
                for k in range(self.seq - 1):
                    total = total + buf[tuple([k] + lead)].astype(F32)
            elif lead:
                total = total + buf[tuple(lead)].astype(F32)
            else:
                total = total + buf[...].astype(F32)
            if last:
                self.finish(total)
            else:
                own[...] = total.astype(BF)
            return carry

        if free == 0:
            add(0, 0)
        else:
            lax.fori_loop(0, 2**free, add, 0)

    def step(self):
        self.end()
        if self.stage < len(self.order):
            self.begin()


def grad_buffers(shape, kind, order, seq):
    lead, payload, out, cut, free = 3, list(shape), [], False, 3
    for what in order:
        if what in (CUT, XY1, XY2):
            cut = True
        elif what in (0, 1, 2):
            free -= 1
        elif what == L2:
            free = 0
        p = list(payload)
        if cut:
            if kind == COLS:
                p[-1] //= seq
            else:
                p = [p[1], p[2] // 2]
        head = {CUT: [seq - 1], XY1: [2, 2, 2], XY2: [2, 2], L0: [2], L1: [2], L2: [2]}.get(what, [])
        if what in (CUT, 0, 1, 2):
            head = head + [2] * free
        out.append(pltpu.VMEM(tuple(head + p), BF))
    return out


GRADS = dict(
    fc2=(PACK, (0, XY1, XY2, 1, 2)),
    fc1=(COLS, (0, L0, L1, L2, CUT)),
    cout=(PACK, (0, XY1, XY2, 1, 2)),
    cq=(PACK, (0, XY1, XY2, 1, 2)),
    proj=(PACK, (0, XY1, XY2, 1, 2)),
    ckv=(None, (0, 1, 2)),
    qkv=(None, (0, 1, 2)),
)
K2_OUTS = tuple(dict(block_out=0, grad_frames=0, grad_text=0, ada=0, qkv=0, proj=0, cq=0, ckv=0, cout=0, fc1=0, fc2=0))
K2_LOADS = tuple(dict(x2=0, x1=0, aout=0, oT=0, h2T=0, cqT=0, coT=0, lsec=0, lse=0, kv=0))
K2_HELD = tuple(dict(ckT=0, qT=0, kT=0, kn=0, vn=0))
K2_WEIGHTS = tuple(dict(fc1=0, fc2=0, cout=0, cq=0, proj=0))


def backward_kernel(dims, names, dp, *refs):
    seq, tok, full, width, keys, group, dc_all = dims
    hl, chunk, tl, stride = H // seq, width, keys // seq, dp // BLOCKS
    r = Bag(zip(names, refs))
    local, remote = Local(r.lsem), Remote(r.ssem, r.rsem)
    s, d = lax.axis_index(SEQ), lax.axis_index(DP)
    bits = [lax.rem(lax.div(d, stride << b), 2) for b in range(3)]
    sx, sy = lax.rem(s, 2), lax.div(s, 2)
    flip = [s, s + 1 - 2 * sx, s + 2 - 4 * sy, 3 - s]
    where = (s, seq, d, stride, bits, flip, dp)
    codes, mods = r.codes, r.mods

    loads = Bag()
    loads["x2"] = local.start(r.in_x2, r.x2)
    loads["cot"] = local.start(r.in_cot, r.cot)
    for n in K2_WEIGHTS:
        loads["w_" + n] = local.start(r["w_" + n], r["g_" + n])
    for n in K2_LOADS[1:]:
        loads[n] = local.start(r["in_" + n], r[n])
    loads.x = local.start(r.in_x, r.x)

    stores = []

    def stored(n, slot):
        return pltpu.make_async_copy(r["out_" + n], r["hbm_" + n], r.lsem.at[slot])

    def store(n):
        stores.append((n, local.used))
        stored(n, local.used).start()
        local.used += 1

    barrier = pltpu.get_barrier_semaphore()
    for k in range(1, seq):
        pl.semaphore_signal(barrier, inc=1, device_id={SEQ: lax.rem(s + k, seq)}, device_id_type=MESH)

    def greet_dp(j, carry):
        pl.semaphore_signal(barrier, inc=1, device_id={DP: lax.rem(d + j, dp)}, device_id_type=MESH)
        return carry

    lax.fori_loop(1, dp, greet_dp, 0)
    pl.semaphore_wait(barrier, seq - 1 + dp - 1)

    emb_base = remote.slots(dp)
    dm_base = remote.slots(dp)

    def send_emb(j):
        to = lax.rem(d + j, dp)
        return remote.make(r.in_emb.at[to], r.emball.at[d], emb_base + j, {DP: to})

    def start_emb(j, carry):
        send_emb(j).start()
        return carry

    lax.fori_loop(1, dp, start_emb, 0)
    own_emb = local.start(r.in_emb.at[d], r.emball.at[d])

    def into_cols(n):
        def finish(total):
            r["out_" + n][...] = total
            store(n)

        return finish

    def into_pack(n):
        def finish(total):
            rows, lanes = total.shape
            if n == "fc2":
                turned = total.T
                r.out_fc2[:, 0:rows] = turned[: lanes // 2]
                r.out_fc2[:, rows : 2 * rows] = turned[lanes // 2 :]
            else:
                r["out_" + n][0:rows, :] = total[:, : lanes // 2]
                r["out_" + n][rows : 2 * rows, :] = total[:, lanes // 2 :]
            store(n)

        return finish

    def into_blocks(total):
        for t in range(3):
            r.fq[t] = total[:, t * group : (t + 1) * group]

    grads = Bag()
    for n, (kind, order) in GRADS.items():
        finish = into_blocks if n == "qkv" else (into_pack(n) if kind == PACK else into_cols(n))
        bufs = [r["r_%s%d" % (n, i)] for i in range(len(order))]
        grads[n] = Grad(r["g_" + n], kind, order, bufs, where, remote, finish)

    rows_own = pl.ds(pl.multiple_of(s * tok, tok), tok)
    seg_row = codes[0:1, rows_own]
    seg = jnp.broadcast_to(column(seg_row)[:, :1], (tok, width))
    clip_id = lax.broadcasted_iota(jnp.int32, (16, tok), 0).astype(F32)
    onehot = jnp.where(clip_id == seg_row, 1.0, 0.0).astype(BF)

    def clip_sum(part, value):
        high = value.astype(BF)
        rest = (value - high.astype(F32)).astype(BF)
        r.dmod[:, part * width : (part + 1) * width] = (nn(onehot, high) + nn(onehot, rest))[:8]

    def square(n, lhs, rhs):
        g = r["g_" + n]

        def four(i, carry):
            val = nn(lhs(i), rhs).astype(BF)
            for g0 in range(2):
                for q in range(seq):
                    half = val.shape[0] // 4
                    low = g0 * 2 * half
                    lane = (q % 2) * 2 * group
                    at = (lax.div(i, 2), lax.rem(i, 2), g0, q // 2)
                    g[at + (slice(None), slice(lane, lane + group))] = val[low : low + half, q * group : (q + 1) * group]
                    g[at + (slice(None), slice(lane + group, lane + 2 * group))] = val[
                        low + half : low + 2 * half, q * group : (q + 1) * group
                    ]
            return carry

        lax.fori_loop(0, 4, four, 0)

    def weight(n):
        return r["g_" + n][...].reshape(width, width)

    v = pltpu.VMEM
    dkv_copies = []
    quarter = 2 * width // seq
    do_base = remote.slots(seq)

    def send_do(k):
        to = lax.rem(s + k, seq)
        return remote.make(r.dosend.at[to], r.dorecv.at[s], do_base + k, {SEQ: to})

    def kv_part(a, owner):
        lanes = pl.ds(pl.multiple_of(owner * quarter, quarter), quarter)
        return r.kv.at[pl.ds(a * keys // 2, keys // 2), lanes]

    def begin_kv():
        for a in range(2):
            for w, owner in enumerate((flip[1 + a], flip[3])):

                def describe(a=a, w=w, owner=owner):
                    return kv_part(a, owner), r.dkvr.at[a, w], {SEQ: flip[1 + a]}

                dkv_copies.append(remote.start(describe))

    def step_kv():
        for c in dkv_copies:
            c().wait_recv()
        dkv_copies.clear()
        for a in range(2):
            for w, owner in enumerate((s, flip[2 - a])):
                own = kv_part(a, owner)
                own[...] = (own[...].astype(F32) + r.dkvr[a, w].astype(F32)).astype(BF)

            def describe(a=a):
                return kv_part(a, flip[2 - a]), r.dkvs.at[a], {SEQ: flip[2 - a]}

            dkv_copies.append(remote.start(describe))

    def end_kv():
        for c in dkv_copies:
            c().wait_recv()
        for a in range(2):
            own = kv_part(a, s)[...].astype(F32) + r.dkvs[a].astype(F32)
            r.dkvq[a * seq // 2 : (a + 1) * seq // 2] = own.astype(BF).reshape(seq // 2, tl, quarter)

    def middle(*held):
        for n, ref in zip(K2_HELD, held):
            r[n] = ref
            loads[n] = local.start(r["in_" + n], ref)

        loads.x2.wait()
        loads.cot.wait()
        x2v = r.x2[...]
        n3, _ = norm_parts(x2v)
        h3 = (n3 * (1.0 + pick(mods, seg, 4, width)) + pick(mods, seg, 3, width)).astype(BF)

        def feed(h3_ref, h3T_ref, dm_ref, m_ref, dh_ref):
            h3_ref[...] = h3
            h3T_ref[...] = h3.astype(F32).T.astype(BF)
            dm_ref[...] = (pick(mods, seg, 5, width) * r.cot[...].astype(F32)).astype(BF)
            m_ref[...] = jnp.zeros_like(m_ref)
            dh_ref[...] = jnp.zeros_like(dh_ref)
            loads.w_fc1.wait()
            loads.w_fc2.wait()
            g1, g2 = r.g_fc1, r.g_fc2
            k0, k1 = math.sqrt(2.0 / math.pi), 0.044715

            def one(c, carry):
                cols = pl.ds(pl.multiple_of(c * chunk, chunk), chunk)
                ca, cb = lax.div(c, 2), lax.rem(c, 2)
                w1 = g1[:, :, :, :, cols].reshape(width, chunk)
                w2 = g2[ca, cb].reshape(chunk, width)
                z = nn(h3_ref[...], w1)
                zz = z * z
                t = jnp.tanh(k0 * (z + k1 * z * zz))
                u = (0.5 * z * (1.0 + t)).astype(BF)
                slope = 0.5 * (1.0 + t) + 0.5 * z * (1.0 - t * t) * (k0 * (1.0 + 3.0 * k1 * zz))
                m_ref[...] += nn(u, w2)
                dz = (nt(dm_ref[...], w2) * slope).astype(BF)
                dh_ref[...] += nt(dz, w1)
                g1[:, :, :, :, cols] = nn(h3T_ref[...], dz).astype(BF).reshape(2, 2, 2, width // BLOCKS, chunk)
                for g0 in range(2):
                    half = chunk // 4
                    val = tn(u[:, g0 * 2 * half : (g0 + 1) * 2 * half], dm_ref[...]).astype(BF)
                    for q in range(seq):
                        lane = (q % 2) * 2 * group
                        g2[ca, cb, g0, q // 2, :, lane : lane + group] = val[:half, q * group : (q + 1) * group]
                        g2[ca, cb, g0, q // 2, :, lane + group : lane + 2 * group] = val[half:, q * group : (q + 1) * group]
                return carry

            lax.fori_loop(0, seq, one, 0)
            grads.fc2.begin()
            grads.fc1.begin()
            dy = r.cot[...].astype(F32)
            m = m_ref[...]
            x2w = r.x2[...]
            r.out_block_out[...] = (x2w + pick(mods, seg, 5, width) * m).astype(BF)
            store("block_out")
            clip_sum(5, dy * m)
            dh = dh_ref[...]
            nw, rstd = norm_parts(x2w)
            clip_sum(3, dh)
            clip_sum(4, dh * nw)
            r.dx[...] = dy + norm_back(dh * (1.0 + pick(mods, seg, 4, width)), nw, rstd)

        pl.run_scoped(feed, v((tok, width), BF), v((width, tok), BF), v((tok, width), BF), v((tok, width), F32), v((tok, width), F32))

        for c in (loads.w_cout, loads.coT, loads.cqT, loads.lsec, loads.kv, loads.ckT):
            c.wait()

        def cross_back(dcoT, dcqT, biasc):
            dc = r.dx[...].astype(BF)
            dcoT[...] = nt(weight("cout"), dc).astype(BF)
            square("cout", lambda i: r.coT[pl.ds(pl.multiple_of(i * group, group), group), :], dc)
            grads.cout.begin()
            tcol = column(codes[2:3, :keys])
            biasc[...] = jnp.where(jnp.broadcast_to(tcol[:, :1], (keys, tok)) == seg_row, 0.0, MASKED)
            grads.fc2.step()
            kv = r.kv

            def pair(p, carry):
                cols = pl.ds(pl.multiple_of(p * 128, 128), 128)
                vcols = pl.ds(pl.multiple_of(width + p * 128, 128), 128)
                ck, cv = kv[:, cols], kv[:, vcols]
                parts_k, parts_v = [], []
                for a in range(2):
                    hrows = pl.ds(pl.multiple_of(p * 128 + a * HD, HD), HD)
                    q_h, do_h = r.cqT[hrows, :], dcoT[hrows, :]
                    lse_h = r.lsec[pl.ds(2 * p + a, 1), :]
                    pr = jnp.exp(nn(ck[:, a * HD : (a + 1) * HD], q_h) + biasc[...] - lse_h)
                    dpr = nn(cv[:, a * HD : (a + 1) * HD], do_h)
                    delta = jnp.sum(pr * dpr, axis=0, keepdims=True)
                    ds = (pr * (dpr - delta)).astype(BF)
                    parts_k.append(nt(ds, q_h))
                    parts_v.append(nt(pr.astype(BF), do_h))
                    dcqT[hrows, :] = nn(r.ckT[hrows, :], ds) * SCALE
                kv[:, cols] = jnp.concatenate(parts_k, axis=1).astype(BF)
                kv[:, vcols] = jnp.concatenate(parts_v, axis=1).astype(BF)
                return carry

            lax.fori_loop(0, 2, pair, 0)
            grads.fc1.step()
            lax.fori_loop(2, H // 2, pair, 0)
            begin_kv()
            dcq = dcqT[...].T.astype(BF)
            loads.w_cq.wait()
            loads.h2T.wait()
            loads.x1.wait()
            dh2 = nt(dcq, weight("cq"))
            square("cq", lambda i: r.h2T[pl.ds(pl.multiple_of(i * group, group), group), :], dcq)
            nw, rstd = norm_parts(r.x1[...])
            r.dx[...] += norm_back(dh2, nw, rstd)

        pl.run_scoped(cross_back, v((width, tok), BF), v((width, tok), F32), v((keys, tok), F32))

        for c in (loads.w_proj, loads.aout, loads.oT):
            c.wait()
        dx1 = r.dx[...]
        da = (pick(mods, seg, 2, width) * dx1).astype(BF)
        doT = nt(weight("proj"), da).astype(BF)
        for q in range(seq):
            r.dosend[q] = doT[q * group : (q + 1) * group, :]
        for k in range(1, seq):
            send_do(k).start()
        r.dorecv[s] = r.dosend[s]
        grads.cq.begin()
        clip_sum(2, dx1 * r.aout[...])
        square("proj", lambda i: r.oT[i], da)
        grads.proj.begin()
        grads.fc2.step()
        grads.fc1.step()
        for c in (loads.qT, loads.kT, loads.kn, loads.vn, loads.lse):
            c.wait()

        def self_back(kcol, bias, dk, dv):
            kcol[...] = column(codes[1:2, :full])
            dk[...] = jnp.zeros_like(dk)
            dv[...] = jnp.zeros_like(dv)

            def block(k, carry):
                @pl.when(k > 0)
                def _():
                    send_do(k).wait_recv()

                at = lax.rem(s - k + seq, seq)
                rows = pl.ds(pl.multiple_of(at * tok, tok), tok)
                row_id = lax.broadcasted_iota(jnp.int32, (full, tok), 0)
                col_id = lax.broadcasted_iota(jnp.int32, (full, tok), 1) + at * tok
                key = jnp.broadcast_to(kcol[:, :1], (full, tok))
                bias[...] = jnp.where((key == codes[0:1, rows]) | (row_id == col_id), 0.0, MASKED)
                for h in range(hl):
                    hs = slice(h * HD, (h + 1) * HD)
                    q_h, do_h = r.qT[hs, rows], r.dorecv[at, hs, :]
                    pr = jnp.exp(nn(r.kn[h], q_h) + bias[...] - r.lse[h : h + 1, rows])
                    dpr = nn(r.vn[h], do_h)
                    delta = jnp.sum(pr * dpr, axis=0, keepdims=True)
                    ds = (pr * (dpr - delta)).astype(BF)
                    dk[h] += nt(ds, q_h)
                    dv[h] += nt(pr.astype(BF), do_h)
                    dq = nn(r.kT[hs, :], ds) * SCALE
                    r.dqs[at, :, hs] = dq.T.astype(BF)
                return carry

            lax.fori_loop(0, 2, block, 0)
            step_kv()
            lax.fori_loop(2, seq, block, 0)
            for h in range(hl):
                for b in range(seq):
                    br = slice(b * tok, (b + 1) * tok)
                    r.dqs[b, :, group + h * HD : group + (h + 1) * HD] = dk[h, br, :].astype(BF)
                    r.dqs[b, :, 2 * group + h * HD : 2 * group + (h + 1) * HD] = dv[h, br, :].astype(BF)

        pl.run_scoped(self_back, v((full, 128), F32), v((full, tok), F32), v((hl, full, HD), F32), v((hl, full, HD), F32))

    pl.run_scoped(
        middle,
        v((width, keys), BF),
        v((group, full), BF),
        v((group, full), BF),
        v((hl, full, HD), BF),
        v((hl, full, HD), BF),
    )

    dq_base = remote.slots(seq)

    def send_dq(k):
        to = lax.rem(s + k, seq)
        return remote.make(r.dqs.at[to], r.dqr.at[s], dq_base + k, {SEQ: to})

    for k in range(1, seq):
        send_dq(k).start()
    for n in ("cout", "cq", "proj"):
        grads[n].step()
    grads.fc2.step()
    grads.fc1.step()
    r.dqr[s] = r.dqs[s]

    def tail(h1, text, wqkv, wckv, dqf):
        tail_loads = [
            local.start(a, b)
            for a, b in ((r.in_h1, h1), (r.w_qkv, wqkv), (r.in_text, text), (r.w_ckv, wckv))
        ]
        loads.x.wait()
        tail_loads[0].wait()
        gq = tn(h1[...].reshape(full, width), r.dqs[...].reshape(full, 3 * group))
        r.g_qkv[...] = gq.astype(BF).reshape(2, 2, 2, width // BLOCKS, 3 * group)
        grads.qkv.begin()
        end_kv()
        kv_base = remote.slots(seq)

        def send_kv(k):
            to = lax.rem(s + k, seq)
            return remote.make(r.dkvq.at[to], r.dkvl.at[s], kv_base + k, {SEQ: to})

        for k in range(1, seq):
            send_kv(k).start()
        r.dkvl[s] = r.dkvq[s]
        tail_loads[2].wait()
        gc = tn(text[...].reshape(keys, dc_all), r.dkvq[...].reshape(keys, quarter))
        r.g_ckv[...] = gc.astype(BF).reshape(2, 2, 2, dc_all // BLOCKS, quarter)
        grads.ckv.begin()
        grads.qkv.step()
        for k in range(1, seq):
            send_dq(k).wait_recv()
        for b in range(seq):
            got = r.dqr[b]
            for t in range(3):
                dqf[:, t * width + b * group : t * width + (b + 1) * group] = got[:, t * group : (t + 1) * group]
        tail_loads[1].wait()
        dh1 = nt(dqf[...], wqkv[...])
        nx, rstd = norm_parts(r.x[...].astype(F32))
        clip_sum(0, dh1)
        clip_sum(1, dh1 * nx)
        dm_copies = []
        part = 6 * width // seq
        for k in range(1, seq):

            def describe_dm(k=k):
                to = lax.rem(s + k, seq)
                lanes = pl.ds(pl.multiple_of(to * part, part), part)
                return r.dmod.at[:, lanes], r.dmr.at[k - 1], {SEQ: to}

            dm_copies.append(remote.start(describe_dm))
        back = norm_back(dh1 * (1.0 + pick(mods, seg, 1, width)), nx, rstd)
        r.out_grad_frames[...] = (r.dx[...] + back).astype(BF)
        store("grad_frames")
        grads.fc1.step()
        grads.ckv.step()
        grads.qkv.step()
        for n in ("cout", "cq", "proj"):
            grads[n].step()
        grads.fc2.step()
        for c in dm_copies:
            c().wait_recv()
        total = r.dmod[:, pl.ds(pl.multiple_of(s * part, part), part)]
        for k in range(seq - 1):
            total = total + r.dmr[k]
        r.dmall[d] = total

        def send_dm(j):
            to = lax.rem(d + j, dp)
            return remote.make(r.dmall.at[d], r.dmall.at[d], dm_base + j, {DP: to})

        def start_dm(j, carry):
            send_dm(j).start()
            return carry

        lax.fori_loop(1, dp, start_dm, 0)
        for k in range(1, seq):
            send_kv(k).wait_recv()
        tail_loads[3].wait()
        gt = nt(r.dkvl[0], wckv[:, 0:quarter])
        for b in range(1, seq):
            gt = gt + nt(r.dkvl[b], wckv[:, b * quarter : (b + 1) * quarter])
        r.out_grad_text[...] = gt.astype(BF)
        store("grad_text")
        grads.qkv.step()
        q_base = remote.slots(3)

        def send_q(t):
            b = 4 * t + s
            to = lax.div(b, 3)
            slot = b - 3 * to
            return to, slot, pltpu.make_async_remote_copy(
                src_ref=r.fq.at[t],
                dst_ref=r.rq.at[slot],
                send_sem=r.ssem.at[q_base + t],
                recv_sem=r.rsem.at[q_base + slot],
                device_id={SEQ: to},
                device_id_type=MESH,
            )

        for t in range(3):
            to, slot, copy = send_q(t)

            @pl.when(to != s)
            def _():
                copy.start()

            @pl.when(to == s)
            def _():
                r.rq[slot] = r.fq[t]

        for n in ("cout", "cq", "proj", "ckv", "fc2", "cout", "cq", "proj", "ckv", "fc1", "cout", "cq", "proj"):
            grads[n].step()

        def wait_dm(j, carry):
            send_dm(j).wait_recv()
            send_emb(j).wait_recv()
            return carry

        own_emb.wait()
        lax.fori_loop(1, dp, wait_dm, 0)
        emb = r.emball[...].reshape(dp * 8, 128)
        allm = r.dmall[...].reshape(dp * 8, part)
        high = allm.astype(BF)
        rest = (allm - high.astype(F32)).astype(BF)
        ga = tn(emb, high) + tn(emb, rest)
        r.out_ada[...] = ga[: width // dp]
        store("ada")
        for j in range(3):
            src = lax.rem(3 * s + j, seq)

            @pl.when(src != s)
            def _():
                remote.make(r.fq.at[j], r.rq.at[j], q_base + j, {SEQ: src}).wait_recv()

            r.out_qkv[:, j * group : (j + 1) * group] = r.rq[j]
        store("qkv")

        for t in range(3):
            to, slot, copy = send_q(t)

            @pl.when(to != s)
            def _():
                copy.wait_send()

        for k in range(1, seq):
            send_do(k).wait_send()
            send_dq(k).wait_send()
            send_kv(k).wait_send()

        def wait_sent(j, carry):
            send_dm(j).wait_send()
            send_emb(j).wait_send()
            return carry

        lax.fori_loop(1, dp, wait_sent, 0)
        for sent in remote.open:
            sent()
        for n, slot in stores:
            stored(n, slot).wait()

    pl.run_scoped(
        tail,
        v((seq, tok, width), BF),
        v((seq, tl, dc_all), BF),
        v((width, 3 * width), BF),
        v((dc_all, 2 * width), BF),
        v((tok, 3 * width), BF),
    )


def run_backward(dims, dp, fwd, args):
    seq, tok, full, width, keys, group, dc = dims
    hl, tl, block = H // seq, keys // seq, width // BLOCKS
    ff = 4 * width
    v = pltpu.VMEM
    lead = (2, 2, 2)
    gshape = dict(
        fc1=(block, ff),
        fc2=(2, ff // BLOCKS // 2, width),
        cout=(2, block // 2, width),
        cq=(2, block // 2, width),
        proj=(2, block // 2, width),
        ckv=(dc // BLOCKS, 2 * width // seq),
        qkv=(block, 3 * group),
    )
    names, ins, specs = [], [], []

    def add_in(spec=ANY, **kw):
        for name, value in kw.items():
            names.append(name)
            ins.append(value)
            specs.append(spec)

    add_in(codes=fwd.codes, spec=INV)
    add_in(mods=fwd.mods, spec=INV)
    add_in(in_x=args.x)
    add_in(in_cot=args.cot)
    add_in(in_emb=args.emb)
    for n in K2_LOADS + K2_HELD + ("h1", "text"):
        add_in(**{"in_" + n: fwd[n]})
    for n in K2_WEIGHTS:
        add_in(**{"w_" + n: args[n].reshape(lead + gshape[n])})
    add_in(w_ckv=args.ckv)
    add_in(w_qkv=args.qkv)

    outs = dict(
        block_out=((tok, width), BF),
        grad_frames=((tok, width), BF),
        grad_text=((tl, dc), BF),
        ada=((width // dp, 6 * width // seq), F32),
        qkv=((block, 3 * group), F32),
        proj=((block, group), F32),
        cq=((block, group), F32),
        ckv=((dc // BLOCKS, 2 * width // seq), F32),
        cout=((block, group), F32),
        fc1=((block, ff // seq), F32),
        fc2=((group, ff // BLOCKS), F32),
    )
    for n in K2_OUTS:
        names.append("hbm_" + n)
    scratch = []

    def add(**kw):
        for name, (shape, dtype) in kw.items():
            names.append(name)
            scratch.append(v(shape, dtype))

    for n in K2_OUTS:
        add(**{"out_" + n: outs[n]})
    add(cot=((tok, width), BF))
    add(x=((tok, width), BF))
    for n in K2_LOADS:
        add(**{n: (fwd[n].shape, fwd[n].dtype)})
    for n, (kind, order) in GRADS.items():
        add(**{"g_" + n: (lead + gshape[n], BF)})
        for i, b in enumerate(grad_buffers(gshape[n], kind, order, seq)):
            names.append("r_%s%d" % (n, i))
            scratch.append(b)
    quarter = 2 * width // seq
    add(dx=((tok, width), F32))
    add(dkvr=((2, 2, keys // 2, quarter), BF))
    add(dkvs=((2, keys // 2, quarter), BF))
    add(dkvq=((seq, tl, quarter), BF))
    add(dkvl=((seq, tl, quarter), BF))
    add(dosend=((seq, group, tok), BF))
    add(dorecv=((seq, group, tok), BF))
    add(dqs=((seq, tok, 3 * group), BF))
    add(dqr=((seq, tok, 3 * group), BF))
    add(dmod=((8, 6 * width), F32))
    add(dmr=((seq - 1, 8, 6 * width // seq), F32))
    add(dmall=((dp, 8, 6 * width // seq), F32))
    add(emball=((dp, 8, 128), BF))
    add(fq=((3, block, group), F32))
    add(rq=((3, block, group), F32))
    count = 2 * dp + 96
    for n, k in dict(lsem=64, ssem=count, rsem=count).items():
        names.append(n)
        scratch.append(pltpu.SemaphoreType.DMA((k,)))
    got = pl.pallas_call(
        functools.partial(backward_kernel, dims, tuple(names), dp),
        out_shape=[jax.ShapeDtypeStruct(*outs[n]) for n in K2_OUTS],
        in_specs=specs,
        out_specs=[ANY] * len(K2_OUTS),
        scratch_shapes=scratch,
        compiler_params=pltpu.CompilerParams(
            collective_id=1, has_side_effects=True, vmem_limit_bytes=67043328
        ),
        name="backward_part",
    )(*ins)
    return Bag(zip(K2_OUTS, got))


def hand_over(*refs):
    count = len(K2_OUTS)
    ins, outs, held, sems = refs[:count], refs[count : 2 * count], refs[2 * count : -1], refs[-1]
    first = [pltpu.make_async_copy(a, b, sems.at[0, i]) for i, (a, b) in enumerate(zip(ins, held))]
    second = [pltpu.make_async_copy(a, b, sems.at[1, i]) for i, (a, b) in enumerate(zip(held, outs))]
    for c in first:
        c.start()
    for c, n in zip(first, second):
        c.wait()
        n.start()
    for c in second:
        c.wait()


def run_hand_over(g):
    values = [g[n] for n in K2_OUTS]
    got = pl.pallas_call(
        hand_over,
        out_shape=[jax.ShapeDtypeStruct(a.shape, a.dtype) for a in values],
        in_specs=[ANY] * len(values),
        out_specs=[ANY] * len(values),
        scratch_shapes=[pltpu.VMEM(a.shape, a.dtype) for a in values] + [pltpu.SemaphoreType.DMA((2, len(values)))],
        name="hand_over",
    )(*values)
    return Bag(zip(K2_OUTS, got))


def per_device(
    frames, seg_ids, padding, step_ids, text_states, text_len, w_ada, w_qkv, w_proj, w_cq, w_ckv, w_cout, w_fc1, w_fc2,
    cotangent,
):
    rows, tok, width = frames.shape
    seq, dp = lax.axis_size(SEQ), lax.axis_size(DP)
    segs = step_ids.shape[1]
    full = seg_ids.shape[1]
    tl, dc = text_states.shape[2], text_states.shape[3]
    keys = segs * tl * seq
    group = (H // seq) * HD
    dims = (seq, tok, full, width, keys, group, dc)
    emb = embed_steps(jnp.pad(step_ids[0], (0, 8 - segs)), width).astype(BF)
    span = width // dp
    emb_parts = jnp.pad(jnp.swapaxes(emb.reshape(8, dp, span), 0, 1), ((0, 0), (0, 0), (0, 128 - span)))
    x = frames[0]
    text = text_states.reshape(segs * tl, dc)
    fwd = run_forward(dims, (x, text, seg_ids, padding, text_len, emb, w_ada, w_qkv, w_ckv, w_proj, w_cq, w_cout))
    args = Bag(
        x=x, cot=cotangent[0], emb=emb_parts, ckv=w_ckv, qkv=w_qkv,
        fc1=w_fc1, fc2=w_fc2, cout=w_cout, cq=w_cq, proj=w_proj,
    )
    g = run_hand_over(run_backward(dims, dp, fwd, args))
    stride = dp // BLOCKS
    if stride > 1:
        groups = [[b * stride + j for j in range(stride)] for b in range(BLOCKS)]
        for n in GRADS:
            g[n] = lax.psum_scatter(g[n], DP, scatter_dimension=1 if n == "fc2" else 0, axis_index_groups=groups, tiled=True)
    return (
        g.block_out.reshape(frames.shape),
        g.grad_frames.reshape(frames.shape),
        g.grad_text.reshape(text_states.shape),
        g.ada, g.qkv, g.proj, g.cq, g.ckv, g.cout, g.fc1, g.fc2.T,
    )


def solution(mesh):
    own, row, rep = P(DP, SEQ, None), P(DP, None), P()
    text, grad = P(DP, None, SEQ, None), P(DP, SEQ)
    return jax.shard_map(
        per_device,
        mesh=mesh,
        in_specs=(own, row, row, row, text, row) + (rep,) * 8 + (own,),
        out_specs=(own, own, text) + (grad,) * 8,
        check_vma=False,
    )
```

```python
import functools
import math

import jax
import jax.numpy as jnp
from jax import lax
from jax.experimental import pallas as pl
from jax.experimental.pallas import tpu as pltpu
from jax.sharding import PartitionSpec as P

H = 12
HD = 64
BLOCKS = 8
SEQ = "seq"
DP = "dp"
COLS, PACK = 1, 2
CUT, XY1, XY2, L0, L1, L2 = 3, 4, 5, 6, 7, 8
BF = jnp.bfloat16
F32 = jnp.float32
MESH = pl.DeviceIdType.MESH
MASKED = -1e30
EPS = 1e-06
SCALE = HD ** (-0.5)
ANY = pl.BlockSpec(memory_space=pl.ANY)
INV = pl.BlockSpec(memory_space=pltpu.VMEM)


def nn(a, b):
    return lax.dot_general(a, b, (((1,), (0,)), ((), ())), preferred_element_type=F32)


def nt(a, b):
    return lax.dot_general(a, b, (((1,), (1,)), ((), ())), preferred_element_type=F32)


def tn(a, b):
    return lax.dot_general(a, b, (((0,), (0,)), ((), ())), preferred_element_type=F32)


def embed_steps(step_values, width_all):
    half_width = width_all // 2
    frequency = jnp.exp(
        -math.log(10000.0) * jnp.arange(half_width).astype(F32) / half_width
    )
    angles = step_values.astype(F32)[..., None] * frequency
    return jax.nn.silu(jnp.concatenate([jnp.cos(angles), jnp.sin(angles)], axis=-1))


def norm_parts(v):
    centered = v - jnp.mean(v, axis=-1, keepdims=True)
    rstd = lax.rsqrt(jnp.mean(centered * centered, axis=-1, keepdims=True) + EPS)
    return centered * rstd, rstd


def norm_back(g, n, rstd):
    return (g - jnp.mean(g, axis=-1, keepdims=True) - n * jnp.mean(g * n, axis=-1, keepdims=True)) * rstd


def pick(mods, seg, part, width):
    low = part * width
    a = mods[0:1, low : low + width]
    b = mods[1:2, low : low + width]
    c = mods[2:3, low : low + width]
    return jnp.where(seg == 0.0, a, jnp.where(seg == 1.0, b, c))


def column(row):
    return jnp.broadcast_to(row, (128, row.shape[1])).T


class Bag(dict):
    __getattr__ = dict.__getitem__


class Remote:
    def __init__(self, send, recv):
        self.send, self.recv, self.used, self.open = send, recv, 0, []

    def slots(self, count):
        first = self.used
        self.used += count
        return first

    def make(self, src, dst, slot, where):
        return pltpu.make_async_remote_copy(
            src_ref=src,
            dst_ref=dst,
            send_sem=self.send.at[slot],
            recv_sem=self.recv.at[slot],
            device_id=where,
            device_id_type=MESH,
        )

    def start(self, describe, when=None):
        slot = self.slots(1)

        def again():
            src, dst, where = describe()
            return self.make(src, dst, slot, where)

        def launch():
            again().start()

        def sent():
            again().wait_send()

        if when is None:
            launch()
            self.open.append(sent)
        else:
            pl.when(when())(launch)
            self.open.append(lambda: pl.when(when())(sent))
        return again


class Local:
    def __init__(self, sems):
        self.sems, self.used = sems, 0

    def start(self, src, dst):
        copy = pltpu.make_async_copy(src, dst, self.sems.at[self.used])
        self.used += 1
        copy.start()
        return copy


def greet(seq, at_seq, dp_peers):
    barrier = pltpu.get_barrier_semaphore()
    for k in range(1, seq):
        pl.semaphore_signal(
            barrier, inc=1, device_id={SEQ: lax.rem(at_seq + k, seq)}, device_id_type=MESH
        )
    for peer in dp_peers:
        pl.semaphore_signal(barrier, inc=1, device_id={DP: peer}, device_id_type=MESH)
    pl.semaphore_wait(barrier, seq - 1 + len(dp_peers))


K1_OUTS = tuple(dict(h1=0, qT=0, kT=0, kn=0, vn=0, lse=0, oT=0, aout=0, x1=0, h2T=0, cqT=0, kv=0, ckT=0, lsec=0, coT=0, x2=0, text=0, mods=0, codes=0))


def forward_kernel(dims, segs, *refs):
    seq, tok, full, width, keys, group, dc = dims
    hl = H // seq
    ins, refs = refs[:12], refs[12:]
    x_hbm, text_hbm, seg_in, pad_in, len_in, emb, wada_hbm, wqkv_hbm, wckv_hbm, wp_hbm, wcq_hbm, wco_hbm = ins
    outs, refs = Bag(zip(K1_OUTS, refs[: len(K1_OUTS)])), refs[len(K1_OUTS) :]
    (
        x_all, text_all, wg, wckv, wp, wcq, wco, qT, kT, vT, kn, vn, lse, osend, orecv, aout, x1, h2T, cqT, kv, kvT,
        lsec, coT, x2, bias, biasc, kcol, tcol, xin, wada, mods, codes, h1_all, lsem, ssem, rsem,
    ) = refs
    local, remote = Local(lsem), Remote(ssem, rsem)
    s = lax.axis_index(SEQ)
    load_x = local.start(x_hbm, xin)
    load_own = local.start(x_hbm, x_all.at[s])
    load_ada = local.start(wada_hbm, wada)
    first = lax.div(s * group, 128) * 128
    odd = lax.rem(s * group, 128) > 0
    load_wg = [
        local.start(
            wqkv_hbm.at[:, pl.ds(pl.multiple_of(t * width + first, 128), 256)], wg.at[:, pl.ds(t * 256, 256)]
        )
        for t in range(3)
    ]
    load_text = local.start(text_hbm, text_all.at[s])
    load_w = [local.start(a, b) for a, b in ((wckv_hbm, wckv), (wp_hbm, wp), (wcq_hbm, wcq), (wco_hbm, wco))]
    greet(seq, s, ())

    base_x = remote.slots(5)
    base_t = remote.slots(5)
    base_o = remote.slots(4)
    sx, sy = lax.rem(s, 2), lax.div(s, 2)

    def other(k):
        kx, ky = (k % 2, k // 2) if isinstance(k, int) else (lax.rem(k, 2), lax.div(k, 2))
        return 2 * (sy + ky - 2 * sy * ky) + sx + kx - 2 * sx * kx

    def direct(src, held, base, m):
        return remote.make(src, held.at[s], base + m, {SEQ: other(m)})

    def relay(held, base, m):
        half = held.shape[1] // 2
        part = held.at[other(3 - m), pl.ds((m - 1) * half, half)]
        return remote.make(part, part, base + 2 + m, {SEQ: other(m)})

    for m in (1, 2):
        direct(x_hbm, x_all, base_x, m).start()

    tl = keys // seq // segs
    place = lax.broadcasted_iota(jnp.int32, (1, full), 1).astype(F32)
    block = jnp.floor((place + 0.5) / tl)
    owner = jnp.floor((block + 0.5) / segs)
    clip = block - owner * segs
    length = jnp.zeros((1, full), F32)
    for c in range(segs):
        length = jnp.where(clip == c, jnp.broadcast_to(len_in[0:1, c : c + 1].astype(F32), (1, full)), length)
    codes[...] = jnp.zeros_like(codes)
    codes[0:1, :] = seg_in[...].astype(F32)
    codes[1:2, :] = jnp.where(pad_in[...] == 1, seg_in[...].astype(F32), -1.0)
    codes[2:3, :] = jnp.where(owner * tl + place - block * tl < length, clip, -1.0)
    save_codes = local.start(codes, outs.codes)
    kcol[...] = column(codes[1:2, :full])
    tcol[...] = column(codes[2:3, :keys])
    load_x.wait()
    load_own.wait()
    load_ada.wait()
    mods[...] = nn(emb[...], wada[...])
    save_mods = local.start(mods, outs.mods)
    for c in load_wg:
        c.wait()

    def project(k, carry):
        @pl.when(k == 1)
        def _():
            for m in (1, 2):
                direct(x_hbm, x_all, base_x, m).wait_recv()
            for m in (1, 2):
                relay(x_all, base_x, m).start()
            for m in (1, 2):
                direct(text_hbm, text_all, base_t, m).start()

        @pl.when(k == 3)
        def _():
            for m in (1, 2):
                relay(x_all, base_x, m).wait_recv()

        at = other(k)
        rows = pl.ds(pl.multiple_of(at * tok, tok), tok)
        seg = column(codes[0:1, rows])[:, :1]
        seg = jnp.broadcast_to(seg, (tok, width))
        n, _ = norm_parts(x_all[at].astype(F32))
        h1 = (n * (1.0 + pick(mods, seg, 1, width)) + pick(mods, seg, 0, width)).astype(BF)
        h1_all[at] = h1
        wide = nn(h1, wg[...])
        out = jnp.concatenate(
            [
                jnp.where(odd, wide[:, t * 256 + 64 : t * 256 + 64 + group], wide[:, t * 256 : t * 256 + group])
                for t in range(3)
            ],
            axis=1,
        )
        for h in range(hl):
            kn[h, rows, :] = out[:, group + h * HD : group + (h + 1) * HD].astype(BF)
            vn[h, rows, :] = out[:, 2 * group + h * HD : 2 * group + (h + 1) * HD].astype(BF)
        low = out.astype(BF).astype(F32)
        outT = low.T
        qT[:, rows] = (outT[:group] * SCALE).astype(BF)
        kT[:, rows] = outT[group : 2 * group].astype(BF)
        vT[:, rows] = outT[2 * group :].astype(BF)
        return carry

    lax.fori_loop(0, seq, project, 0)
    saves = [save_mods, save_codes] + [
        local.start(a, b)
        for a, b in ((h1_all, outs.h1), (qT, outs.qT), (kT, outs.kT), (kn, outs.kn), (vn, outs.vn))
    ]

    def send_o(k):
        at = other(k)
        return remote.make(osend.at[at], orecv.at[s], base_o + k, {SEQ: at})

    def attend(k, carry):
        @pl.when(k == 3)
        def _():
            for m in (1, 2):
                direct(text_hbm, text_all, base_t, m).wait_recv()
            for m in (1, 2):
                relay(text_all, base_t, m).start()

        at = other(3 - k)
        rows = pl.ds(pl.multiple_of(at * tok, tok), tok)
        seg = codes[0:1, rows]
        row_id = lax.broadcasted_iota(jnp.int32, (full, tok), 0)
        col_id = lax.broadcasted_iota(jnp.int32, (full, tok), 1) + at * tok
        key = jnp.broadcast_to(kcol[:, :1], (full, tok))
        bias[...] = jnp.where((key == seg) | (row_id == col_id), 0.0, MASKED)

        def head(h, c2):
            hrows = pl.ds(pl.multiple_of(h * HD, HD), HD)
            st = nn(kn[h], qT[hrows, rows]) + bias[...]
            peak = jnp.max(st, axis=0, keepdims=True)
            ex = jnp.exp(st - peak)
            total = jnp.sum(ex, axis=0, keepdims=True)
            ov = nn(vT[hrows, :], ex.astype(BF)) * (1.0 / total)
            osend[at, hrows, :] = ov.astype(BF)
            lse[pl.ds(h, 1), rows] = peak + jnp.log(total)
            return c2

        lax.fori_loop(0, hl, head, 0)

        @pl.when(k < seq - 1)
        def _():
            send_o(3 - k).start()

        return carry

    lax.fori_loop(0, seq, attend, 0)
    orecv[s] = osend[s]

    load_text.wait()
    saves.append(local.start(lse, outs.lse))
    for c in load_w:
        c.wait()
    tl = keys // seq

    def project_text(k, carry):
        @pl.when(k == 3)
        def _():
            for m in (1, 2):
                relay(text_all, base_t, m).wait_recv()

        b = other(k)
        trows = pl.ds(pl.multiple_of(b * tl, tl), tl)
        kv[trows, :] = nn(text_all[b], wckv[...]).astype(BF)
        return carry

    lax.fori_loop(0, seq, project_text, 0)
    saves.append(local.start(text_all, outs.text))

    def turn_text(c, carry):
        cols = pl.ds(pl.multiple_of(c * 256, 256), 256)
        kvT[cols, :] = kv[:, cols].astype(F32).T.astype(BF)
        return carry

    lax.fori_loop(0, 2 * width // 256, turn_text, 0)
    rows = pl.ds(pl.multiple_of(s * tok, tok), tok)
    seg_row = codes[0:1, rows]
    biasc[...] = jnp.where(jnp.broadcast_to(tcol[:, :1], (keys, tok)) == seg_row, 0.0, MASKED)
    saves.append(local.start(kv, outs.kv))
    saves.append(local.start(kvT.at[pl.ds(0, width)], outs.ckT))

    for k in range(1, seq):
        send_o(k).wait_recv()
    saves.append(local.start(orecv, outs.oT))
    seg = jnp.broadcast_to(column(seg_row)[:, :1], (tok, width))
    branch = tn(orecv[...].reshape(width, tok), wp[...])
    aout[...] = branch
    mid = xin[...].astype(F32) + pick(mods, seg, 2, width) * branch
    x1[...] = mid
    n, _ = norm_parts(mid)
    h2 = n.astype(BF)
    h2T[...] = n.astype(BF).astype(F32).T.astype(BF)
    cq = nn(h2, wcq[...]).astype(BF).astype(F32)
    cqT[...] = (cq.T * SCALE).astype(BF)
    saves += [local.start(a, b) for a, b in ((aout, outs.aout), (x1, outs.x1), (h2T, outs.h2T), (cqT, outs.cqT))]

    def cross(p, carry):
        cols = pl.ds(pl.multiple_of(p * 128, 128), 128)
        pair = kv[:, cols]
        for a in range(2):
            hrows = pl.ds(pl.multiple_of(p * 128 + a * HD, HD), HD)
            vrows = pl.ds(pl.multiple_of(width + p * 128 + a * HD, HD), HD)
            st = nn(pair[:, a * HD : (a + 1) * HD], cqT[hrows, :]) + biasc[...]
            peak = jnp.max(st, axis=0, keepdims=True)
            ex = jnp.exp(st - peak)
            total = jnp.sum(ex, axis=0, keepdims=True)
            ov = nn(kvT[vrows, :], ex.astype(BF)) * (1.0 / total)
            coT[hrows, :] = ov.astype(BF)
            lsec[pl.ds(2 * p + a, 1), :] = peak + jnp.log(total)
        return carry

    lax.fori_loop(0, H // 2, cross, 0)
    x2[...] = x1[...] + tn(coT[...], wco[...])
    saves += [local.start(a, b) for a, b in ((lsec, outs.lsec), (coT, outs.coT), (x2, outs.x2))]
    for m in (1, 2):
        direct(x_hbm, x_all, base_x, m).wait_send()
        relay(x_all, base_x, m).wait_send()
        direct(text_hbm, text_all, base_t, m).wait_send()
        relay(text_all, base_t, m).wait_send()
    for k in range(1, seq):
        send_o(k).wait_send()
    for c in saves:
        c.wait()


def run_forward(dims, args):
    seq, tok, full, width, keys, group, dc = dims
    hl = H // seq
    shapes = dict(
        h1=((seq, tok, width), BF),
        qT=((group, full), BF),
        kT=((group, full), BF),
        kn=((hl, full, HD), BF),
        vn=((hl, full, HD), BF),
        lse=((8, full), F32),
        oT=((seq, group, tok), BF),
        aout=((tok, width), F32),
        x1=((tok, width), F32),
        h2T=((width, tok), BF),
        cqT=((width, tok), BF),
        kv=((keys, 2 * width), BF),
        ckT=((width, keys), BF),
        lsec=((16, tok), F32),
        coT=((width, tok), BF),
        x2=((tok, width), F32),
        text=((seq, keys // seq, dc), BF),
        mods=((8, 6 * width), F32),
        codes=((8, full), F32),
    )
    v = pltpu.VMEM
    scratch = [
        v((seq, tok, width), BF), v((seq, keys // seq, dc), BF), v((width, 3 * 256), BF), v((dc, 2 * width), BF),
        v((width, width), BF), v((width, width), BF), v((width, width), BF),
        v((group, full), BF), v((group, full), BF), v((group, full), BF), v((hl, full, HD), BF), v((hl, full, HD), BF),
        v((8, full), F32), v((seq, group, tok), BF), v((seq, group, tok), BF),
        v((tok, width), F32), v((tok, width), F32), v((width, tok), BF), v((width, tok), BF),
        v((keys, 2 * width), BF), v((2 * width, keys), BF), v((16, tok), F32), v((width, tok), BF), v((tok, width), F32),
        v((full, tok), F32), v((keys, tok), F32), v((full, 128), F32), v((keys, 128), F32), v((tok, width), BF),
        v((width, 6 * width), BF), v((8, 6 * width), F32), v((8, full), F32), v((seq, tok, width), BF),
        pltpu.SemaphoreType.DMA((32,)), pltpu.SemaphoreType.DMA((16,)), pltpu.SemaphoreType.DMA((16,)),
    ]
    outs = pl.pallas_call(
        functools.partial(forward_kernel, dims, args[4].shape[1]),
        out_shape=[jax.ShapeDtypeStruct(*shapes[n]) for n in K1_OUTS],
        in_specs=[ANY, ANY, INV, INV, INV, INV, ANY, ANY, ANY, ANY, ANY, ANY],
        out_specs=[ANY] * len(K1_OUTS),
        scratch_shapes=scratch,
        compiler_params=pltpu.CompilerParams(
            collective_id=0, has_side_effects=True, vmem_limit_bytes=60 * 1024 * 1024
        ),
        name="forward_part",
    )(*args)
    return Bag(zip(K1_OUTS, outs))


class Grad:
    def __init__(self, ref, kind, order, bufs, where, remote, finish):
        self.ref, self.kind, self.order, self.bufs = ref, kind, order, bufs
        self.s, self.seq, self.d, self.stride, self.bits, self.flip, self.dp = where
        self.remote, self.finish = remote, finish
        self.fixed, self.cut, self.stage, self.copies = {}, False, 0, []

    def view(self, fixed, quarter, lead=None):
        index, lead = [], list(lead or [])
        for bit in (2, 1, 0):
            if bit in fixed:
                index.append(fixed[bit])
            elif lead:
                index.append(lead.pop(0))
            else:
                index.append(slice(None))
        if quarter is not None:
            size = self.ref.shape[-1] // (self.seq if self.kind == COLS else 2)
            if self.kind == COLS:
                lanes = pl.ds(pl.multiple_of(quarter * size, 128), size)
                index += [slice(None), lanes]
            else:
                lanes = pl.ds(pl.multiple_of(lax.rem(quarter, 2) * size, 128), size)
                index += [lax.div(quarter, 2), slice(None), lanes]
        return self.ref.at[tuple(index)]

    def line(self):
        return 2 * self.bits[2] + self.bits[1]

    def chunk(self, fixed, quarter, number):
        number = lax.rem(number, 4)
        return self.view({**fixed, 2: lax.div(number, 2), 1: lax.rem(number, 2)}, quarter)

    def end_halving(self, what, buf):
        for a in range(2):
            for w in range(2 if what == XY1 else 1):
                owner = self.flip[2 - a] if w else self.s

                def add(b, carry):
                    own = self.view({**self.fixed, 2: a}, owner, [b])
                    more = buf[a, w, b] if what == XY1 else buf[a, b]
                    own[...] = (own[...].astype(F32) + more.astype(F32)).astype(BF)
                    return carry

                lax.fori_loop(0, 2, add, 0)

    def end_line(self, t, buf):
        quarter, line = self.s if self.cut else None, self.line()
        above, below = self.copies

        def take(copy, side, number):
            copy().wait_recv()
            own = self.chunk(self.fixed, quarter, number)
            own[...] = (own[...].astype(F32) + buf[side].astype(F32)).astype(BF)

        @pl.when((line >= 1) & (line <= t + 1))
        def _():
            take(above, 0, line + 2 - t)

        @pl.when((line <= 2) & (line >= 2 - t))
        def _():
            take(below, 1, line + 2 + t)

    def begin(self):
        what, buf = self.order[self.stage], self.bufs[self.stage]
        self.copies = []
        if what == XY1:
            for a in range(2):
                to = self.flip[1 + a]
                for w, owner in enumerate((to, self.flip[3])):

                    def describe(a=a, w=w, owner=owner, to=to, fixed=dict(self.fixed)):
                        return self.view({**fixed, 2: a}, owner), buf.at[a, w], {SEQ: to}

                    self.copies.append(self.remote.start(describe))
        elif what == XY2:
            for a in range(2):

                def describe(a=a, to=self.flip[2 - a], fixed=dict(self.fixed)):
                    return self.view({**fixed, 2: a}, to), buf.at[a], {SEQ: to}

                self.copies.append(self.remote.start(describe))
        elif what >= L0:
            t = what - L0

            def upward(fixed=dict(self.fixed), quarter=self.s if self.cut else None):
                peer = lax.rem(self.d + 2 * self.stride, self.dp)
                return self.chunk(fixed, quarter, self.line() + 3 - t), buf.at[0], {DP: peer}

            def downward(fixed=dict(self.fixed), quarter=self.s if self.cut else None):
                peer = lax.rem(self.d - 2 * self.stride + self.dp, self.dp)
                return self.chunk(fixed, quarter, self.line() + 1 + t), buf.at[1], {DP: peer}

            self.copies.append(self.remote.start(upward, lambda: self.line() <= t))
            self.copies.append(self.remote.start(downward, lambda: self.line() >= 3 - t))
        elif what == CUT:
            for k in range(1, self.seq):

                def describe(k=k, fixed=dict(self.fixed)):
                    to = lax.rem(self.s + k, self.seq)
                    return self.view(fixed, to), buf.at[k - 1], {SEQ: to}

                self.copies.append(self.remote.start(describe))
        else:

            def describe(fixed=dict(self.fixed), quarter=self.s if self.cut else None):
                mine = self.bits[what]
                peer = self.d + (1 - 2 * mine) * (self.stride << what)
                return self.view({**fixed, what: 1 - mine}, quarter), buf, {DP: peer}

            self.copies.append(self.remote.start(describe))

    def end(self):
        what, buf = self.order[self.stage], self.bufs[self.stage]
        if what >= L0:
            self.end_line(what - L0, buf)
            self.stage += 1
            if what == L2:
                self.fixed[1], self.fixed[2] = self.bits[1], self.bits[2]
            return
        for c in self.copies:
            c().wait_recv()
        if what in (XY1, XY2):
            self.end_halving(what, buf)
            self.stage += 1
            self.cut = what == XY2
            return
        if what == CUT:
            self.cut = True
        else:
            self.fixed[what] = self.bits[what]
        free = 3 - len(self.fixed)
        quarter = self.s if self.cut else None
        last = self.stage == len(self.order) - 1
        self.stage += 1

        def add(i, carry):
            lead = [lax.rem(lax.div(i, 2 ** (free - 1 - j)), 2) for j in range(free)]
            own = self.view(self.fixed, quarter, lead)
            total = own[...].astype(F32)
            if what == CUT:
                for k in range(self.seq - 1):
                    total = total + buf[tuple([k] + lead)].astype(F32)
            elif lead:
                total = total + buf[tuple(lead)].astype(F32)
            else:
                total = total + buf[...].astype(F32)
            if last:
                self.finish(total)
            else:
                own[...] = total.astype(BF)
            return carry

        if free == 0:
            add(0, 0)
        else:
            lax.fori_loop(0, 2**free, add, 0)

    def step(self):
        self.end()
        if self.stage < len(self.order):
            self.begin()


def grad_buffers(shape, kind, order, seq):
    lead, payload, out, cut, free = 3, list(shape), [], False, 3
    for what in order:
        if what in (CUT, XY1, XY2):
            cut = True
        elif what in (0, 1, 2):
            free -= 1
        elif what == L2:
            free = 0
        p = list(payload)
        if cut:
            if kind == COLS:
                p[-1] //= seq
            else:
                p = [p[1], p[2] // 2]
        head = {CUT: [seq - 1], XY1: [2, 2, 2], XY2: [2, 2], L0: [2], L1: [2], L2: [2]}.get(what, [])
        if what in (CUT, 0, 1, 2):
            head = head + [2] * free
        out.append(pltpu.VMEM(tuple(head + p), BF))
    return out


GRADS = dict(
    fc2=(PACK, (0, XY1, XY2, 1, 2)),
    fc1=(COLS, (0, L0, L1, L2, CUT)),
    cout=(PACK, (0, XY1, XY2, 1, 2)),
    cq=(PACK, (0, XY1, XY2, 1, 2)),
    proj=(PACK, (0, XY1, XY2, 1, 2)),
    ckv=(None, (0, 1, 2)),
    qkv=(None, (0, 1, 2)),
)
K2_OUTS = tuple(dict(block_out=0, grad_frames=0, grad_text=0, ada=0, qkv=0, proj=0, cq=0, ckv=0, cout=0, fc1=0, fc2=0))
K2_LOADS = tuple(dict(x2=0, x1=0, aout=0, oT=0, h2T=0, cqT=0, coT=0, lsec=0, lse=0, kv=0))
K2_HELD = tuple(dict(ckT=0, qT=0, kT=0, kn=0, vn=0))
K2_WEIGHTS = tuple(dict(fc1=0, fc2=0, cout=0, cq=0, proj=0))


def backward_kernel(dims, names, dp, *refs):
    seq, tok, full, width, keys, group, dc_all = dims
    hl, chunk, tl, stride = H // seq, width, keys // seq, dp // BLOCKS
    r = Bag(zip(names, refs))
    local, remote = Local(r.lsem), Remote(r.ssem, r.rsem)
    s, d = lax.axis_index(SEQ), lax.axis_index(DP)
    bits = [lax.rem(lax.div(d, stride << b), 2) for b in range(3)]
    sx, sy = lax.rem(s, 2), lax.div(s, 2)
    flip = [s, s + 1 - 2 * sx, s + 2 - 4 * sy, 3 - s]
    where = (s, seq, d, stride, bits, flip, dp)
    codes, mods = r.codes, r.mods

    loads = Bag()
    loads["x2"] = local.start(r.in_x2, r.x2)
    loads["cot"] = local.start(r.in_cot, r.cot)
    load_base = local.used
    local.used += 2 * seq

    def load_chunk(n, c):
        if n:
            ca, cb = (c // 2, c % 2) if isinstance(c, int) else (lax.div(c, 2), lax.rem(c, 2))
            src, dst = r.w_fc2.at[ca, cb], r.g_fc2.at[ca, cb]
        else:
            cols = pl.ds(c * chunk if isinstance(c, int) else pl.multiple_of(c * chunk, chunk), chunk)
            src, dst = r.w_fc1.at[:, :, :, :, cols], r.g_fc1.at[:, :, :, :, cols]
        return pltpu.make_async_copy(src, dst, r.lsem.at[load_base + 2 * c + n])

    for c in range(seq):
        for n in range(2):
            load_chunk(n, c).start()
    for n in K2_WEIGHTS[2:]:
        loads["w_" + n] = local.start(r["w_" + n], r["g_" + n])
    for n in K2_LOADS[1:]:
        loads[n] = local.start(r["in_" + n], r[n])
    loads.x = local.start(r.in_x, r.x)

    stores = []

    def stored(n, slot):
        return pltpu.make_async_copy(r["out_" + n], r["hbm_" + n], r.lsem.at[slot])

    def store(n):
        stores.append((n, local.used))
        stored(n, local.used).start()
        local.used += 1

    barrier = pltpu.get_barrier_semaphore()
    for k in range(1, seq):
        pl.semaphore_signal(barrier, inc=1, device_id={SEQ: lax.rem(s + k, seq)}, device_id_type=MESH)

    def greet_dp(j, carry):
        pl.semaphore_signal(barrier, inc=1, device_id={DP: lax.rem(d + j, dp)}, device_id_type=MESH)
        return carry

    lax.fori_loop(1, dp, greet_dp, 0)
    pl.semaphore_wait(barrier, seq - 1 + dp - 1)

    emb_base = remote.slots(dp)
    dm_base = remote.slots(dp)

    def send_emb(j):
        to = lax.rem(d + j, dp)
        return remote.make(r.in_emb.at[to], r.emball.at[d], emb_base + j, {DP: to})

    def start_emb(j, carry):
        send_emb(j).start()
        return carry

    lax.fori_loop(1, dp, start_emb, 0)
    own_emb = local.start(r.in_emb.at[d], r.emball.at[d])

    def into_cols(n):
        def finish(total):
            r["out_" + n][...] = total
            store(n)

        return finish

    def into_pack(n):
        def finish(total):
            rows, lanes = total.shape
            if n == "fc2":
                turned = total.T
                r.out_fc2[:, 0:rows] = turned[: lanes // 2]
                r.out_fc2[:, rows : 2 * rows] = turned[lanes // 2 :]
            else:
                r["out_" + n][0:rows, :] = total[:, : lanes // 2]
                r["out_" + n][rows : 2 * rows, :] = total[:, lanes // 2 :]
            store(n)

        return finish

    def into_blocks(total):
        for t in range(3):
            r.fq[t] = total[:, t * group : (t + 1) * group]

    grads = Bag()
    for n, (kind, order) in GRADS.items():
        finish = into_blocks if n == "qkv" else (into_pack(n) if kind == PACK else into_cols(n))
        bufs = [r["r_%s%d" % (n, i)] for i in range(len(order))]
        grads[n] = Grad(r["g_" + n], kind, order, bufs, where, remote, finish)

    rows_own = pl.ds(pl.multiple_of(s * tok, tok), tok)
    seg_row = codes[0:1, rows_own]
    seg = jnp.broadcast_to(column(seg_row)[:, :1], (tok, width))
    clip_id = lax.broadcasted_iota(jnp.int32, (16, tok), 0).astype(F32)
    onehot = jnp.where(clip_id == seg_row, 1.0, 0.0).astype(BF)

    def clip_sum(part, value):
        high = value.astype(BF)
        rest = (value - high.astype(F32)).astype(BF)
        r.dmod[:, part * width : (part + 1) * width] = (nn(onehot, high) + nn(onehot, rest))[:8]

    def square(n, lhs, rhs):
        g = r["g_" + n]

        def four(i, carry):
            val = nn(lhs(i), rhs).astype(BF)
            for g0 in range(2):
                for q in range(seq):
                    half = val.shape[0] // 4
                    low = g0 * 2 * half
                    lane = (q % 2) * 2 * group
                    at = (lax.div(i, 2), lax.rem(i, 2), g0, q // 2)
                    g[at + (slice(None), slice(lane, lane + group))] = val[low : low + half, q * group : (q + 1) * group]
                    g[at + (slice(None), slice(lane + group, lane + 2 * group))] = val[
                        low + half : low + 2 * half, q * group : (q + 1) * group
                    ]
            return carry

        lax.fori_loop(0, 4, four, 0)

    def weight(n):
        return r["g_" + n][...].reshape(width, width)

    core_base = remote.slots(seq)

    def core_copy(c):
        ca, cb = (c // 2, c % 2) if isinstance(c, int) else (lax.div(c, 2), lax.rem(c, 2))
        peer = d + (1 - 2 * bits[0]) * stride
        return remote.make(r.g_fc2.at[ca, cb, 1 - bits[0]], r.r_fc20.at[ca, cb], core_base + c, {DP: peer})

    v = pltpu.VMEM
    dkv_copies = []
    quarter = 2 * width // seq
    do_base = remote.slots(seq)

    def send_do(k):
        to = lax.rem(s + k, seq)
        return remote.make(r.dosend.at[to], r.dorecv.at[s], do_base + k, {SEQ: to})

    def kv_part(a, owner):
        lanes = pl.ds(pl.multiple_of(owner * quarter, quarter), quarter)
        return r.kv.at[pl.ds(a * keys // 2, keys // 2), lanes]

    def begin_kv():
        for a in range(2):
            for w, owner in enumerate((flip[1 + a], flip[3])):

                def describe(a=a, w=w, owner=owner):
                    return kv_part(a, owner), r.dkvr.at[a, w], {SEQ: flip[1 + a]}

                dkv_copies.append(remote.start(describe))

    def step_kv():
        for c in dkv_copies:
            c().wait_recv()
        dkv_copies.clear()
        for a in range(2):
            for w, owner in enumerate((s, flip[2 - a])):
                own = kv_part(a, owner)
                own[...] = (own[...].astype(F32) + r.dkvr[a, w].astype(F32)).astype(BF)

            def describe(a=a):
                return kv_part(a, flip[2 - a]), r.dkvs.at[a], {SEQ: flip[2 - a]}

            dkv_copies.append(remote.start(describe))

    def end_kv():
        for c in dkv_copies:
            c().wait_recv()
        for a in range(2):
            own = kv_part(a, s)[...].astype(F32) + r.dkvs[a].astype(F32)
            r.dkvq[a * seq // 2 : (a + 1) * seq // 2] = own.astype(BF).reshape(seq // 2, tl, quarter)

    def middle(*held):
        for n, ref in zip(K2_HELD, held):
            r[n] = ref
            loads[n] = local.start(r["in_" + n], ref)

        loads.x2.wait()
        loads.cot.wait()
        x2v = r.x2[...]
        n3, _ = norm_parts(x2v)
        h3 = (n3 * (1.0 + pick(mods, seg, 4, width)) + pick(mods, seg, 3, width)).astype(BF)

        def feed(h3_ref, h3T_ref, dm_ref, m_ref, dh_ref):
            h3_ref[...] = h3
            h3T_ref[...] = h3.astype(F32).T.astype(BF)
            dm_ref[...] = (pick(mods, seg, 5, width) * r.cot[...].astype(F32)).astype(BF)
            m_ref[...] = jnp.zeros_like(m_ref)
            dh_ref[...] = jnp.zeros_like(dh_ref)
            g1, g2 = r.g_fc1, r.g_fc2
            k0, k1 = math.sqrt(2.0 / math.pi), 0.044715

            def one(c, carry):
                load_chunk(0, c).wait()
                load_chunk(1, c).wait()
                cols = pl.ds(pl.multiple_of(c * chunk, chunk), chunk)
                ca, cb = lax.div(c, 2), lax.rem(c, 2)
                w1 = g1[:, :, :, :, cols].reshape(width, chunk)
                w2 = g2[ca, cb].reshape(chunk, width)
                z = nn(h3_ref[...], w1)
                zz = z * z
                t = jnp.tanh(k0 * (z + k1 * z * zz))
                u = (0.5 * z * (1.0 + t)).astype(BF)
                slope = 0.5 * (1.0 + t) + 0.5 * z * (1.0 - t * t) * (k0 * (1.0 + 3.0 * k1 * zz))
                m_ref[...] += nn(u, w2)
                dz = (nt(dm_ref[...], w2) * slope).astype(BF)
                dh_ref[...] += nt(dz, w1)
                g1[:, :, :, :, cols] = nn(h3T_ref[...], dz).astype(BF).reshape(2, 2, 2, width // BLOCKS, chunk)
                for g0 in range(2):
                    half = chunk // 4
                    val = tn(u[:, g0 * 2 * half : (g0 + 1) * 2 * half], dm_ref[...]).astype(BF)
                    for q in range(seq):
                        lane = (q % 2) * 2 * group
                        g2[ca, cb, g0, q // 2, :, lane : lane + group] = val[:half, q * group : (q + 1) * group]
                        g2[ca, cb, g0, q // 2, :, lane + group : lane + 2 * group] = val[half:, q * group : (q + 1) * group]
                core_copy(c).start()
                return carry

            lax.fori_loop(0, seq, one, 0)
            grads.fc2.copies = [functools.partial(core_copy, c) for c in range(seq)]
            for c in range(seq):
                remote.open.append(lambda c=c: core_copy(c).wait_send())
            grads.fc1.begin()
            dy = r.cot[...].astype(F32)
            m = m_ref[...]
            x2w = r.x2[...]
            r.out_block_out[...] = (x2w + pick(mods, seg, 5, width) * m).astype(BF)
            store("block_out")
            clip_sum(5, dy * m)
            dh = dh_ref[...]
            nw, rstd = norm_parts(x2w)
            clip_sum(3, dh)
            clip_sum(4, dh * nw)
            r.dx[...] = dy + norm_back(dh * (1.0 + pick(mods, seg, 4, width)), nw, rstd)
            grads.fc2.step()

        pl.run_scoped(feed, v((tok, width), BF), v((width, tok), BF), v((tok, width), BF), v((tok, width), F32), v((tok, width), F32))

        for c in (loads.w_cout, loads.coT, loads.cqT, loads.lsec, loads.kv, loads.ckT):
            c.wait()

        def cross_back(dcoT, dcqT, biasc):
            dc = r.dx[...].astype(BF)
            dcoT[...] = nt(weight("cout"), dc).astype(BF)
            square("cout", lambda i: r.coT[pl.ds(pl.multiple_of(i * group, group), group), :], dc)
            grads.cout.begin()
            tcol = column(codes[2:3, :keys])
            biasc[...] = jnp.where(jnp.broadcast_to(tcol[:, :1], (keys, tok)) == seg_row, 0.0, MASKED)
            grads.fc1.step()
            kv = r.kv

            def pair(p, carry):
                cols = pl.ds(pl.multiple_of(p * 128, 128), 128)
                vcols = pl.ds(pl.multiple_of(width + p * 128, 128), 128)
                ck, cv = kv[:, cols], kv[:, vcols]
                parts_k, parts_v = [], []
                for a in range(2):
                    hrows = pl.ds(pl.multiple_of(p * 128 + a * HD, HD), HD)
                    q_h, do_h = r.cqT[hrows, :], dcoT[hrows, :]
                    lse_h = r.lsec[pl.ds(2 * p + a, 1), :]
                    pr = jnp.exp(nn(ck[:, a * HD : (a + 1) * HD], q_h) + biasc[...] - lse_h)
                    dpr = nn(cv[:, a * HD : (a + 1) * HD], do_h)
                    delta = jnp.sum(pr * dpr, axis=0, keepdims=True)
                    ds = (pr * (dpr - delta)).astype(BF)
                    parts_k.append(nt(ds, q_h))
                    parts_v.append(nt(pr.astype(BF), do_h))
                    dcqT[hrows, :] = nn(r.ckT[hrows, :], ds) * SCALE
                kv[:, cols] = jnp.concatenate(parts_k, axis=1).astype(BF)
                kv[:, vcols] = jnp.concatenate(parts_v, axis=1).astype(BF)
                return carry

            lax.fori_loop(0, H // 2, pair, 0)
            grads.fc2.step()
            dcq = dcqT[...].T.astype(BF)
            loads.w_cq.wait()
            loads.h2T.wait()
            loads.x1.wait()
            dh2 = nt(dcq, weight("cq"))
            square("cq", lambda i: r.h2T[pl.ds(pl.multiple_of(i * group, group), group), :], dcq)
            nw, rstd = norm_parts(r.x1[...])
            r.dx[...] += norm_back(dh2, nw, rstd)

        pl.run_scoped(cross_back, v((width, tok), BF), v((width, tok), F32), v((keys, tok), F32))

        grads.fc1.step()
        for c in (loads.w_proj, loads.aout, loads.oT):
            c.wait()
        dx1 = r.dx[...]
        da = (pick(mods, seg, 2, width) * dx1).astype(BF)
        doT = nt(weight("proj"), da).astype(BF)
        for q in range(seq):
            r.dosend[q] = doT[q * group : (q + 1) * group, :]
        for k in range(1, seq):
            send_do(k).start()
        r.dorecv[s] = r.dosend[s]
        grads.cq.begin()
        grads.cout.step()
        begin_kv()
        clip_sum(2, dx1 * r.aout[...])
        square("proj", lambda i: r.oT[i], da)
        grads.proj.begin()
        for c in (loads.qT, loads.kT, loads.kn, loads.vn, loads.lse):
            c.wait()

        def self_back(kcol, bias, dk, dv):
            kcol[...] = column(codes[1:2, :full])
            dk[...] = jnp.zeros_like(dk)
            dv[...] = jnp.zeros_like(dv)

            def block(k, carry):
                @pl.when(k > 0)
                def _():
                    send_do(k).wait_recv()

                at = lax.rem(s - k + seq, seq)
                rows = pl.ds(pl.multiple_of(at * tok, tok), tok)
                row_id = lax.broadcasted_iota(jnp.int32, (full, tok), 0)
                col_id = lax.broadcasted_iota(jnp.int32, (full, tok), 1) + at * tok
                key = jnp.broadcast_to(kcol[:, :1], (full, tok))
                bias[...] = jnp.where((key == codes[0:1, rows]) | (row_id == col_id), 0.0, MASKED)
                for h in range(hl):
                    hs = slice(h * HD, (h + 1) * HD)
                    q_h, do_h = r.qT[hs, rows], r.dorecv[at, hs, :]
                    pr = jnp.exp(nn(r.kn[h], q_h) + bias[...] - r.lse[h : h + 1, rows])
                    dpr = nn(r.vn[h], do_h)
                    delta = jnp.sum(pr * dpr, axis=0, keepdims=True)
                    ds = (pr * (dpr - delta)).astype(BF)
                    dk[h] += nt(ds, q_h)
                    dv[h] += nt(pr.astype(BF), do_h)
                    dq = nn(r.kT[hs, :], ds) * SCALE
                    r.dqs[at, :, hs] = dq.T.astype(BF)
                return carry

            lax.fori_loop(0, 2, block, 0)
            grads.fc1.step()
            grads.fc2.step()
            lax.fori_loop(2, seq, block, 0)
            for h in range(hl):
                for b in range(seq):
                    br = slice(b * tok, (b + 1) * tok)
                    r.dqs[b, :, group + h * HD : group + (h + 1) * HD] = dk[h, br, :].astype(BF)
                    r.dqs[b, :, 2 * group + h * HD : 2 * group + (h + 1) * HD] = dv[h, br, :].astype(BF)

        pl.run_scoped(self_back, v((full, 128), F32), v((full, tok), F32), v((hl, full, HD), F32), v((hl, full, HD), F32))

    pl.run_scoped(
        middle,
        v((width, keys), BF),
        v((group, full), BF),
        v((group, full), BF),
        v((hl, full, HD), BF),
        v((hl, full, HD), BF),
    )

    dq_base = remote.slots(seq)

    def send_dq(k):
        to = lax.rem(s + k, seq)
        return remote.make(r.dqs.at[to], r.dqr.at[s], dq_base + k, {SEQ: to})

    for k in range(1, seq):
        send_dq(k).start()
    step_kv()
    for n in ("cq", "proj", "cout"):
        grads[n].step()
    r.dqr[s] = r.dqs[s]

    def tail(h1, text, wqkv, wckv, dqf):
        tail_loads = [
            local.start(a, b)
            for a, b in ((r.in_h1, h1), (r.w_qkv, wqkv), (r.in_text, text), (r.w_ckv, wckv))
        ]
        loads.x.wait()
        tail_loads[0].wait()
        gq = tn(h1[...].reshape(full, width), r.dqs[...].reshape(full, 3 * group))
        r.g_qkv[...] = gq.astype(BF).reshape(2, 2, 2, width // BLOCKS, 3 * group)
        grads.qkv.begin()
        grads.qkv.step()
        grads.fc2.step()
        for k in range(1, seq):
            send_dq(k).wait_recv()
        for b in range(seq):
            got = r.dqr[b]
            for t in range(3):
                dqf[:, t * width + b * group : t * width + (b + 1) * group] = got[:, t * group : (t + 1) * group]
        tail_loads[1].wait()
        dh1 = nt(dqf[...], wqkv[...])
        nx, rstd = norm_parts(r.x[...].astype(F32))
        clip_sum(0, dh1)
        clip_sum(1, dh1 * nx)
        dm_copies = []
        part = 6 * width // seq
        for k in range(1, seq):

            def describe_dm(k=k):
                to = lax.rem(s + k, seq)
                lanes = pl.ds(pl.multiple_of(to * part, part), part)
                return r.dmod.at[:, lanes], r.dmr.at[k - 1], {SEQ: to}

            dm_copies.append(remote.start(describe_dm))
        back = norm_back(dh1 * (1.0 + pick(mods, seg, 1, width)), nx, rstd)
        r.out_grad_frames[...] = (r.dx[...] + back).astype(BF)
        store("grad_frames")
        end_kv()
        kv_base = remote.slots(seq)

        def send_kv(k):
            to = lax.rem(s + k, seq)
            return remote.make(r.dkvq.at[to], r.dkvl.at[s], kv_base + k, {SEQ: to})

        for k in range(1, seq):
            send_kv(k).start()
        r.dkvl[s] = r.dkvq[s]
        tail_loads[2].wait()
        gc = tn(text[...].reshape(keys, dc_all), r.dkvq[...].reshape(keys, quarter))
        r.g_ckv[...] = gc.astype(BF).reshape(2, 2, 2, dc_all // BLOCKS, quarter)
        grads.ckv.begin()
        for n in ("qkv", "cq", "proj", "cout", "fc1", "ckv"):
            grads[n].step()
        for c in dm_copies:
            c().wait_recv()
        total = r.dmod[:, pl.ds(pl.multiple_of(s * part, part), part)]
        for k in range(seq - 1):
            total = total + r.dmr[k]
        r.dmall[d] = total

        def send_dm(j):
            to = lax.rem(d + j, dp)
            return remote.make(r.dmall.at[d], r.dmall.at[d], dm_base + j, {DP: to})

        def start_dm(j, carry):
            send_dm(j).start()
            return carry

        lax.fori_loop(1, dp, start_dm, 0)
        grads.fc2.step()
        grads.qkv.step()
        q_base = remote.slots(3)

        def send_q(t):
            b = 4 * t + s
            to = lax.div(b, 3)
            slot = b - 3 * to
            return to, slot, pltpu.make_async_remote_copy(
                src_ref=r.fq.at[t],
                dst_ref=r.rq.at[slot],
                send_sem=r.ssem.at[q_base + t],
                recv_sem=r.rsem.at[q_base + slot],
                device_id={SEQ: to},
                device_id_type=MESH,
            )

        for t in range(3):
            to, slot, copy = send_q(t)

            @pl.when(to != s)
            def _():
                copy.start()

            @pl.when(to == s)
            def _():
                r.rq[slot] = r.fq[t]

        for n in ("cout", "cq", "proj", "ckv"):
            grads[n].step()
        for k in range(1, seq):
            send_kv(k).wait_recv()
        tail_loads[3].wait()
        gt = nt(r.dkvl[0], wckv[:, 0:quarter])
        for b in range(1, seq):
            gt = gt + nt(r.dkvl[b], wckv[:, b * quarter : (b + 1) * quarter])
        r.out_grad_text[...] = gt.astype(BF)
        store("grad_text")
        for n in ("cq", "proj", "cout", "ckv", "fc1", "cq", "proj"):
            grads[n].step()

        def wait_dm(j, carry):
            send_dm(j).wait_recv()
            send_emb(j).wait_recv()
            return carry

        own_emb.wait()
        lax.fori_loop(1, dp, wait_dm, 0)
        emb = r.emball[...].reshape(dp * 8, 128)
        allm = r.dmall[...].reshape(dp * 8, part)
        high = allm.astype(BF)
        rest = (allm - high.astype(F32)).astype(BF)
        ga = tn(emb, high) + tn(emb, rest)
        r.out_ada[...] = ga[: width // dp]
        store("ada")
        for j in range(3):
            src = lax.rem(3 * s + j, seq)

            @pl.when(src != s)
            def _():
                remote.make(r.fq.at[j], r.rq.at[j], q_base + j, {SEQ: src}).wait_recv()

            r.out_qkv[:, j * group : (j + 1) * group] = r.rq[j]
        store("qkv")

        for t in range(3):
            to, slot, copy = send_q(t)

            @pl.when(to != s)
            def _():
                copy.wait_send()

        for k in range(1, seq):
            send_do(k).wait_send()
            send_dq(k).wait_send()
            send_kv(k).wait_send()

        def wait_sent(j, carry):
            send_dm(j).wait_send()
            send_emb(j).wait_send()
            return carry

        lax.fori_loop(1, dp, wait_sent, 0)
        for sent in remote.open:
            sent()
        for n, slot in stores:
            stored(n, slot).wait()

    pl.run_scoped(
        tail,
        v((seq, tok, width), BF),
        v((seq, tl, dc_all), BF),
        v((width, 3 * width), BF),
        v((dc_all, 2 * width), BF),
        v((tok, 3 * width), BF),
    )


def run_backward(dims, dp, fwd, args):
    seq, tok, full, width, keys, group, dc = dims
    hl, tl, block = H // seq, keys // seq, width // BLOCKS
    ff = 4 * width
    v = pltpu.VMEM
    lead = (2, 2, 2)
    gshape = dict(
        fc1=(block, ff),
        fc2=(2, ff // BLOCKS // 2, width),
        cout=(2, block // 2, width),
        cq=(2, block // 2, width),
        proj=(2, block // 2, width),
        ckv=(dc // BLOCKS, 2 * width // seq),
        qkv=(block, 3 * group),
    )
    names, ins, specs = [], [], []

    def add_in(spec=ANY, **kw):
        for name, value in kw.items():
            names.append(name)
            ins.append(value)
            specs.append(spec)

    add_in(codes=fwd.codes, spec=INV)
    add_in(mods=fwd.mods, spec=INV)
    add_in(in_x=args.x)
    add_in(in_cot=args.cot)
    add_in(in_emb=args.emb)
    for n in K2_LOADS + K2_HELD + ("h1", "text"):
        add_in(**{"in_" + n: fwd[n]})
    for n in K2_WEIGHTS:
        add_in(**{"w_" + n: args[n].reshape(lead + gshape[n])})
    add_in(w_ckv=args.ckv)
    add_in(w_qkv=args.qkv)

    outs = dict(
        block_out=((tok, width), BF),
        grad_frames=((tok, width), BF),
        grad_text=((tl, dc), BF),
        ada=((width // dp, 6 * width // seq), F32),
        qkv=((block, 3 * group), F32),
        proj=((block, group), F32),
        cq=((block, group), F32),
        ckv=((dc // BLOCKS, 2 * width // seq), F32),
        cout=((block, group), F32),
        fc1=((block, ff // seq), F32),
        fc2=((group, ff // BLOCKS), F32),
    )
    for n in K2_OUTS:
        names.append("hbm_" + n)
    scratch = []

    def add(**kw):
        for name, (shape, dtype) in kw.items():
            names.append(name)
            scratch.append(v(shape, dtype))

    for n in K2_OUTS:
        add(**{"out_" + n: outs[n]})
    add(cot=((tok, width), BF))
    add(x=((tok, width), BF))
    for n in K2_LOADS:
        add(**{n: (fwd[n].shape, fwd[n].dtype)})
    for n, (kind, order) in GRADS.items():
        add(**{"g_" + n: (lead + gshape[n], BF)})
        for i, b in enumerate(grad_buffers(gshape[n], kind, order, seq)):
            names.append("r_%s%d" % (n, i))
            scratch.append(b)
    quarter = 2 * width // seq
    add(dx=((tok, width), F32))
    add(dkvr=((2, 2, keys // 2, quarter), BF))
    add(dkvs=((2, keys // 2, quarter), BF))
    add(dkvq=((seq, tl, quarter), BF))
    add(dkvl=((seq, tl, quarter), BF))
    add(dosend=((seq, group, tok), BF))
    add(dorecv=((seq, group, tok), BF))
    add(dqs=((seq, tok, 3 * group), BF))
    add(dqr=((seq, tok, 3 * group), BF))
    add(dmod=((8, 6 * width), F32))
    add(dmr=((seq - 1, 8, 6 * width // seq), F32))
    add(dmall=((dp, 8, 6 * width // seq), F32))
    add(emball=((dp, 8, 128), BF))
    add(fq=((3, block, group), F32))
    add(rq=((3, block, group), F32))
    count = 2 * dp + 96
    for n, k in dict(lsem=64, ssem=count, rsem=count).items():
        names.append(n)
        scratch.append(pltpu.SemaphoreType.DMA((k,)))
    got = pl.pallas_call(
        functools.partial(backward_kernel, dims, tuple(names), dp),
        out_shape=[jax.ShapeDtypeStruct(*outs[n]) for n in K2_OUTS],
        in_specs=specs,
        out_specs=[ANY] * len(K2_OUTS),
        scratch_shapes=scratch,
        compiler_params=pltpu.CompilerParams(
            collective_id=1, has_side_effects=True, vmem_limit_bytes=67043328
        ),
        name="backward_part",
    )(*ins)
    return Bag(zip(K2_OUTS, got))


def hand_over(*refs):
    count = len(K2_OUTS)
    ins, outs, held, sems = refs[:count], refs[count : 2 * count], refs[2 * count : -1], refs[-1]
    first = [pltpu.make_async_copy(a, b, sems.at[0, i]) for i, (a, b) in enumerate(zip(ins, held))]
    second = [pltpu.make_async_copy(a, b, sems.at[1, i]) for i, (a, b) in enumerate(zip(held, outs))]
    for c in first:
        c.start()
    for c, n in zip(first, second):
        c.wait()
        n.start()
    for c in second:
        c.wait()


def run_hand_over(g):
    values = [g[n] for n in K2_OUTS]
    got = pl.pallas_call(
        hand_over,
        out_shape=[jax.ShapeDtypeStruct(a.shape, a.dtype) for a in values],
        in_specs=[ANY] * len(values),
        out_specs=[ANY] * len(values),
        scratch_shapes=[pltpu.VMEM(a.shape, a.dtype) for a in values] + [pltpu.SemaphoreType.DMA((2, len(values)))],
        name="hand_over",
    )(*values)
    return Bag(zip(K2_OUTS, got))


def per_device(
    frames, seg_ids, padding, step_ids, text_states, text_len, w_ada, w_qkv, w_proj, w_cq, w_ckv, w_cout, w_fc1, w_fc2,
    cotangent,
):
    rows, tok, width = frames.shape
    seq, dp = lax.axis_size(SEQ), lax.axis_size(DP)
    segs = step_ids.shape[1]
    full = seg_ids.shape[1]
    tl, dc = text_states.shape[2], text_states.shape[3]
    keys = segs * tl * seq
    group = (H // seq) * HD
    dims = (seq, tok, full, width, keys, group, dc)
    emb = embed_steps(jnp.pad(step_ids[0], (0, 8 - segs)), width).astype(BF)
    span = width // dp
    emb_parts = jnp.pad(jnp.swapaxes(emb.reshape(8, dp, span), 0, 1), ((0, 0), (0, 0), (0, 128 - span)))
    x = frames[0]
    text = text_states.reshape(segs * tl, dc)
    fwd = run_forward(dims, (x, text, seg_ids, padding, text_len, emb, w_ada, w_qkv, w_ckv, w_proj, w_cq, w_cout))
    args = Bag(
        x=x, cot=cotangent[0], emb=emb_parts, ckv=w_ckv, qkv=w_qkv,
        fc1=w_fc1, fc2=w_fc2, cout=w_cout, cq=w_cq, proj=w_proj,
    )
    g = run_hand_over(run_backward(dims, dp, fwd, args))
    stride = dp // BLOCKS
    if stride > 1:
        groups = [[b * stride + j for j in range(stride)] for b in range(BLOCKS)]
        for n in GRADS:
            g[n] = lax.psum_scatter(g[n], DP, scatter_dimension=1 if n == "fc2" else 0, axis_index_groups=groups, tiled=True)
    return (
        g.block_out.reshape(frames.shape),
        g.grad_frames.reshape(frames.shape),
        g.grad_text.reshape(text_states.shape),
        g.ada, g.qkv, g.proj, g.cq, g.ckv, g.cout, g.fc1, g.fc2.T,
    )


def solution(mesh):
    own, row, rep = P(DP, SEQ, None), P(DP, None), P()
    text, grad = P(DP, None, SEQ, None), P(DP, SEQ)
    return jax.shard_map(
        per_device,
        mesh=mesh,
        in_specs=(own, row, row, row, text, row) + (rep,) * 8 + (own,),
        out_specs=(own, own, text) + (grad,) * 8,
        check_vma=False,
    )
```

```python
import functools
import math

import jax
import jax.numpy as jnp
from jax import lax
from jax.experimental import pallas as pl
from jax.experimental.pallas import tpu as pltpu
from jax.sharding import PartitionSpec as P

H = 12
HD = 64
BLOCKS = 8
SEQ = "seq"
DP = "dp"
COLS, PACK = 1, 2
CUT, XY1, XY2, L0, L1, L2 = 3, 4, 5, 6, 7, 8
BF = jnp.bfloat16
F32 = jnp.float32
MESH = pl.DeviceIdType.MESH
MASKED = -1e30
EPS = 1e-06
SCALE = HD ** (-0.5)
ANY = pl.BlockSpec(memory_space=pl.ANY)
INV = pl.BlockSpec(memory_space=pltpu.VMEM)


def nn(a, b):
    return lax.dot_general(a, b, (((1,), (0,)), ((), ())), preferred_element_type=F32)


def nt(a, b):
    return lax.dot_general(a, b, (((1,), (1,)), ((), ())), preferred_element_type=F32)


def tn(a, b):
    return lax.dot_general(a, b, (((0,), (0,)), ((), ())), preferred_element_type=F32)


def embed_steps(step_values, width_all):
    half_width = width_all // 2
    frequency = jnp.exp(
        -math.log(10000.0) * jnp.arange(half_width).astype(F32) / half_width
    )
    angles = step_values.astype(F32)[..., None] * frequency
    return jax.nn.silu(jnp.concatenate([jnp.cos(angles), jnp.sin(angles)], axis=-1))


def norm_parts(v):
    centered = v - jnp.mean(v, axis=-1, keepdims=True)
    rstd = lax.rsqrt(jnp.mean(centered * centered, axis=-1, keepdims=True) + EPS)
    return centered * rstd, rstd


def norm_back(g, n, rstd):
    return (g - jnp.mean(g, axis=-1, keepdims=True) - n * jnp.mean(g * n, axis=-1, keepdims=True)) * rstd


def pick(mods, seg, part, width):
    low = part * width
    a = mods[0:1, low : low + width]
    b = mods[1:2, low : low + width]
    c = mods[2:3, low : low + width]
    return jnp.where(seg == 0.0, a, jnp.where(seg == 1.0, b, c))


def column(row):
    return jnp.broadcast_to(row, (128, row.shape[1])).T


class Bag(dict):
    __getattr__ = dict.__getitem__


class Remote:
    def __init__(self, send, recv):
        self.send, self.recv, self.used, self.open = send, recv, 0, []

    def slots(self, count):
        first = self.used
        self.used += count
        return first

    def make(self, src, dst, slot, where):
        return pltpu.make_async_remote_copy(
            src_ref=src,
            dst_ref=dst,
            send_sem=self.send.at[slot],
            recv_sem=self.recv.at[slot],
            device_id=where,
            device_id_type=MESH,
        )

    def start(self, describe, when=None):
        slot = self.slots(1)

        def again():
            src, dst, where = describe()
            return self.make(src, dst, slot, where)

        def launch():
            again().start()

        def sent():
            again().wait_send()

        if when is None:
            launch()
            self.open.append(sent)
        else:
            pl.when(when())(launch)
            self.open.append(lambda: pl.when(when())(sent))
        return again


class Local:
    def __init__(self, sems):
        self.sems, self.used = sems, 0

    def start(self, src, dst):
        copy = pltpu.make_async_copy(src, dst, self.sems.at[self.used])
        self.used += 1
        copy.start()
        return copy


def greet(seq, at_seq, dp_peers):
    barrier = pltpu.get_barrier_semaphore()
    for k in range(1, seq):
        pl.semaphore_signal(
            barrier, inc=1, device_id={SEQ: lax.rem(at_seq + k, seq)}, device_id_type=MESH
        )
    for peer in dp_peers:
        pl.semaphore_signal(barrier, inc=1, device_id={DP: peer}, device_id_type=MESH)
    pl.semaphore_wait(barrier, seq - 1 + len(dp_peers))


K1_OUTS = tuple(dict(h1=0, qT=0, kT=0, kn=0, vn=0, lse=0, oT=0, aout=0, x1=0, h2T=0, cqT=0, kv=0, ckT=0, lsec=0, coT=0, x2=0, text=0, mods=0, codes=0))


def forward_kernel(dims, segs, *refs):
    seq, tok, full, width, keys, group, dc = dims
    hl = H // seq
    ins, refs = refs[:12], refs[12:]
    x_hbm, text_hbm, seg_in, pad_in, len_in, emb, wada_hbm, wqkv_hbm, wckv_hbm, wp_hbm, wcq_hbm, wco_hbm = ins
    outs, refs = Bag(zip(K1_OUTS, refs[: len(K1_OUTS)])), refs[len(K1_OUTS) :]
    (
        x_all, text_all, wg, wckv, wp, wcq, wco, qT, kT, vT, kn, vn, lse, osend, orecv, aout, x1, h2T, cqT, kv, kvT,
        lsec, coT, x2, bias, biasc, kcol, tcol, xin, wada, mods, codes, h1_all, lsem, ssem, rsem,
    ) = refs
    local, remote = Local(lsem), Remote(ssem, rsem)
    s = lax.axis_index(SEQ)
    load_x = local.start(x_hbm, xin)
    load_own = local.start(x_hbm, x_all.at[s])
    load_ada = local.start(wada_hbm, wada)
    first = lax.div(s * group, 128) * 128
    odd = lax.rem(s * group, 128) > 0
    load_wg = [
        local.start(
            wqkv_hbm.at[:, pl.ds(pl.multiple_of(t * width + first, 128), 256)], wg.at[:, pl.ds(t * 256, 256)]
        )
        for t in range(3)
    ]
    load_text = local.start(text_hbm, text_all.at[s])
    load_w = [local.start(a, b) for a, b in ((wckv_hbm, wckv), (wp_hbm, wp), (wcq_hbm, wcq), (wco_hbm, wco))]
    greet(seq, s, ())

    base_x = remote.slots(5)
    base_t = remote.slots(5)
    base_o = remote.slots(4)
    sx, sy = lax.rem(s, 2), lax.div(s, 2)

    def other(k):
        kx, ky = (k % 2, k // 2) if isinstance(k, int) else (lax.rem(k, 2), lax.div(k, 2))
        return 2 * (sy + ky - 2 * sy * ky) + sx + kx - 2 * sx * kx

    def direct(src, held, base, m):
        return remote.make(src, held.at[s], base + m, {SEQ: other(m)})

    def relay(held, base, m):
        half = held.shape[1] // 2
        part = held.at[other(3 - m), pl.ds((m - 1) * half, half)]
        return remote.make(part, part, base + 2 + m, {SEQ: other(m)})

    for m in (1, 2):
        direct(x_hbm, x_all, base_x, m).start()

    tl = keys // seq // segs
    place = lax.broadcasted_iota(jnp.int32, (1, full), 1).astype(F32)
    block = jnp.floor((place + 0.5) / tl)
    owner = jnp.floor((block + 0.5) / segs)
    clip = block - owner * segs
    length = jnp.zeros((1, full), F32)
    for c in range(segs):
        length = jnp.where(clip == c, jnp.broadcast_to(len_in[0:1, c : c + 1].astype(F32), (1, full)), length)
    codes[...] = jnp.zeros_like(codes)
    codes[0:1, :] = seg_in[...].astype(F32)
    codes[1:2, :] = jnp.where(pad_in[...] == 1, seg_in[...].astype(F32), -1.0)
    codes[2:3, :] = jnp.where(owner * tl + place - block * tl < length, clip, -1.0)
    save_codes = local.start(codes, outs.codes)
    kcol[...] = column(codes[1:2, :full])
    tcol[...] = column(codes[2:3, :keys])
    load_x.wait()
    load_own.wait()
    load_ada.wait()
    mods[...] = jnp.zeros_like(mods)
    mods[0:segs, :] = nn(emb[...], wada[...])
    save_mods = local.start(mods, outs.mods)
    for c in load_wg:
        c.wait()

    def project(k, carry):
        @pl.when(k == 1)
        def _():
            for m in (1, 2):
                direct(x_hbm, x_all, base_x, m).wait_recv()
            for m in (1, 2):
                relay(x_all, base_x, m).start()
            for m in (1, 2):
                direct(text_hbm, text_all, base_t, m).start()

        @pl.when(k == 3)
        def _():
            for m in (1, 2):
                relay(x_all, base_x, m).wait_recv()

        at = other(k)
        rows = pl.ds(pl.multiple_of(at * tok, tok), tok)
        seg = column(codes[0:1, rows])[:, :1]
        seg = jnp.broadcast_to(seg, (tok, width))
        n, _ = norm_parts(x_all[at].astype(F32))
        h1 = (n * (1.0 + pick(mods, seg, 1, width)) + pick(mods, seg, 0, width)).astype(BF)
        h1_all[at] = h1
        wide = nn(h1, wg[...])
        out = jnp.concatenate(
            [
                jnp.where(odd, wide[:, t * 256 + 64 : t * 256 + 64 + group], wide[:, t * 256 : t * 256 + group])
                for t in range(3)
            ],
            axis=1,
        )
        for h in range(hl):
            kn[h, rows, :] = out[:, group + h * HD : group + (h + 1) * HD].astype(BF)
            vn[h, rows, :] = out[:, 2 * group + h * HD : 2 * group + (h + 1) * HD].astype(BF)
        low = out.astype(BF).astype(F32)
        outT = low.T
        qT[:, rows] = (outT[:group] * SCALE).astype(BF)
        kT[:, rows] = outT[group : 2 * group].astype(BF)
        vT[:, rows] = outT[2 * group :].astype(BF)
        return carry

    lax.fori_loop(0, seq, project, 0)
    saves = [save_mods, save_codes] + [
        local.start(a, b)
        for a, b in ((h1_all, outs.h1), (qT, outs.qT), (kT, outs.kT), (kn, outs.kn), (vn, outs.vn))
    ]

    def send_o(k):
        at = other(k)
        return remote.make(osend.at[at], orecv.at[s], base_o + k, {SEQ: at})

    def attend(k, carry):
        @pl.when(k == 3)
        def _():
            for m in (1, 2):
                direct(text_hbm, text_all, base_t, m).wait_recv()
            for m in (1, 2):
                relay(text_all, base_t, m).start()

        at = other(3 - k)
        rows = pl.ds(pl.multiple_of(at * tok, tok), tok)
        seg = codes[0:1, rows]
        row_id = lax.broadcasted_iota(jnp.int32, (full, tok), 0)
        col_id = lax.broadcasted_iota(jnp.int32, (full, tok), 1) + at * tok
        key = jnp.broadcast_to(kcol[:, :1], (full, tok))
        bias[...] = jnp.where((key == seg) | (row_id == col_id), 0.0, MASKED)

        def head(h, c2):
            hrows = pl.ds(pl.multiple_of(h * HD, HD), HD)
            st = nn(kn[h], qT[hrows, rows]) + bias[...]
            peak = jnp.max(st, axis=0, keepdims=True)
            ex = jnp.exp(st - peak)
            total = jnp.sum(ex, axis=0, keepdims=True)
            ov = nn(vT[hrows, :], ex.astype(BF)) * (1.0 / total)
            osend[at, hrows, :] = ov.astype(BF)
            lse[pl.ds(h, 1), rows] = peak + jnp.log(total)
            return c2

        lax.fori_loop(0, hl, head, 0)

        @pl.when(k < seq - 1)
        def _():
            send_o(3 - k).start()

        return carry

    lax.fori_loop(0, seq, attend, 0)
    orecv[s] = osend[s]

    load_text.wait()
    saves.append(local.start(lse, outs.lse))
    for c in load_w:
        c.wait()
    tl = keys // seq

    def project_text(k, carry):
        @pl.when(k == 3)
        def _():
            for m in (1, 2):
                relay(text_all, base_t, m).wait_recv()

        b = other(k)
        trows = pl.ds(pl.multiple_of(b * tl, tl), tl)
        kv[trows, :] = nn(text_all[b], wckv[...]).astype(BF)
        return carry

    lax.fori_loop(0, seq, project_text, 0)
    saves.append(local.start(text_all, outs.text))

    def turn_text(c, carry):
        cols = pl.ds(pl.multiple_of(c * 256, 256), 256)
        kvT[cols, :] = kv[:, cols].astype(F32).T.astype(BF)
        return carry

    lax.fori_loop(0, 2 * width // 256, turn_text, 0)
    rows = pl.ds(pl.multiple_of(s * tok, tok), tok)
    seg_row = codes[0:1, rows]
    biasc[...] = jnp.where(jnp.broadcast_to(tcol[:, :1], (keys, tok)) == seg_row, 0.0, MASKED)
    saves.append(local.start(kv, outs.kv))
    saves.append(local.start(kvT.at[pl.ds(0, width)], outs.ckT))

    for k in range(1, seq):
        send_o(k).wait_recv()
    saves.append(local.start(orecv, outs.oT))
    seg = jnp.broadcast_to(column(seg_row)[:, :1], (tok, width))
    branch = tn(orecv[...].reshape(width, tok), wp[...])
    aout[...] = branch
    mid = xin[...].astype(F32) + pick(mods, seg, 2, width) * branch
    x1[...] = mid
    n, _ = norm_parts(mid)
    h2 = n.astype(BF)
    h2T[...] = n.astype(BF).astype(F32).T.astype(BF)
    cq = nn(h2, wcq[...]).astype(BF).astype(F32)
    cqT[...] = (cq.T * SCALE).astype(BF)
    saves += [local.start(a, b) for a, b in ((aout, outs.aout), (x1, outs.x1), (h2T, outs.h2T), (cqT, outs.cqT))]

    def cross(p, carry):
        cols = pl.ds(pl.multiple_of(p * 128, 128), 128)
        pair = kv[:, cols]
        for a in range(2):
            hrows = pl.ds(pl.multiple_of(p * 128 + a * HD, HD), HD)
            vrows = pl.ds(pl.multiple_of(width + p * 128 + a * HD, HD), HD)
            st = nn(pair[:, a * HD : (a + 1) * HD], cqT[hrows, :]) + biasc[...]
            peak = jnp.max(st, axis=0, keepdims=True)
            ex = jnp.exp(st - peak)
            total = jnp.sum(ex, axis=0, keepdims=True)
            ov = nn(kvT[vrows, :], ex.astype(BF)) * (1.0 / total)
            coT[hrows, :] = ov.astype(BF)
            lsec[pl.ds(2 * p + a, 1), :] = peak + jnp.log(total)
        return carry

    lax.fori_loop(0, H // 2, cross, 0, unroll=2)
    x2[...] = x1[...] + tn(coT[...], wco[...])
    saves += [local.start(a, b) for a, b in ((lsec, outs.lsec), (coT, outs.coT), (x2, outs.x2))]
    for m in (1, 2):
        direct(x_hbm, x_all, base_x, m).wait_send()
        relay(x_all, base_x, m).wait_send()
        direct(text_hbm, text_all, base_t, m).wait_send()
        relay(text_all, base_t, m).wait_send()
    for k in range(1, seq):
        send_o(k).wait_send()
    for c in saves:
        c.wait()


def run_forward(dims, args):
    seq, tok, full, width, keys, group, dc = dims
    hl = H // seq
    shapes = dict(
        h1=((seq, tok, width), BF),
        qT=((group, full), BF),
        kT=((group, full), BF),
        kn=((hl, full, HD), BF),
        vn=((hl, full, HD), BF),
        lse=((8, full), F32),
        oT=((seq, group, tok), BF),
        aout=((tok, width), F32),
        x1=((tok, width), F32),
        h2T=((width, tok), BF),
        cqT=((width, tok), BF),
        kv=((keys, 2 * width), BF),
        ckT=((width, keys), BF),
        lsec=((16, tok), F32),
        coT=((width, tok), BF),
        x2=((tok, width), F32),
        text=((seq, keys // seq, dc), BF),
        mods=((8, 6 * width), F32),
        codes=((8, full), F32),
    )
    v = pltpu.VMEM
    scratch = [
        v((seq, tok, width), BF), v((seq, keys // seq, dc), BF), v((width, 3 * 256), BF), v((dc, 2 * width), BF),
        v((width, width), BF), v((width, width), BF), v((width, width), BF),
        v((group, full), BF), v((group, full), BF), v((group, full), BF), v((hl, full, HD), BF), v((hl, full, HD), BF),
        v((8, full), F32), v((seq, group, tok), BF), v((seq, group, tok), BF),
        v((tok, width), F32), v((tok, width), F32), v((width, tok), BF), v((width, tok), BF),
        v((keys, 2 * width), BF), v((2 * width, keys), BF), v((16, tok), F32), v((width, tok), BF), v((tok, width), F32),
        v((full, tok), F32), v((keys, tok), F32), v((full, 128), F32), v((keys, 128), F32), v((tok, width), BF),
        v((width, 6 * width), BF), v((8, 6 * width), F32), v((8, full), F32), v((seq, tok, width), BF),
        pltpu.SemaphoreType.DMA((32,)), pltpu.SemaphoreType.DMA((16,)), pltpu.SemaphoreType.DMA((16,)),
    ]
    outs = pl.pallas_call(
        functools.partial(forward_kernel, dims, args[4].shape[1]),
        out_shape=[jax.ShapeDtypeStruct(*shapes[n]) for n in K1_OUTS],
        in_specs=[ANY, ANY, INV, INV, INV, INV, ANY, ANY, ANY, ANY, ANY, ANY],
        out_specs=[ANY] * len(K1_OUTS),
        scratch_shapes=scratch,
        compiler_params=pltpu.CompilerParams(
            collective_id=0, has_side_effects=True, vmem_limit_bytes=60 * 1024 * 1024
        ),
        name="forward_part",
    )(*args)
    return Bag(zip(K1_OUTS, outs))


class Grad:
    def __init__(self, ref, kind, order, bufs, where, remote, finish):
        self.ref, self.kind, self.order, self.bufs = ref, kind, order, bufs
        self.s, self.seq, self.d, self.stride, self.bits, self.flip, self.dp = where
        self.remote, self.finish = remote, finish
        self.fixed, self.cut, self.stage, self.copies = {}, False, 0, []

    def view(self, fixed, quarter, lead=None):
        index, lead = [], list(lead or [])
        for bit in (2, 1, 0):
            if bit in fixed:
                index.append(fixed[bit])
            elif lead:
                index.append(lead.pop(0))
            else:
                index.append(slice(None))
        if quarter is not None:
            size = self.ref.shape[-1] // (self.seq if self.kind == COLS else 2)
            if self.kind == COLS:
                lanes = pl.ds(pl.multiple_of(quarter * size, 128), size)
                index += [slice(None), lanes]
            else:
                lanes = pl.ds(pl.multiple_of(lax.rem(quarter, 2) * size, 128), size)
                index += [lax.div(quarter, 2), slice(None), lanes]
        return self.ref.at[tuple(index)]

    def line(self):
        return 2 * self.bits[2] + self.bits[1]

    def chunk(self, fixed, quarter, number):
        number = lax.rem(number, 4)
        return self.view({**fixed, 2: lax.div(number, 2), 1: lax.rem(number, 2)}, quarter)

    def end_halving(self, what, buf):
        for a in range(2):
            for w in range(2 if what == XY1 else 1):
                owner = self.flip[2 - a] if w else self.s

                def add(b, carry):
                    own = self.view({**self.fixed, 2: a}, owner, [b])
                    more = buf[a, w, b] if what == XY1 else buf[a, b]
                    own[...] = (own[...].astype(F32) + more.astype(F32)).astype(BF)
                    return carry

                lax.fori_loop(0, 2, add, 0)

    def end_line(self, t, buf):
        quarter, line = self.s if self.cut else None, self.line()
        above, below = self.copies

        def take(copy, side, number):
            copy().wait_recv()
            own = self.chunk(self.fixed, quarter, number)
            own[...] = (own[...].astype(F32) + buf[side].astype(F32)).astype(BF)

        @pl.when((line >= 1) & (line <= t + 1))
        def _():
            take(above, 0, line + 2 - t)

        @pl.when((line <= 2) & (line >= 2 - t))
        def _():
            take(below, 1, line + 2 + t)

    def begin(self):
        what, buf = self.order[self.stage], self.bufs[self.stage]
        self.copies = []
        if what == XY1:
            for a in range(2):
                to = self.flip[1 + a]
                for w, owner in enumerate((to, self.flip[3])):

                    def describe(a=a, w=w, owner=owner, to=to, fixed=dict(self.fixed)):
                        return self.view({**fixed, 2: a}, owner), buf.at[a, w], {SEQ: to}

                    self.copies.append(self.remote.start(describe))
        elif what == XY2:
            for a in range(2):

                def describe(a=a, to=self.flip[2 - a], fixed=dict(self.fixed)):
                    return self.view({**fixed, 2: a}, to), buf.at[a], {SEQ: to}

                self.copies.append(self.remote.start(describe))
        elif what >= L0:
            t = what - L0

            def upward(fixed=dict(self.fixed), quarter=self.s if self.cut else None):
                peer = lax.rem(self.d + 2 * self.stride, self.dp)
                return self.chunk(fixed, quarter, self.line() + 3 - t), buf.at[0], {DP: peer}

            def downward(fixed=dict(self.fixed), quarter=self.s if self.cut else None):
                peer = lax.rem(self.d - 2 * self.stride + self.dp, self.dp)
                return self.chunk(fixed, quarter, self.line() + 1 + t), buf.at[1], {DP: peer}

            self.copies.append(self.remote.start(upward, lambda: self.line() <= t))
            self.copies.append(self.remote.start(downward, lambda: self.line() >= 3 - t))
        elif what == CUT:
            for k in range(1, self.seq):

                def describe(k=k, fixed=dict(self.fixed)):
                    to = lax.rem(self.s + k, self.seq)
                    return self.view(fixed, to), buf.at[k - 1], {SEQ: to}

                self.copies.append(self.remote.start(describe))
        else:

            def describe(fixed=dict(self.fixed), quarter=self.s if self.cut else None):
                mine = self.bits[what]
                peer = self.d + (1 - 2 * mine) * (self.stride << what)
                return self.view({**fixed, what: 1 - mine}, quarter), buf, {DP: peer}

            self.copies.append(self.remote.start(describe))

    def end(self):
        what, buf = self.order[self.stage], self.bufs[self.stage]
        if what >= L0:
            self.end_line(what - L0, buf)
            self.stage += 1
            if what == L2:
                self.fixed[1], self.fixed[2] = self.bits[1], self.bits[2]
            return
        for c in self.copies:
            c().wait_recv()
        if what in (XY1, XY2):
            self.end_halving(what, buf)
            self.stage += 1
            self.cut = what == XY2
            return
        if what == CUT:
            self.cut = True
        else:
            self.fixed[what] = self.bits[what]
        free = 3 - len(self.fixed)
        quarter = self.s if self.cut else None
        last = self.stage == len(self.order) - 1
        self.stage += 1

        def add(i, carry):
            lead = [lax.rem(lax.div(i, 2 ** (free - 1 - j)), 2) for j in range(free)]
            own = self.view(self.fixed, quarter, lead)
            total = own[...].astype(F32)
            if what == CUT:
                for k in range(self.seq - 1):
                    total = total + buf[tuple([k] + lead)].astype(F32)
            elif lead:
                total = total + buf[tuple(lead)].astype(F32)
            else:
                total = total + buf[...].astype(F32)
            if last:
                self.finish(total)
            else:
                own[...] = total.astype(BF)
            return carry

        if free == 0:
            add(0, 0)
        else:
            lax.fori_loop(0, 2**free, add, 0)

    def step(self):
        self.end()
        if self.stage < len(self.order):
            self.begin()


def grad_buffers(shape, kind, order, seq):
    lead, payload, out, cut, free = 3, list(shape), [], False, 3
    for what in order:
        if what in (CUT, XY1, XY2):
            cut = True
        elif what in (0, 1, 2):
            free -= 1
        elif what == L2:
            free = 0
        p = list(payload)
        if cut:
            if kind == COLS:
                p[-1] //= seq
            else:
                p = [p[1], p[2] // 2]
        head = {CUT: [seq - 1], XY1: [2, 2, 2], XY2: [2, 2], L0: [2], L1: [2], L2: [2]}.get(what, [])
        if what in (CUT, 0, 1, 2):
            head = head + [2] * free
        out.append(pltpu.VMEM(tuple(head + p), BF))
    return out


GRADS = dict(
    fc2=(PACK, (0, XY1, XY2, 1, 2)),
    fc1=(COLS, (0, L0, L1, L2, CUT)),
    cout=(PACK, (0, XY1, XY2, 1, 2)),
    cq=(PACK, (0, XY1, XY2, 1, 2)),
    proj=(PACK, (0, XY1, XY2, 1, 2)),
    ckv=(None, (0, 1, 2)),
    qkv=(None, (0, 1, 2)),
)
K2_OUTS = tuple(dict(block_out=0, grad_frames=0, grad_text=0, ada=0, qkv=0, proj=0, cq=0, ckv=0, cout=0, fc1=0, fc2=0))
K2_LOADS = tuple(dict(x2=0, x1=0, aout=0, oT=0, h2T=0, cqT=0, coT=0, lsec=0, lse=0, kv=0))
K2_HELD = tuple(dict(ckT=0, qT=0, kT=0, kn=0, vn=0))
K2_WEIGHTS = tuple(dict(fc1=0, fc2=0, cout=0, cq=0, proj=0))


def backward_kernel(dims, names, dp, *refs):
    seq, tok, full, width, keys, group, dc_all = dims
    hl, chunk, tl, stride = H // seq, width, keys // seq, dp // BLOCKS
    r = Bag(zip(names, refs))
    local, remote = Local(r.lsem), Remote(r.ssem, r.rsem)
    s, d = lax.axis_index(SEQ), lax.axis_index(DP)
    bits = [lax.rem(lax.div(d, stride << b), 2) for b in range(3)]
    sx, sy = lax.rem(s, 2), lax.div(s, 2)
    flip = [s, s + 1 - 2 * sx, s + 2 - 4 * sy, 3 - s]
    where = (s, seq, d, stride, bits, flip, dp)
    codes, mods = r.codes, r.mods

    loads = Bag()
    loads["x2"] = local.start(r.in_x2, r.x2)
    loads["cot"] = local.start(r.in_cot, r.cot)
    load_base = local.used
    local.used += 2 * seq

    def load_chunk(n, c):
        if n:
            ca, cb = (c // 2, c % 2) if isinstance(c, int) else (lax.div(c, 2), lax.rem(c, 2))
            src, dst = r.w_fc2.at[ca, cb], r.g_fc2.at[ca, cb]
        else:
            cols = pl.ds(c * chunk if isinstance(c, int) else pl.multiple_of(c * chunk, chunk), chunk)
            src, dst = r.w_fc1.at[:, :, :, :, cols], r.g_fc1.at[:, :, :, :, cols]
        return pltpu.make_async_copy(src, dst, r.lsem.at[load_base + 2 * c + n])

    for c in range(seq):
        for n in range(2):
            load_chunk(n, c).start()
    for n in K2_WEIGHTS[2:]:
        loads["w_" + n] = local.start(r["w_" + n], r["g_" + n])
    for n in K2_LOADS[1:]:
        loads[n] = local.start(r["in_" + n], r[n])
    loads.x = local.start(r.in_x, r.x)

    stores = []

    def stored(n, slot):
        return pltpu.make_async_copy(r["out_" + n], r["hbm_" + n], r.lsem.at[slot])

    def store(n):
        stores.append((n, local.used))
        stored(n, local.used).start()
        local.used += 1

    barrier = pltpu.get_barrier_semaphore()
    for k in range(1, seq):
        pl.semaphore_signal(barrier, inc=1, device_id={SEQ: lax.rem(s + k, seq)}, device_id_type=MESH)

    def greet_dp(j, carry):
        pl.semaphore_signal(barrier, inc=1, device_id={DP: lax.rem(d + j, dp)}, device_id_type=MESH)
        return carry

    lax.fori_loop(1, dp, greet_dp, 0)
    pl.semaphore_wait(barrier, seq - 1 + dp - 1)

    emb_base = remote.slots(dp)
    dm_base = remote.slots(dp)

    def send_emb(j):
        to = lax.rem(d + j, dp)
        return remote.make(r.in_emb.at[to], r.emball.at[d], emb_base + j, {DP: to})

    def start_emb(j, carry):
        send_emb(j).start()
        return carry

    lax.fori_loop(1, dp, start_emb, 0)
    own_emb = local.start(r.in_emb.at[d], r.emball.at[d])

    def into_cols(n):
        def finish(total):
            r["out_" + n][...] = total
            store(n)

        return finish

    def into_pack(n):
        def finish(total):
            rows, lanes = total.shape
            if n == "fc2":
                turned = total.T
                r.out_fc2[:, 0:rows] = turned[: lanes // 2]
                r.out_fc2[:, rows : 2 * rows] = turned[lanes // 2 :]
            else:
                r["out_" + n][0:rows, :] = total[:, : lanes // 2]
                r["out_" + n][rows : 2 * rows, :] = total[:, lanes // 2 :]
            store(n)

        return finish

    def into_blocks(total):
        for t in range(3):
            r.fq[t] = total[:, t * group : (t + 1) * group]

    grads = Bag()
    for n, (kind, order) in GRADS.items():
        finish = into_blocks if n == "qkv" else (into_pack(n) if kind == PACK else into_cols(n))
        bufs = [r["r_%s%d" % (n, i)] for i in range(len(order))]
        grads[n] = Grad(r["g_" + n], kind, order, bufs, where, remote, finish)

    rows_own = pl.ds(pl.multiple_of(s * tok, tok), tok)
    seg_row = codes[0:1, rows_own]
    seg = jnp.broadcast_to(column(seg_row)[:, :1], (tok, width))
    clip_id = lax.broadcasted_iota(jnp.int32, (16, tok), 0).astype(F32)
    onehot = jnp.where(clip_id == seg_row, 1.0, 0.0).astype(BF)

    def clip_sum(part, value):
        high = value.astype(BF)
        rest = (value - high.astype(F32)).astype(BF)
        r.dmod[:, part * width : (part + 1) * width] = (nn(onehot, high) + nn(onehot, rest))[:8]

    def square(n, lhs, rhs):
        g = r["g_" + n]

        def four(i, carry):
            val = nn(lhs(i), rhs).astype(BF)
            for g0 in range(2):
                for q in range(seq):
                    half = val.shape[0] // 4
                    low = g0 * 2 * half
                    lane = (q % 2) * 2 * group
                    at = (lax.div(i, 2), lax.rem(i, 2), g0, q // 2)
                    g[at + (slice(None), slice(lane, lane + group))] = val[low : low + half, q * group : (q + 1) * group]
                    g[at + (slice(None), slice(lane + group, lane + 2 * group))] = val[
                        low + half : low + 2 * half, q * group : (q + 1) * group
                    ]
            return carry

        lax.fori_loop(0, 4, four, 0)

    def weight(n):
        return r["g_" + n][...].reshape(width, width)

    core_base = remote.slots(seq)

    def core_copy(c):
        ca, cb = (c // 2, c % 2) if isinstance(c, int) else (lax.div(c, 2), lax.rem(c, 2))
        peer = d + (1 - 2 * bits[0]) * stride
        return remote.make(r.g_fc2.at[ca, cb, 1 - bits[0]], r.r_fc20.at[ca, cb], core_base + c, {DP: peer})

    v = pltpu.VMEM
    dkv_copies = []
    quarter = 2 * width // seq
    do_base = remote.slots(seq)

    def send_do(k):
        to = lax.rem(s + k, seq)
        return remote.make(r.dosend.at[to], r.dorecv.at[s], do_base + k, {SEQ: to})

    def kv_part(a, owner):
        lanes = pl.ds(pl.multiple_of(owner * quarter, quarter), quarter)
        return r.kv.at[pl.ds(a * keys // 2, keys // 2), lanes]

    def begin_kv():
        for a in range(2):
            for w, owner in enumerate((flip[1 + a], flip[3])):

                def describe(a=a, w=w, owner=owner):
                    return kv_part(a, owner), r.dkvr.at[a, w], {SEQ: flip[1 + a]}

                dkv_copies.append(remote.start(describe))

    def step_kv():
        for c in dkv_copies:
            c().wait_recv()
        dkv_copies.clear()
        for a in range(2):
            for w, owner in enumerate((s, flip[2 - a])):
                own = kv_part(a, owner)
                own[...] = (own[...].astype(F32) + r.dkvr[a, w].astype(F32)).astype(BF)

            def describe(a=a):
                return kv_part(a, flip[2 - a]), r.dkvs.at[a], {SEQ: flip[2 - a]}

            dkv_copies.append(remote.start(describe))

    def end_kv():
        for c in dkv_copies:
            c().wait_recv()
        for a in range(2):
            own = kv_part(a, s)[...].astype(F32) + r.dkvs[a].astype(F32)
            r.dkvq[a * seq // 2 : (a + 1) * seq // 2] = own.astype(BF).reshape(seq // 2, tl, quarter)

    def middle(*held):
        for n, ref in zip(K2_HELD, held):
            r[n] = ref
            loads[n] = local.start(r["in_" + n], ref)

        loads.x2.wait()
        loads.cot.wait()
        x2v = r.x2[...]
        n3, _ = norm_parts(x2v)
        h3 = (n3 * (1.0 + pick(mods, seg, 4, width)) + pick(mods, seg, 3, width)).astype(BF)

        def feed(h3_ref, h3T_ref, dm_ref, m_ref, dh_ref):
            h3_ref[...] = h3
            h3T_ref[...] = h3.astype(F32).T.astype(BF)
            dm_ref[...] = (pick(mods, seg, 5, width) * r.cot[...].astype(F32)).astype(BF)
            m_ref[...] = jnp.zeros_like(m_ref)
            dh_ref[...] = jnp.zeros_like(dh_ref)
            g1, g2 = r.g_fc1, r.g_fc2
            k0, k1 = math.sqrt(2.0 / math.pi), 0.044715

            def one(c, carry):
                load_chunk(0, c).wait()
                load_chunk(1, c).wait()
                cols = pl.ds(pl.multiple_of(c * chunk, chunk), chunk)
                ca, cb = lax.div(c, 2), lax.rem(c, 2)
                w1 = g1[:, :, :, :, cols].reshape(width, chunk)
                w2 = g2[ca, cb].reshape(chunk, width)
                z = nn(h3_ref[...], w1)
                zz = z * z
                t = jnp.tanh(k0 * (z + k1 * z * zz))
                u = (0.5 * z * (1.0 + t)).astype(BF)
                slope = 0.5 * (1.0 + t) + 0.5 * z * (1.0 - t * t) * (k0 * (1.0 + 3.0 * k1 * zz))
                m_ref[...] += nn(u, w2)
                dz = (nt(dm_ref[...], w2) * slope).astype(BF)
                dh_ref[...] += nt(dz, w1)
                g1[:, :, :, :, cols] = nn(h3T_ref[...], dz).astype(BF).reshape(2, 2, 2, width // BLOCKS, chunk)
                for g0 in range(2):
                    half = chunk // 4
                    val = tn(u[:, g0 * 2 * half : (g0 + 1) * 2 * half], dm_ref[...]).astype(BF)
                    for q in range(seq):
                        lane = (q % 2) * 2 * group
                        g2[ca, cb, g0, q // 2, :, lane : lane + group] = val[:half, q * group : (q + 1) * group]
                        g2[ca, cb, g0, q // 2, :, lane + group : lane + 2 * group] = val[half:, q * group : (q + 1) * group]
                core_copy(c).start()
                return carry

            lax.fori_loop(0, seq, one, 0)
            grads.fc2.copies = [functools.partial(core_copy, c) for c in range(seq)]
            for c in range(seq):
                remote.open.append(lambda c=c: core_copy(c).wait_send())
            grads.fc1.begin()
            dy = r.cot[...].astype(F32)
            m = m_ref[...]
            x2w = r.x2[...]
            r.out_block_out[...] = (x2w + pick(mods, seg, 5, width) * m).astype(BF)
            store("block_out")
            clip_sum(5, dy * m)
            dh = dh_ref[...]
            nw, rstd = norm_parts(x2w)
            clip_sum(3, dh)
            clip_sum(4, dh * nw)
            r.dx[...] = dy + norm_back(dh * (1.0 + pick(mods, seg, 4, width)), nw, rstd)
            grads.fc2.step()

        pl.run_scoped(feed, v((tok, width), BF), v((width, tok), BF), v((tok, width), BF), v((tok, width), F32), v((tok, width), F32))

        for c in (loads.w_cout, loads.coT, loads.cqT, loads.lsec, loads.kv, loads.ckT):
            c.wait()

        def cross_back(dcoT, dcqT, biasc):
            dc = r.dx[...].astype(BF)
            dcoT[...] = nt(weight("cout"), dc).astype(BF)
            square("cout", lambda i: r.coT[pl.ds(pl.multiple_of(i * group, group), group), :], dc)
            grads.cout.begin()
            tcol = column(codes[2:3, :keys])
            biasc[...] = jnp.where(jnp.broadcast_to(tcol[:, :1], (keys, tok)) == seg_row, 0.0, MASKED)
            grads.fc1.step()
            kv = r.kv

            def pair(p, carry):
                cols = pl.ds(pl.multiple_of(p * 128, 128), 128)
                vcols = pl.ds(pl.multiple_of(width + p * 128, 128), 128)
                ck, cv = kv[:, cols], kv[:, vcols]
                parts_k, parts_v = [], []
                for a in range(2):
                    hrows = pl.ds(pl.multiple_of(p * 128 + a * HD, HD), HD)
                    q_h, do_h = r.cqT[hrows, :], dcoT[hrows, :]
                    lse_h = r.lsec[pl.ds(2 * p + a, 1), :]
                    pr = jnp.exp(nn(ck[:, a * HD : (a + 1) * HD], q_h) + biasc[...] - lse_h)
                    dpr = nn(cv[:, a * HD : (a + 1) * HD], do_h)
                    delta = jnp.sum(pr * dpr, axis=0, keepdims=True)
                    ds = (pr * (dpr - delta)).astype(BF)
                    parts_k.append(nt(ds, q_h))
                    parts_v.append(nt(pr.astype(BF), do_h))
                    dcqT[hrows, :] = nn(r.ckT[hrows, :], ds) * SCALE
                kv[:, cols] = jnp.concatenate(parts_k, axis=1).astype(BF)
                kv[:, vcols] = jnp.concatenate(parts_v, axis=1).astype(BF)
                return carry

            lax.fori_loop(0, H // 2, pair, 0)
            grads.fc2.step()
            dcq = dcqT[...].T.astype(BF)
            loads.w_cq.wait()
            loads.h2T.wait()
            loads.x1.wait()
            dh2 = nt(dcq, weight("cq"))
            square("cq", lambda i: r.h2T[pl.ds(pl.multiple_of(i * group, group), group), :], dcq)
            nw, rstd = norm_parts(r.x1[...])
            r.dx[...] += norm_back(dh2, nw, rstd)

        pl.run_scoped(cross_back, v((width, tok), BF), v((width, tok), F32), v((keys, tok), F32))

        grads.fc1.step()
        for c in (loads.w_proj, loads.aout, loads.oT):
            c.wait()
        dx1 = r.dx[...]
        da = (pick(mods, seg, 2, width) * dx1).astype(BF)
        doT = nt(weight("proj"), da).astype(BF)
        for q in range(seq):
            r.dosend[q] = doT[q * group : (q + 1) * group, :]
        for k in range(1, seq):
            send_do(k).start()
        r.dorecv[s] = r.dosend[s]
        grads.cq.begin()
        grads.cout.step()
        begin_kv()
        clip_sum(2, dx1 * r.aout[...])
        square("proj", lambda i: r.oT[i], da)
        grads.proj.begin()
        for c in (loads.qT, loads.kT, loads.kn, loads.vn, loads.lse):
            c.wait()

        def self_back(kcol, bias, dk, dv):
            kcol[...] = column(codes[1:2, :full])
            dk[...] = jnp.zeros_like(dk)
            dv[...] = jnp.zeros_like(dv)

            def block(k, carry):
                @pl.when(k > 0)
                def _():
                    send_do(k).wait_recv()

                at = lax.rem(s - k + seq, seq)
                rows = pl.ds(pl.multiple_of(at * tok, tok), tok)
                row_id = lax.broadcasted_iota(jnp.int32, (full, tok), 0)
                col_id = lax.broadcasted_iota(jnp.int32, (full, tok), 1) + at * tok
                key = jnp.broadcast_to(kcol[:, :1], (full, tok))
                bias[...] = jnp.where((key == codes[0:1, rows]) | (row_id == col_id), 0.0, MASKED)
                for h in range(hl):
                    hs = slice(h * HD, (h + 1) * HD)
                    q_h, do_h = r.qT[hs, rows], r.dorecv[at, hs, :]
                    pr = jnp.exp(nn(r.kn[h], q_h) + bias[...] - r.lse[h : h + 1, rows])
                    dpr = nn(r.vn[h], do_h)
                    delta = jnp.sum(pr * dpr, axis=0, keepdims=True)
                    ds = (pr * (dpr - delta)).astype(BF)
                    dk[h] += nt(ds, q_h)
                    dv[h] += nt(pr.astype(BF), do_h)
                    dq = nn(r.kT[hs, :], ds) * SCALE
                    r.dqs[at, :, hs] = dq.T.astype(BF)
                return carry

            lax.fori_loop(0, 2, block, 0)
            grads.fc1.step()
            grads.fc2.step()
            lax.fori_loop(2, seq, block, 0)
            for h in range(hl):
                for b in range(seq):
                    br = slice(b * tok, (b + 1) * tok)
                    r.dqs[b, :, group + h * HD : group + (h + 1) * HD] = dk[h, br, :].astype(BF)
                    r.dqs[b, :, 2 * group + h * HD : 2 * group + (h + 1) * HD] = dv[h, br, :].astype(BF)

        pl.run_scoped(self_back, v((full, 128), F32), v((full, tok), F32), v((hl, full, HD), F32), v((hl, full, HD), F32))

    pl.run_scoped(
        middle,
        v((width, keys), BF),
        v((group, full), BF),
        v((group, full), BF),
        v((hl, full, HD), BF),
        v((hl, full, HD), BF),
    )

    dq_base = remote.slots(seq)

    def send_dq(k):
        to = lax.rem(s + k, seq)
        return remote.make(r.dqs.at[to], r.dqr.at[s], dq_base + k, {SEQ: to})

    for k in range(1, seq):
        send_dq(k).start()
    step_kv()
    for n in ("cq", "proj", "cout"):
        grads[n].step()
    r.dqr[s] = r.dqs[s]

    def tail(h1, text, wqkv, wckv, dqf):
        tail_loads = [
            local.start(a, b)
            for a, b in ((r.in_h1, h1), (r.w_qkv, wqkv), (r.in_text, text), (r.w_ckv, wckv))
        ]
        loads.x.wait()
        tail_loads[0].wait()
        gq = tn(h1[...].reshape(full, width), r.dqs[...].reshape(full, 3 * group))
        r.g_qkv[...] = gq.astype(BF).reshape(2, 2, 2, width // BLOCKS, 3 * group)
        grads.qkv.begin()
        grads.qkv.step()
        grads.fc2.step()
        for k in range(1, seq):
            send_dq(k).wait_recv()
        for b in range(seq):
            got = r.dqr[b]
            for t in range(3):
                dqf[:, t * width + b * group : t * width + (b + 1) * group] = got[:, t * group : (t + 1) * group]
        tail_loads[1].wait()
        dh1 = nt(dqf[...], wqkv[...])
        nx, rstd = norm_parts(r.x[...].astype(F32))
        clip_sum(0, dh1)
        clip_sum(1, dh1 * nx)
        dm_copies = []
        part = 6 * width // seq
        for k in range(1, seq):

            def describe_dm(k=k):
                to = lax.rem(s + k, seq)
                lanes = pl.ds(pl.multiple_of(to * part, part), part)
                return r.dmod.at[:, lanes], r.dmr.at[k - 1], {SEQ: to}

            dm_copies.append(remote.start(describe_dm))
        back = norm_back(dh1 * (1.0 + pick(mods, seg, 1, width)), nx, rstd)
        r.out_grad_frames[...] = (r.dx[...] + back).astype(BF)
        store("grad_frames")
        end_kv()
        kv_base = remote.slots(seq)

        def send_kv(k):
            to = lax.rem(s + k, seq)
            return remote.make(r.dkvq.at[to], r.dkvl.at[s], kv_base + k, {SEQ: to})

        for k in range(1, seq):
            send_kv(k).start()
        r.dkvl[s] = r.dkvq[s]
        tail_loads[2].wait()
        gc = tn(text[...].reshape(keys, dc_all), r.dkvq[...].reshape(keys, quarter))
        r.g_ckv[...] = gc.astype(BF).reshape(2, 2, 2, dc_all // BLOCKS, quarter)
        grads.ckv.begin()
        for n in ("qkv", "cq", "proj", "cout", "fc1", "ckv"):
            grads[n].step()
        for c in dm_copies:
            c().wait_recv()
        total = r.dmod[:, pl.ds(pl.multiple_of(s * part, part), part)]
        for k in range(seq - 1):
            total = total + r.dmr[k]
        r.dmall[d] = total

        def send_dm(j):
            to = lax.rem(d + j, dp)
            return remote.make(r.dmall.at[d], r.dmall.at[d], dm_base + j, {DP: to})

        def start_dm(j, carry):
            send_dm(j).start()
            return carry

        lax.fori_loop(1, dp, start_dm, 0)
        grads.fc2.step()
        grads.qkv.step()
        q_base = remote.slots(3)

        def send_q(t):
            b = 4 * t + s
            to = lax.div(b, 3)
            slot = b - 3 * to
            return to, slot, pltpu.make_async_remote_copy(
                src_ref=r.fq.at[t],
                dst_ref=r.rq.at[slot],
                send_sem=r.ssem.at[q_base + t],
                recv_sem=r.rsem.at[q_base + slot],
                device_id={SEQ: to},
                device_id_type=MESH,
            )

        for t in range(3):
            to, slot, copy = send_q(t)

            @pl.when(to != s)
            def _():
                copy.start()

            @pl.when(to == s)
            def _():
                r.rq[slot] = r.fq[t]

        for n in ("cout", "cq", "proj", "ckv"):
            grads[n].step()
        for k in range(1, seq):
            send_kv(k).wait_recv()
        tail_loads[3].wait()
        gt = nt(r.dkvl[0], wckv[:, 0:quarter])
        for b in range(1, seq):
            gt = gt + nt(r.dkvl[b], wckv[:, b * quarter : (b + 1) * quarter])
        r.out_grad_text[...] = gt.astype(BF)
        store("grad_text")
        for n in ("cq", "proj", "cout", "ckv", "fc1", "cq", "proj"):
            grads[n].step()

        def wait_dm(j, carry):
            send_dm(j).wait_recv()
            send_emb(j).wait_recv()
            return carry

        own_emb.wait()
        lax.fori_loop(1, dp, wait_dm, 0)
        emb = r.emball[...].reshape(dp * 8, 128)
        allm = r.dmall[...].reshape(dp * 8, part)
        high = allm.astype(BF)
        rest = (allm - high.astype(F32)).astype(BF)
        ga = tn(emb, high) + tn(emb, rest)
        r.out_ada[...] = ga[: width // dp]
        store("ada")
        for j in range(3):
            src = lax.rem(3 * s + j, seq)

            @pl.when(src != s)
            def _():
                remote.make(r.fq.at[j], r.rq.at[j], q_base + j, {SEQ: src}).wait_recv()

            r.out_qkv[:, j * group : (j + 1) * group] = r.rq[j]
        store("qkv")

        for t in range(3):
            to, slot, copy = send_q(t)

            @pl.when(to != s)
            def _():
                copy.wait_send()

        for k in range(1, seq):
            send_do(k).wait_send()
            send_dq(k).wait_send()
            send_kv(k).wait_send()

        def wait_sent(j, carry):
            send_dm(j).wait_send()
            send_emb(j).wait_send()
            return carry

        lax.fori_loop(1, dp, wait_sent, 0)
        for sent in remote.open:
            sent()
        for n, slot in stores:
            stored(n, slot).wait()

    pl.run_scoped(
        tail,
        v((seq, tok, width), BF),
        v((seq, tl, dc_all), BF),
        v((width, 3 * width), BF),
        v((dc_all, 2 * width), BF),
        v((tok, 3 * width), BF),
    )


def run_backward(dims, dp, fwd, args):
    seq, tok, full, width, keys, group, dc = dims
    hl, tl, block = H // seq, keys // seq, width // BLOCKS
    ff = 4 * width
    v = pltpu.VMEM
    lead = (2, 2, 2)
    gshape = dict(
        fc1=(block, ff),
        fc2=(2, ff // BLOCKS // 2, width),
        cout=(2, block // 2, width),
        cq=(2, block // 2, width),
        proj=(2, block // 2, width),
        ckv=(dc // BLOCKS, 2 * width // seq),
        qkv=(block, 3 * group),
    )
    names, ins, specs = [], [], []

    def add_in(spec=ANY, **kw):
        for name, value in kw.items():
            names.append(name)
            ins.append(value)
            specs.append(spec)

    add_in(codes=fwd.codes, spec=INV)
    add_in(mods=fwd.mods, spec=INV)
    add_in(in_x=args.x)
    add_in(in_cot=args.cot)
    add_in(in_emb=args.emb)
    for n in K2_LOADS + K2_HELD + ("h1", "text"):
        add_in(**{"in_" + n: fwd[n]})
    for n in K2_WEIGHTS:
        add_in(**{"w_" + n: args[n].reshape(lead + gshape[n])})
    add_in(w_ckv=args.ckv)
    add_in(w_qkv=args.qkv)

    outs = dict(
        block_out=((tok, width), BF),
        grad_frames=((tok, width), BF),
        grad_text=((tl, dc), BF),
        ada=((width // dp, 6 * width // seq), F32),
        qkv=((block, 3 * group), F32),
        proj=((block, group), F32),
        cq=((block, group), F32),
        ckv=((dc // BLOCKS, 2 * width // seq), F32),
        cout=((block, group), F32),
        fc1=((block, ff // seq), F32),
        fc2=((group, ff // BLOCKS), F32),
    )
    for n in K2_OUTS:
        names.append("hbm_" + n)
    scratch = []

    def add(**kw):
        for name, (shape, dtype) in kw.items():
            names.append(name)
            scratch.append(v(shape, dtype))

    for n in K2_OUTS:
        add(**{"out_" + n: outs[n]})
    add(cot=((tok, width), BF))
    add(x=((tok, width), BF))
    for n in K2_LOADS:
        add(**{n: (fwd[n].shape, fwd[n].dtype)})
    for n, (kind, order) in GRADS.items():
        add(**{"g_" + n: (lead + gshape[n], BF)})
        for i, b in enumerate(grad_buffers(gshape[n], kind, order, seq)):
            names.append("r_%s%d" % (n, i))
            scratch.append(b)
    quarter = 2 * width // seq
    add(dx=((tok, width), F32))
    add(dkvr=((2, 2, keys // 2, quarter), BF))
    add(dkvs=((2, keys // 2, quarter), BF))
    add(dkvq=((seq, tl, quarter), BF))
    add(dkvl=((seq, tl, quarter), BF))
    add(dosend=((seq, group, tok), BF))
    add(dorecv=((seq, group, tok), BF))
    add(dqs=((seq, tok, 3 * group), BF))
    add(dqr=((seq, tok, 3 * group), BF))
    add(dmod=((8, 6 * width), F32))
    add(dmr=((seq - 1, 8, 6 * width // seq), F32))
    add(dmall=((dp, 8, 6 * width // seq), F32))
    add(emball=((dp, 8, 128), BF))
    add(fq=((3, block, group), F32))
    add(rq=((3, block, group), F32))
    count = 2 * dp + 96
    for n, k in dict(lsem=64, ssem=count, rsem=count).items():
        names.append(n)
        scratch.append(pltpu.SemaphoreType.DMA((k,)))
    got = pl.pallas_call(
        functools.partial(backward_kernel, dims, tuple(names), dp),
        out_shape=[jax.ShapeDtypeStruct(*outs[n]) for n in K2_OUTS],
        in_specs=specs,
        out_specs=[ANY] * len(K2_OUTS),
        scratch_shapes=scratch,
        compiler_params=pltpu.CompilerParams(
            collective_id=1, has_side_effects=True, vmem_limit_bytes=67043328
        ),
        name="backward_part",
    )(*ins)
    return Bag(zip(K2_OUTS, got))


def hand_over(*refs):
    count = len(K2_OUTS)
    ins, outs, held, sems = refs[:count], refs[count : 2 * count], refs[2 * count : -1], refs[-1]
    first = [pltpu.make_async_copy(a, b, sems.at[0, i]) for i, (a, b) in enumerate(zip(ins, held))]
    second = [pltpu.make_async_copy(a, b, sems.at[1, i]) for i, (a, b) in enumerate(zip(held, outs))]
    for c in first:
        c.start()
    for c, n in zip(first, second):
        c.wait()
        n.start()
    for c in second:
        c.wait()


def run_hand_over(g):
    values = [g[n] for n in K2_OUTS]
    got = pl.pallas_call(
        hand_over,
        out_shape=[jax.ShapeDtypeStruct(a.shape, a.dtype) for a in values],
        in_specs=[ANY] * len(values),
        out_specs=[ANY] * len(values),
        scratch_shapes=[pltpu.VMEM(a.shape, a.dtype) for a in values] + [pltpu.SemaphoreType.DMA((2, len(values)))],
        name="hand_over",
    )(*values)
    return Bag(zip(K2_OUTS, got))


def per_device(
    frames, seg_ids, padding, step_ids, text_states, text_len, w_ada, w_qkv, w_proj, w_cq, w_ckv, w_cout, w_fc1, w_fc2,
    cotangent,
):
    rows, tok, width = frames.shape
    seq, dp = lax.axis_size(SEQ), lax.axis_size(DP)
    segs = step_ids.shape[1]
    full = seg_ids.shape[1]
    tl, dc = text_states.shape[2], text_states.shape[3]
    keys = segs * tl * seq
    group = (H // seq) * HD
    dims = (seq, tok, full, width, keys, group, dc)
    emb = embed_steps(step_ids[0], width).astype(BF)
    span = width // dp
    emb_parts = jnp.pad(
        jnp.swapaxes(emb.reshape(segs, dp, span), 0, 1), ((0, 0), (0, 8 - segs), (0, 128 - span))
    )
    x = frames[0]
    text = text_states.reshape(segs * tl, dc)
    fwd = run_forward(dims, (x, text, seg_ids, padding, text_len, emb, w_ada, w_qkv, w_ckv, w_proj, w_cq, w_cout))
    args = Bag(
        x=x, cot=cotangent[0], emb=emb_parts, ckv=w_ckv, qkv=w_qkv,
        fc1=w_fc1, fc2=w_fc2, cout=w_cout, cq=w_cq, proj=w_proj,
    )
    g = run_hand_over(run_backward(dims, dp, fwd, args))
    stride = dp // BLOCKS
    if stride > 1:
        groups = [[b * stride + j for j in range(stride)] for b in range(BLOCKS)]
        for n in GRADS:
            g[n] = lax.psum_scatter(g[n], DP, scatter_dimension=1 if n == "fc2" else 0, axis_index_groups=groups, tiled=True)
    return (
        g.block_out.reshape(frames.shape),
        g.grad_frames.reshape(frames.shape),
        g.grad_text.reshape(text_states.shape),
        g.ada, g.qkv, g.proj, g.cq, g.ckv, g.cout, g.fc1, g.fc2.T,
    )


def solution(mesh):
    own, row, rep = P(DP, SEQ, None), P(DP, None), P()
    text, grad = P(DP, None, SEQ, None), P(DP, SEQ)
    return jax.shard_map(
        per_device,
        mesh=mesh,
        in_specs=(own, row, row, row, text, row) + (rep,) * 8 + (own,),
        out_specs=(own, own, text) + (grad,) * 8,
        check_vma=False,
    )
```
